256 devices in a mesh: corpus: 64 (over x, z, core), rep: 4 (over y).
Axes of the slice: x: 4, y: 4, z: 8, core: 2. Of those that a mesh axis runs over, the one named last changes fastest.
Arguments:
- queries: bfloat16 [32768, 768], P(('corpus', 'rep')), may hold values from -18 to 18
- teacher: float32 [32768, 64], P(('corpus', 'rep')), may hold values from -15 to 305
- slab: bfloat16 [65536, 768], P('corpus'), may hold values from -12 to 12
- candidates: int32 [32768, 64], P(('corpus', 'rep')), may hold values from 0 to 65535, as said below
- hot_ids: int32 [2048], replicated, may hold values from 0 to 65535, as said below
- location: int32 [65536], replicated, may hold values from 0 to 65535, as said below
Outputs:
- loss: float32 [32768], P(('corpus', 'rep'))
- query_grad: float32 [32768, 768], P(('corpus', 'rep'))
- slab_grad: float32 [65536, 768], P(('corpus', 'rep'))
The draws below stay inside these ranges and needn't reach their ends.
Inputs may be any that keep to these rules, and one draw needn't show every extreme that they name: `candidates`: every query names 64 passage ids, exactly 8 of them absent from hot_ids; ids may repeat. With the owner of id p being location[p] // 1024, the ids absent from hot_ids among one device's 128 queries (aligned blocks of 128 rows) fall at most 24 times on any owner; in each block some owner gets exactly 24, the same owner for all blocks whose block number has the same remainder modulo the number of rep devices. `hot_ids`: 2048 distinct ids; entries 32 * c to 32 * c + 31 are owned by corpus index c. `location`: A permutation of the passage ids onto slab rows.
All inputs are finite; a program needn't handle non-finite values.
Results may differ from the reference program's by a relative error of at most 0.0026.
Values may be sent and summed in bfloat16 or wider, within the bound.
No kernel may reach another device: no remote copies, remote signals or barrier semaphores. Data moves between devices by JAX's collectives and lax.ppermute only.
A program may use at most 128 MiB of HBM per device.

```python
import math
import jax
import jax.numpy as jnp
from jax import lax

D = 768
K = 64
COLD = 8
HOT_DEV = 32
Q_DEV = 128
P_DEV = 1024
H = 2048
Q = 32768
P_SIZE = 65536
CAP = 24


def row_scales(key, count, low, high):
    return jnp.exp(jax.random.uniform(key, (count, 1), jnp.float32, math.log(low), math.log(high)))


def layout(key):
    base_key = jax.random.fold_in(key, 7001)
    groups = P_SIZE // P_DEV
    owner_keys = jax.random.split(jax.random.fold_in(base_key, 1), groups)
    owner_perm = jax.vmap(lambda one_key: jax.random.permutation(one_key, P_DEV))(owner_keys).astype(jnp.int32)
    id_of_row = jax.random.permutation(jax.random.fold_in(base_key, 2), P_SIZE).astype(jnp.int32)
    location = jnp.argsort(id_of_row).astype(jnp.int32)
    hot_where = (jnp.arange(groups, dtype=jnp.int32)[:, None] * P_DEV + owner_perm[:, :HOT_DEV]).reshape(H)
    hot_list = id_of_row[hot_where]
    return (owner_perm, id_of_row, location, hot_list)


def draw_location(key, part):
    return layout(key)[2]


def draw_hot_ids(key, part):
    return layout(key)[3]


def draw_candidates(key, part):
    owner_perm, id_of_row, location, hot_list = layout(key)
    groups = P_SIZE // P_DEV
    rep_count = Q // (Q_DEV * groups)
    blocks = Q // Q_DEV
    cold_passage_count = Q_DEV * COLD
    tickets = groups * CAP
    busy = jax.random.randint(jax.random.fold_in(key, 7101), (rep_count,), 0, groups)

    def one_block(block_num):
        blk_key = jax.random.fold_in(jax.random.fold_in(key, 7201), block_num)
        ticket_owner = jnp.arange(tickets, dtype=jnp.int32) // CAP
        order = jax.random.permutation(jax.random.fold_in(blk_key, 1), tickets).astype(jnp.int32)
        priority = order - (ticket_owner == busy[block_num % rep_count]).astype(jnp.int32) * tickets
        chosen = jnp.argsort(priority)[:cold_passage_count]
        owners = ticket_owner[chosen]
        owners = owners[jax.random.permutation(jax.random.fold_in(blk_key, 2), cold_passage_count)]
        pick = jax.random.randint(jax.random.fold_in(blk_key, 3), (cold_passage_count,), HOT_DEV, P_DEV)
        local_rows = owner_perm[owners, pick]
        cold_ids = id_of_row[owners * P_DEV + local_rows]
        hot_pick = jax.random.randint(jax.random.fold_in(blk_key, 4), (Q_DEV * (K - COLD),), 0, H)
        hot_part = hot_list[hot_pick]
        merged = jnp.concatenate([cold_ids.reshape(Q_DEV, COLD), hot_part.reshape(Q_DEV, K - COLD)], axis=1)
        sort_keys = jax.random.randint(jax.random.fold_in(blk_key, 5), (Q_DEV, K), 0, 1 << 20) * K + jnp.arange(K, dtype=jnp.int32)[None, :]
        placing = jnp.argsort(sort_keys, axis=1)
        return jnp.take_along_axis(merged, placing, axis=1)
    return lax.map(one_block, jnp.arange(blocks, dtype=jnp.int32)).reshape(Q, K).astype(jnp.int32)


def draw_queries(key, part):
    spread = row_scales(jax.random.fold_in(key, 101), Q, 0.3, 3.0)
    values = jax.random.truncated_normal(jax.random.fold_in(key, 102), -6.0, 6.0, (Q, D), jnp.float32) * spread
    return values.astype(jnp.bfloat16)


def draw_slab(key, part):
    spread = row_scales(jax.random.fold_in(key, 201), P_SIZE, 0.5, 2.0)
    values = jax.random.truncated_normal(jax.random.fold_in(key, 202), -6.0, 6.0, (P_SIZE, D), jnp.float32) * spread
    return values.astype(jnp.bfloat16)


def draw_teacher(key, part):
    values = 2.5 * jax.random.truncated_normal(jax.random.fold_in(key, 302), -6.0, 6.0, (Q, K), jnp.float32)
    return values


def setup_inputs(seed: int = 0) -> dict:
    streams_of = jax.random.split(jax.random.key(seed), 7)
    return {
        "queries": draw_queries(jax.random.fold_in(streams_of[6], 71), 0),
        "teacher": draw_teacher(jax.random.fold_in(streams_of[6], 71), 0),
        "slab": draw_slab(jax.random.fold_in(streams_of[6], 71), 0),
        "candidates": draw_candidates(jax.random.fold_in(streams_of[6], 71), 0),
        "hot_ids": draw_hot_ids(jax.random.fold_in(streams_of[6], 71), 0),
        "location": draw_location(jax.random.fold_in(streams_of[6], 71), 0),
    }


def distill(student_logits, hot_scores, teacher, cold_mask, hot_index):
    row_top = jnp.maximum(lax.optimization_barrier(jnp.max(student_logits, axis=1)), lax.optimization_barrier(jnp.max(hot_scores, axis=1)))[:, None]
    totals = lax.optimization_barrier(jnp.sum(jnp.exp(student_logits - row_top), axis=1)) + lax.optimization_barrier(jnp.sum(jnp.exp(hot_scores - row_top), axis=1))
    log_partition_total = row_top[:, 0] + jnp.log(totals)
    teach_top = lax.optimization_barrier(jnp.max(teacher, axis=1, keepdims=True))
    shifted = teacher - teach_top
    log_target = shifted - jnp.log(lax.optimization_barrier(jnp.sum(jnp.exp(shifted), axis=1, keepdims=True)))
    target = jnp.exp(log_target)
    loss_rows = lax.optimization_barrier(jnp.sum(target * (log_target - student_logits), axis=1)) + log_partition_total
    d_scores = jnp.exp(student_logits - log_partition_total[:, None]) - target
    d_hot = jnp.exp(hot_scores - log_partition_total[:, None])
    row_index = jnp.broadcast_to(jnp.arange(student_logits.shape[0], dtype=jnp.int32)[:, None], student_logits.shape)
    coef_hot = d_hot.at[row_index, hot_index].add(jnp.where(cold_mask, 0.0, d_scores)).astype(jnp.bfloat16)
    cold_passage_weight = jnp.where(cold_mask, d_scores, 0.0).astype(jnp.bfloat16)
    return (loss_rows, coef_hot, cold_passage_weight)

def reference(queries, teacher, slab, candidates, hot_ids, location):
    logit_scale = 2.0 / math.sqrt(D)
    hot_where = location[hot_ids]
    hot_mark = jnp.full((P_SIZE,), -1, jnp.int32).at[hot_where].set(jnp.arange(H, dtype=jnp.int32))
    hot_emb = slab[hot_where]

    def block_step(carry, block_idx):
        slab_acc, hot_acc = carry
        start = (block_idx * Q_DEV).astype(jnp.int32)
        query_blk = lax.dynamic_slice_in_dim(queries, start, Q_DEV)
        teach_blk = lax.dynamic_slice_in_dim(teacher, start, Q_DEV)
        cand_blk = lax.dynamic_slice_in_dim(candidates, start, Q_DEV)
        slab_rows = location[cand_blk]
        hot_slot = hot_mark[slab_rows]
        cold_mask = hot_slot < 0
        hot_index = jnp.maximum(hot_slot, 0)
        selected_scores = slab[slab_rows].astype(jnp.float32)
        query_broadcast = query_blk.astype(jnp.float32)
        student_logits = logit_scale * jnp.einsum('ho,hao->ha', query_broadcast, selected_scores)
        hot_scores = logit_scale * jnp.dot(query_blk, hot_emb.T, preferred_element_type=jnp.float32)
        loss_rows, coef_hot, cold_passage_weight = distill(student_logits, hot_scores, teach_blk, cold_mask, hot_index)
        cold_score_sum = jnp.einsum('xj,xjz->xz', cold_passage_weight.astype(jnp.float32), selected_scores)
        query_grad = logit_scale * (jnp.dot(coef_hot, hot_emb, preferred_element_type=jnp.float32) + cold_score_sum)
        terms = (logit_scale * cold_passage_weight.astype(jnp.float32)[:, :, None] * query_broadcast[:, None, :]).astype(jnp.bfloat16)
        target_rows = jnp.where(cold_mask, slab_rows, P_SIZE).reshape(-1)
        slab_acc = slab_acc.at[target_rows].add(terms.reshape(-1, D).astype(jnp.float32), mode='drop')
        hot_acc = hot_acc + logit_scale * jnp.dot(coef_hot.T, query_blk, preferred_element_type=jnp.float32)
        return ((slab_acc, hot_acc), (loss_rows, query_grad))
    init = (jnp.zeros((P_SIZE, D), jnp.float32), jnp.zeros((H, D), jnp.float32))
    (slab_acc, hot_acc), (loss_rows, query_grad) = lax.scan(block_step, init, jnp.arange(Q // Q_DEV, dtype=jnp.int32))
    slab_grad = slab_acc.at[hot_where].add(hot_acc)
    return (loss_rows.reshape(Q), query_grad.reshape(Q, D), slab_grad)
```

```python
import functools
import math

import jax
import jax.numpy as jnp
from jax import lax
from jax.experimental import pallas as pl
from jax.experimental.pallas import tpu as pltpu
from jax.sharding import PartitionSpec as P

COLD = 8
LANES = 128
RADIX = 256
PAD_SLOTS = 32
F32 = jnp.float32
BF16 = jnp.bfloat16
VMEM_SPEC = pl.BlockSpec(memory_space=pltpu.VMEM)
ROWS_DOT = (((1,), (1,)), ((), ()))


def iota(shape, axis):
    return lax.broadcasted_iota(jnp.int32, shape, axis)


def one_hot(mask, dtype=BF16):
    return jnp.where(mask, 1.0, 0.0).astype(dtype)


def pick_rows(mask, values):
    return jnp.sum(jnp.where(mask, values, jnp.zeros_like(values)), axis=0, keepdims=True)


def request_kernel(per_owner, capacity, groups, cand_t, hot_ref, loc_ref, req_ref, place_ref, sel_ref, hit_t):
    cand_count, q_rows = cand_t.shape
    hot_total = hot_ref.shape[1]
    high_rows = loc_ref.shape[0]
    hot = hot_ref[...]
    low_hot = one_hot(iota((RADIX, hot_total), 0) == (hot & (RADIX - 1)))
    high_hot = one_hot(iota((high_rows, hot_total), 0) == (hot // RADIX))
    marks = lax.dot_general(low_hot, high_hot, ROWS_DOT, preferred_element_type=F32).astype(BF16)
    low_iota = iota((RADIX, q_rows), 0)
    high_iota = iota((high_rows, q_rows), 0)

    def lookup(tables, ids):
        hots = jnp.concatenate([one_hot(high_iota == (i // RADIX)) for i in ids], axis=1)
        found = [jnp.dot(t, hots, preferred_element_type=F32) for t in tables]
        masks = [low_iota == (i & (RADIX - 1)) for i in ids]
        return [
            [pick_rows(m, f[:, n * q_rows : (n + 1) * q_rows]) for n, m in enumerate(masks)]
            for f in found
        ]

    def check(j, carry):
        start = pl.multiple_of(j * 8, 8)
        rows = cand_t[pl.ds(start, 8), :]
        hits = lookup([marks], [rows[n : n + 1, :] for n in range(8)])[0]
        hit_t[pl.ds(start, 8), :] = jnp.concatenate(hits, axis=0)
        return carry

    lax.fori_loop(0, cand_count // 8, check, 0)
    cold = hit_t[...] < 0.5
    earlier = one_hot(iota((cand_count, cand_count), 0) > iota((cand_count, cand_count), 1))
    order = jnp.dot(earlier, one_hot(cold), preferred_element_type=F32).astype(jnp.int32)
    sel = jnp.where(cold, order, -1)
    sel_ref[...] = sel
    cand = cand_t[...]
    ids = [pick_rows(sel == r, cand) for r in range(COLD)]
    loc = loc_ref[...]
    high_table = jnp.transpose((loc // RADIX).astype(F32)).astype(BF16)
    low_table = jnp.transpose((loc & (RADIX - 1)).astype(F32)).astype(BF16)
    high_part, low_part = lookup([high_table, low_table], ids)
    before = one_hot(iota((q_rows, q_rows), 0) < iota((q_rows, q_rows), 1))
    owner_iota = iota((groups, q_rows), 0)
    slot_iota = iota((LANES, q_rows), 0)
    query = iota((1, q_rows), 1).astype(F32)
    base = jnp.zeros((groups, 1), F32)
    owners, ranks, owner_hots, low_vals, high_vals, query_vals = [], [], [], [], [], []
    for r in range(COLD):
        row = high_part[r].astype(jnp.int32) * RADIX + low_part[r].astype(jnp.int32)
        owner = row // per_owner
        local = row & (per_owner - 1)
        owner_hot = one_hot(owner_iota == owner, F32)
        count = jnp.dot(owner_hot.astype(BF16), before, preferred_element_type=F32) + base
        rank = jnp.sum(owner_hot * count, axis=0, keepdims=True).astype(jnp.int32)
        base = base + jnp.sum(owner_hot, axis=1, keepdims=True)
        at_slot = slot_iota == rank
        owners.append(owner)
        ranks.append(rank)
        owner_hots.append(owner_hot.astype(BF16))
        low_vals.append(jnp.where(at_slot, (local & (RADIX - 1)).astype(F32), 0.0).astype(BF16))
        high_vals.append(jnp.where(at_slot, (local // RADIX + RADIX // 2).astype(F32), 0.0).astype(BF16))
        query_vals.append(jnp.where(at_slot, query, 0.0).astype(BF16))
    owner_all = jnp.concatenate(owner_hots, axis=1)

    def spread(vals):
        got = lax.dot_general(owner_all, jnp.concatenate(vals, axis=1), ROWS_DOT, preferred_element_type=F32)
        return got.astype(jnp.int32)

    low_got, high_got, query_got = spread(low_vals), spread(high_vals), spread(query_vals)
    packed = low_got + RADIX * (high_got - RADIX // 2) + per_owner * query_got
    req_ref[...] = jnp.where(high_got > 0, packed, -1)
    place_ref[...] = jnp.concatenate(owners + ranks, axis=0)


def count_kernel(cand_t, teacher_ref, hot_ref, sel_ref, count_ref, target_ref, misc_ref, soft_t):
    cand_count, q_rows = cand_t.shape
    teacher = teacher_ref[...]
    shifted = teacher - jnp.max(teacher, axis=0, keepdims=True)
    log_target = shifted - jnp.log(jnp.sum(jnp.exp(shifted), axis=0, keepdims=True))
    target = jnp.exp(log_target)
    soft_t[...] = target
    sel = sel_ref[...]
    entropy = jnp.sum(target * log_target, axis=0, keepdims=True)
    rows = [pick_rows(sel == r, target) for r in range(COLD)]
    misc_ref[...] = jnp.concatenate(rows + [jnp.broadcast_to(entropy, (8, q_rows))], axis=0)
    hot_cols = jnp.transpose(hot_ref[...])
    for a in range(hot_ref.shape[0]):
        column = jnp.broadcast_to(hot_cols[:, a : a + 1], (LANES, q_rows))

        def add(k, carry):
            count, total = carry
            match = column == cand_t[pl.ds(k, 1), :]
            count = count + jnp.where(match, 1.0, 0.0)
            total = total + jnp.where(match, soft_t[pl.ds(k, 1), :], 0.0)
            return count, total

        start = (jnp.ones((LANES, q_rows), F32), jnp.zeros((LANES, q_rows), F32))
        count, total = lax.fori_loop(0, cand_count, add, start, unroll=4)
        count_ref[a * LANES : (a + 1) * LANES, :] = count
        target_ref[a * LANES : (a + 1) * LANES, :] = total


def score_kernel(scale, capacity, q_ref, hot_ref, found_ref, count_ref, target_ref, place_ref, misc_ref, loss_ref, pay_ref, weight_ref, hot_scr, slot_scr):
    groups, hot_each, feat = hot_ref.shape
    slots = found_ref.shape[0]
    q_rows = q_ref.shape[0]
    q = q_ref[...]
    step = 8
    place = place_ref[...]
    dests = [place[r : r + 1] * capacity + place[COLD + r : COLD + r + 1] for r in range(COLD)]
    top = jnp.full((1, q_rows), -jnp.inf, F32)
    for j in range(groups // step):
        rows = hot_ref[j * step : (j + 1) * step].reshape(step * hot_each, feat)
        got = scale * lax.dot_general(rows, q, ROWS_DOT, preferred_element_type=F32)
        hot_scr[j * step * hot_each : (j + 1) * step * hot_each, :] = got
        top = jnp.maximum(top, jnp.max(got, axis=0, keepdims=True))
    colds = [jnp.zeros((1, q_rows), F32) for _ in range(COLD)]
    chunk = 256
    for j in range(slots // chunk):
        rows = found_ref[j * chunk : (j + 1) * chunk, :]
        got = scale * lax.dot_general(rows, q, ROWS_DOT, preferred_element_type=F32)
        ids = iota((chunk, q_rows), 0) + j * chunk
        for r in range(COLD):
            colds[r] = colds[r] + pick_rows(ids == dests[r], got)
    cold = jnp.concatenate(colds, axis=0)
    top = jnp.maximum(top, jnp.max(cold, axis=0, keepdims=True))
    total = jnp.sum(jnp.exp(cold - top), axis=0, keepdims=True)
    hot_dot = jnp.zeros((1, q_rows), F32)
    for j in range(groups // step):
        part = slice(j * step * hot_each, (j + 1) * step * hot_each)
        hot = hot_scr[part, :]
        total = total + jnp.sum(count_ref[part, :] * jnp.exp(hot - top), axis=0, keepdims=True)
        hot_dot = hot_dot + jnp.sum(target_ref[part, :] * hot, axis=0, keepdims=True)
    log_total = top + jnp.log(total)
    cold_target = misc_ref[0:COLD, :]
    entropy = misc_ref[COLD : COLD + 1, :]
    loss_ref[...] = entropy - hot_dot - jnp.sum(cold_target * cold, axis=0, keepdims=True) + log_total
    weight = (jnp.exp(cold - log_total) - cold_target).astype(BF16).astype(F32)
    owner_iota = iota((groups, q_rows), 0)
    slot_iota = iota((LANES, q_rows), 0)
    owner_all = jnp.concatenate([one_hot(owner_iota == place[r : r + 1]) for r in range(COLD)], axis=1)
    slot_all = jnp.concatenate(
        [
            jnp.where(slot_iota == place[COLD + r : COLD + r + 1], weight[r : r + 1], 0.0).astype(BF16)
            for r in range(COLD)
        ],
        axis=1,
    )
    slot_scr[...] = lax.dot_general(owner_all, slot_all, ROWS_DOT, preferred_element_type=F32)
    for g in range(groups):
        part = slice(g * hot_each, (g + 1) * hot_each)
        coef = count_ref[part, :] * jnp.exp(hot_scr[part, :] - log_total) - target_ref[part, :]
        slot_row = jnp.broadcast_to(slot_scr[g : g + 1, :], (8, q_rows))
        pay_ref[g] = jnp.concatenate([coef, slot_row], axis=0).astype(BF16)
    for j in range(slots // chunk):
        ids = iota((chunk, q_rows), 0) + j * chunk
        made = jnp.zeros((chunk, q_rows), F32)
        for r in range(COLD):
            made = jnp.where(ids == dests[r], weight[r : r + 1], made)
        weight_ref[j * chunk : (j + 1) * chunk, :] = made.astype(BF16)


def query_kernel(scale, hot_ref, pay_ref, found_ref, weight_ref, out_ref):
    groups, hot_each, feat = hot_ref.shape
    acc = jnp.zeros(out_ref.shape, F32)
    step = 8
    first = (((0,), (0,)), ((), ()))
    for j in range(groups // step):
        rows = hot_ref[j * step : (j + 1) * step].reshape(step * hot_each, feat)
        coef = jnp.concatenate([pay_ref[j * step + n, 0:hot_each, :] for n in range(step)], axis=0)
        acc = acc + lax.dot_general(coef, rows, first, preferred_element_type=F32)
    chunk = 256
    for j in range(found_ref.shape[0] // chunk):
        part = slice(j * chunk, (j + 1) * chunk)
        acc = acc + lax.dot_general(weight_ref[part, :], found_ref[part, :], first, preferred_element_type=F32)
    out_ref[...] = scale * acc


def slab_kernel(scale, pay_ref, query_ref, row_ref, loc_ref, out_ref, terms, hot_acc):
    step = pl.program_id(0)
    groups = pay_ref.shape[0]
    hot_each = hot_acc.shape[0]
    feat = out_ref.shape[1]

    @pl.when(step == 0)
    def _():
        hot_acc[...] = jnp.zeros_like(hot_acc)

    acc = hot_acc[...]
    for n in range(0, groups, 2):
        left = jnp.concatenate([pay_ref[n, 0:hot_each, :], pay_ref[n + 1, 0:hot_each, :]], axis=1)
        right = jnp.concatenate([query_ref[n], query_ref[n + 1]], axis=0)
        acc = acc + jnp.dot(left, right, preferred_element_type=F32)
    hot_acc[...] = acc
    sent = jnp.concatenate([pay_ref[n, hot_each : hot_each + 8, :].astype(F32)[0:1] for n in range(groups)], axis=0)
    cols = jnp.transpose(sent)
    made = []
    for n in range(groups):
        col = scale * jnp.broadcast_to(cols[0:PAD_SLOTS, n : n + 1], (PAD_SLOTS, LANES))
        wide = jnp.concatenate([col] * (feat // LANES), axis=1)
        rows = row_ref[n * PAD_SLOTS : (n + 1) * PAD_SLOTS, :].astype(F32)
        made.append((wide * rows).astype(BF16))
    size = groups * PAD_SLOTS
    terms[pl.ds(pl.multiple_of(step * size, size), size), :] = jnp.concatenate(made, axis=0)

    @pl.when(step == pl.num_programs(0) - 1)
    def _():
        full = scale * hot_acc[...]
        high = full.astype(BF16)
        rest = full - high.astype(F32)
        mid = rest.astype(BF16)
        low = (rest - mid.astype(F32)).astype(BF16)
        base = terms.shape[0] - LANES
        terms[base:, :] = jnp.concatenate([high, mid, low, jnp.zeros_like(low)], axis=0)
        loc = loc_ref[...]
        tile = 128

        def land(j, carry):
            start = pl.multiple_of(j * tile, tile)
            at = one_hot(iota((tile, loc.shape[1]), 0) + start == loc)
            got = jnp.dot(at, terms[...], preferred_element_type=F32)
            out_ref[pl.ds(start, tile), :] = got.astype(BF16)
            return carry

        lax.fori_loop(0, out_ref.shape[0] // tile, land, 0)


def shards(queries, teacher, slab, candidates, hot_ids, location):
    groups = lax.axis_size("corpus")
    reps = lax.axis_size("rep")
    corpus_idx = lax.axis_index("corpus")
    q_rows, feat = queries.shape
    per_owner = slab.shape[0]
    hot_total = hot_ids.shape[0]
    hot_each = hot_total // groups
    cand_count = candidates.shape[1]
    capacity = q_rows * COLD * 3 // (2 * groups)
    scale = 2.0 / math.sqrt(feat)
    mine = lax.dynamic_slice_in_dim(hot_ids, corpus_idx * hot_each, hot_each)
    own_hot = location[mine] - corpus_idx * per_owner
    sent_rows = jnp.concatenate([queries, slab[own_hot]], axis=0)
    cand_t, sent_rows = lax.optimization_barrier((candidates.T, sent_rows))
    gathered = lax.all_gather(sent_rows, "corpus", axis=0, tiled=False)
    req, place, sel = pl.pallas_call(
        functools.partial(request_kernel, per_owner, capacity, groups),
        out_shape=(
            jax.ShapeDtypeStruct((groups, LANES), jnp.int32),
            jax.ShapeDtypeStruct((2 * COLD, q_rows), jnp.int32),
            jax.ShapeDtypeStruct((cand_count, q_rows), jnp.int32),
        ),
        in_specs=[VMEM_SPEC] * 3,
        out_specs=(VMEM_SPEC,) * 3,
        scratch_shapes=[pltpu.VMEM((cand_count, q_rows), F32)],
        name="request",
    )(cand_t, hot_ids.reshape(1, hot_total), location.reshape(-1, RADIX))
    asked = lax.all_to_all(req.reshape(groups, 1, LANES), "corpus", split_axis=0, concat_axis=0, tiled=True)
    asked = asked.reshape(groups, LANES)
    asked_slots = jnp.maximum(asked[:, :capacity], 0)
    found = slab[asked_slots & (per_owner - 1)]
    found = lax.all_to_all(found, "corpus", split_axis=0, concat_axis=0, tiled=True)
    found = found.reshape(groups * capacity, feat)
    count, target, misc = pl.pallas_call(
        count_kernel,
        out_shape=(
            jax.ShapeDtypeStruct((hot_total, q_rows), F32),
            jax.ShapeDtypeStruct((hot_total, q_rows), F32),
            jax.ShapeDtypeStruct((2 * COLD, q_rows), F32),
        ),
        in_specs=[VMEM_SPEC] * 4,
        out_specs=(VMEM_SPEC,) * 3,
        scratch_shapes=[pltpu.VMEM((cand_count, q_rows), F32)],
        cost_estimate=pl.CostEstimate(flops=80_000_000, bytes_accessed=3_000_000, transcendentals=10_000),
        name="count",
    )(cand_t, teacher.T, hot_ids.reshape(-1, LANES), sel)
    hot_block = pl.BlockSpec((groups, hot_each, feat), lambda i: (0, q_rows // hot_each, 0))

    def whole(shape):
        return pl.BlockSpec(shape, lambda i: (0,) * len(shape))

    slots = groups * capacity
    pay_rows = hot_each + 8
    loss, pay, weight = pl.pallas_call(
        functools.partial(score_kernel, scale, capacity),
        grid=(1,),
        out_shape=(
            jax.ShapeDtypeStruct((1, q_rows), F32),
            jax.ShapeDtypeStruct((groups, pay_rows, q_rows), BF16),
            jax.ShapeDtypeStruct((slots, q_rows), BF16),
        ),
        in_specs=[
            whole((q_rows, feat)),
            hot_block,
            whole((slots, feat)),
            whole((hot_total, q_rows)),
            whole((hot_total, q_rows)),
            whole((2 * COLD, q_rows)),
            whole((2 * COLD, q_rows)),
        ],
        out_specs=(whole((1, q_rows)), whole((groups, pay_rows, q_rows)), whole((slots, q_rows))),
        scratch_shapes=[pltpu.VMEM((hot_total, q_rows), F32), pltpu.VMEM((groups, q_rows), F32)],
        name="score",
    )(queries, gathered, found, count, target, place, misc)
    got = lax.all_to_all(pay, "corpus", split_axis=0, concat_axis=0, tiled=True)
    query_grad = pl.pallas_call(
        functools.partial(query_kernel, scale),
        grid=(1,),
        out_shape=jax.ShapeDtypeStruct((q_rows, feat), F32),
        in_specs=[hot_block, whole((groups, pay_rows, q_rows)), whole((slots, feat)), whole((slots, q_rows))],
        out_specs=whole((q_rows, feat)),
        cost_estimate=pl.CostEstimate(flops=700_000_000, bytes_accessed=7_000_000, transcendentals=0),
        name="query_grad",
    )(gathered, pay, found, weight)
    padded = asked[:, :PAD_SLOTS]
    valid = padded >= 0
    source = jnp.arange(groups, dtype=jnp.int32)[:, None] * (q_rows + hot_each)
    query_rows = gathered.reshape(-1, feat)[(source + jnp.maximum(padded, 0) // per_owner).reshape(-1)]
    local = jnp.where(valid, padded & (per_owner - 1), -1).reshape(1, -1)
    tail = jnp.full((LANES - 3 * hot_each,), -1, jnp.int32)
    local = jnp.concatenate([local, jnp.concatenate([own_hot, own_hot, own_hot, tail])[None, :]], axis=1)
    step = 8
    partial_grad = pl.pallas_call(
        functools.partial(slab_kernel, scale),
        grid=(groups // step,),
        out_shape=jax.ShapeDtypeStruct((per_owner, feat), BF16),
        in_specs=[
            pl.BlockSpec((step, pay_rows, q_rows), lambda i: (i, 0, 0)),
            pl.BlockSpec((step, q_rows, feat), lambda i: (i, 0, 0)),
            pl.BlockSpec((step * PAD_SLOTS, feat), lambda i: (i, 0)),
            whole((1, groups * PAD_SLOTS + LANES)),
        ],
        out_specs=whole((per_owner, feat)),
        scratch_shapes=[
            pltpu.VMEM((groups * PAD_SLOTS + LANES, feat), BF16),
            pltpu.VMEM((hot_each, feat), F32),
        ],
        name="slab_grad",
    )(got, gathered, query_rows, local)
    parts = lax.all_to_all(
        partial_grad.reshape(reps, per_owner // reps, feat), "rep", split_axis=0, concat_axis=0, tiled=True
    )
    slab_grad = jnp.sum(parts.astype(F32), axis=0)
    return (loss.reshape(q_rows), query_grad, slab_grad)


def solution(mesh):
    return jax.shard_map(
        shards,
        mesh=mesh,
        in_specs=(
            P(("corpus", "rep"), None),
            P(("corpus", "rep"), None),
            P("corpus", None),
            P(("corpus", "rep"), None),
            P(),
            P(),
        ),
        out_specs=(P(("corpus", "rep")), P(("corpus", "rep"), None), P(("corpus", "rep"), None)),
        check_vma=False,
    )
```

```python
import functools
import math

import jax
import jax.numpy as jnp
from jax import lax
from jax.experimental import pallas as pl
from jax.experimental.pallas import tpu as pltpu
from jax.sharding import PartitionSpec as P


COLD = 8
LANES = 128
X_SIZE, Z_SIZE, CORES = 4, 8, 2
RADIX = 256
PAD_SLOTS = 32
F32 = jnp.float32
BF16 = jnp.bfloat16
VMEM_SPEC = pl.BlockSpec(memory_space=pltpu.VMEM)
SMEM_SPEC = pl.BlockSpec(memory_space=pltpu.SMEM)
ROWS_DOT = (((1,), (1,)), ((), ()))


def iota(shape, axis):
    return lax.broadcasted_iota(jnp.int32, shape, axis)


def one_hot(mask, dtype=BF16):
    return jnp.where(mask, 1.0, 0.0).astype(dtype)


def pick_rows(mask, values):
    return jnp.sum(jnp.where(mask, values, jnp.zeros_like(values)), axis=0, keepdims=True)


def request_kernel(per_owner, groups, cand_t, hot_ref, loc_ref, req_ref, place_ref, sel_ref, hit_t):
    cand_count, q_rows = cand_t.shape
    hot_total = hot_ref.shape[1]
    high_rows = loc_ref.shape[0]
    hot = hot_ref[...]
    low_hot = one_hot(iota((RADIX, hot_total), 0) == (hot & (RADIX - 1)))
    high_hot = one_hot(iota((high_rows, hot_total), 0) == (hot // RADIX))
    marks = lax.dot_general(low_hot, high_hot, ROWS_DOT, preferred_element_type=F32).astype(BF16)
    low_iota = iota((RADIX, q_rows), 0)
    high_iota = iota((high_rows, q_rows), 0)

    def lookup(tables, ids):
        hots = jnp.concatenate([one_hot(high_iota == (i // RADIX)) for i in ids], axis=1)
        found = [jnp.dot(t, hots, preferred_element_type=F32) for t in tables]
        masks = [low_iota == (i & (RADIX - 1)) for i in ids]
        return [
            [pick_rows(m, f[:, n * q_rows : (n + 1) * q_rows]) for n, m in enumerate(masks)]
            for f in found
        ]

    def check(j, carry):
        start = pl.multiple_of(j * 8, 8)
        rows = cand_t[pl.ds(start, 8), :]
        hits = lookup([marks], [rows[n : n + 1, :] for n in range(8)])[0]
        hit_t[pl.ds(start, 8), :] = jnp.concatenate(hits, axis=0)
        return carry

    lax.fori_loop(0, cand_count // 8, check, 0)
    cold = hit_t[...] < 0.5
    earlier = one_hot(iota((cand_count, cand_count), 0) > iota((cand_count, cand_count), 1))
    order = jnp.dot(earlier, one_hot(cold), preferred_element_type=F32).astype(jnp.int32)
    sel = jnp.where(cold, order, -1)
    sel_ref[...] = sel
    cand = cand_t[...]
    ids = [pick_rows(sel == r, cand) for r in range(COLD)]
    loc = loc_ref[...]
    high_table = jnp.transpose((loc // RADIX).astype(F32)).astype(BF16)
    low_table = jnp.transpose((loc & (RADIX - 1)).astype(F32)).astype(BF16)
    high_part, low_part = lookup([high_table, low_table], ids)
    before = one_hot(iota((q_rows, q_rows), 0) < iota((q_rows, q_rows), 1))
    owner_iota = iota((groups, q_rows), 0)
    slot_iota = iota((LANES, q_rows), 0)
    query = iota((1, q_rows), 1).astype(F32)
    base = jnp.zeros((groups, 1), F32)
    owners, ranks, owner_hots, low_vals, high_vals, query_vals = [], [], [], [], [], []
    for r in range(COLD):
        row = high_part[r].astype(jnp.int32) * RADIX + low_part[r].astype(jnp.int32)
        owner = row // per_owner
        local = row & (per_owner - 1)
        owner_hot = one_hot(owner_iota == owner, F32)
        count = jnp.dot(owner_hot.astype(BF16), before, preferred_element_type=F32) + base
        rank = jnp.sum(owner_hot * count, axis=0, keepdims=True).astype(jnp.int32)
        base = base + jnp.sum(owner_hot, axis=1, keepdims=True)
        at_slot = slot_iota == rank
        owners.append(owner)
        ranks.append(rank)
        owner_hots.append(owner_hot.astype(BF16))
        low_vals.append(jnp.where(at_slot, (local & (RADIX - 1)).astype(F32), 0.0).astype(BF16))
        high_vals.append(jnp.where(at_slot, (local // RADIX + RADIX // 2).astype(F32), 0.0).astype(BF16))
        query_vals.append(jnp.where(at_slot, query, 0.0).astype(BF16))
    owner_all = jnp.concatenate(owner_hots, axis=1)

    def spread(vals):
        got = lax.dot_general(owner_all, jnp.concatenate(vals, axis=1), ROWS_DOT, preferred_element_type=F32)
        return got.astype(jnp.int32)

    low_got, high_got, query_got = spread(low_vals), spread(high_vals), spread(query_vals)
    packed = low_got + RADIX * (high_got - RADIX // 2) + per_owner * query_got
    req_ref[...] = jnp.where(high_got > 0, packed, -1)
    place_ref[...] = jnp.concatenate(owners + ranks, axis=0)


def owner_of(spot_ref, piece, z):
    x = (spot_ref[0] - piece % X_SIZE) & (X_SIZE - 1)
    core = spot_ref[1] ^ (piece // X_SIZE)
    return (x * Z_SIZE + z) * CORES + core


def fetch_kernel(capacity, asked_ref, slab_ref, out_ref):
    groups = asked_ref.shape[0]
    per_owner = slab_ref.shape[0]
    asked = jnp.maximum(asked_ref[...], 0)
    cols = jnp.transpose((asked & (per_owner - 1)).astype(F32))
    step = 16
    lane = iota((capacity, per_owner), 1).astype(F32)
    for j in range(groups // step):
        picks = [
            one_hot(lane == jnp.broadcast_to(cols[0:capacity, n : n + 1], (capacity, per_owner)), F32)
            for n in range(j * step, (j + 1) * step)
        ]
        got = jnp.dot(jnp.concatenate(picks, axis=0).astype(BF16), slab_ref[...], preferred_element_type=F32)
        out_ref[j * step * capacity : (j + 1) * step * capacity, :] = got.astype(BF16)


def count_kernel(cand_t, teacher_ref, hot_ref, sel_ref, count_ref, target_ref, misc_ref, soft_t):
    cand_count, q_rows = cand_t.shape
    teacher = teacher_ref[...]
    shifted = teacher - jnp.max(teacher, axis=0, keepdims=True)
    log_target = shifted - jnp.log(jnp.sum(jnp.exp(shifted), axis=0, keepdims=True))
    target = jnp.exp(log_target)
    soft_t[...] = target
    sel = sel_ref[...]
    entropy = jnp.sum(target * log_target, axis=0, keepdims=True)
    rows = [pick_rows(sel == r, target) for r in range(COLD)]
    misc_ref[...] = jnp.concatenate(rows + [jnp.broadcast_to(entropy, (8, q_rows))], axis=0)
    hot_cols = jnp.transpose(hot_ref[...])
    for a in range(hot_ref.shape[0]):
        column = jnp.broadcast_to(hot_cols[:, a : a + 1], (LANES, q_rows))

        def add(k, carry):
            count, total = carry
            match = column == cand_t[pl.ds(k, 1), :]
            count = count + jnp.where(match, 1.0, 0.0)
            total = total + jnp.where(match, soft_t[pl.ds(k, 1), :], 0.0)
            return count, total

        start = (jnp.ones((LANES, q_rows), F32), jnp.zeros((LANES, q_rows), F32))
        count, total = lax.fori_loop(0, cand_count, add, start, unroll=4)
        count_ref[a * LANES : (a + 1) * LANES, :] = count
        target_ref[a * LANES : (a + 1) * LANES, :] = total


def score_kernel(scale, capacity, spot_ref, q_ref, *refs):
    hot_refs, refs = refs[: X_SIZE * CORES], refs[X_SIZE * CORES :]
    score_body(scale, capacity, spot_ref, q_ref, hot_refs, *refs)


def score_body(scale, capacity, spot_ref, q_ref, hot_refs, found_ref, count_ref, target_ref, place_ref, misc_ref, loss_ref, pay_ref, weight_ref, hot_scr, slot_scr):
    groups = pay_ref.shape[0]
    hot_each = hot_scr.shape[0] // groups
    slots = found_ref.shape[0]
    q_rows = q_ref.shape[0]
    q = q_ref[...]
    step = 8
    place = place_ref[...]
    dests = [place[r : r + 1] * capacity + place[COLD + r : COLD + r + 1] for r in range(COLD)]
    top = jnp.full((1, q_rows), -jnp.inf, F32)
    for piece, hot_ref in enumerate(hot_refs):
        got = scale * lax.dot_general(hot_ref[...], q, ROWS_DOT, preferred_element_type=F32)
        for z in range(Z_SIZE):
            start = pl.multiple_of(owner_of(spot_ref, piece, z) * hot_each, hot_each)
            hot_scr[pl.ds(start, hot_each), :] = got[z * hot_each : (z + 1) * hot_each]
        top = jnp.maximum(top, jnp.max(got, axis=0, keepdims=True))
    colds = [jnp.zeros((1, q_rows), F32) for _ in range(COLD)]
    chunk = 256
    for j in range(slots // chunk):
        rows = found_ref[j * chunk : (j + 1) * chunk, :]
        got = scale * lax.dot_general(rows, q, ROWS_DOT, preferred_element_type=F32)
        ids = iota((chunk, q_rows), 0) + j * chunk
        for r in range(COLD):
            colds[r] = colds[r] + pick_rows(ids == dests[r], got)
    cold = jnp.concatenate(colds, axis=0)
    top = jnp.maximum(top, jnp.max(cold, axis=0, keepdims=True))
    total = jnp.sum(jnp.exp(cold - top), axis=0, keepdims=True)
    hot_dot = jnp.zeros((1, q_rows), F32)
    for j in range(groups // step):
        part = slice(j * step * hot_each, (j + 1) * step * hot_each)
        hot = hot_scr[part, :]
        total = total + jnp.sum(count_ref[part, :] * jnp.exp(hot - top), axis=0, keepdims=True)
        hot_dot = hot_dot + jnp.sum(target_ref[part, :] * hot, axis=0, keepdims=True)
    log_total = top + jnp.log(total)
    cold_target = misc_ref[0:COLD, :]
    entropy = misc_ref[COLD : COLD + 1, :]
    loss_ref[...] = entropy - hot_dot - jnp.sum(cold_target * cold, axis=0, keepdims=True) + log_total
    weight = (jnp.exp(cold - log_total) - cold_target).astype(BF16).astype(F32)
    owner_iota = iota((groups, q_rows), 0)
    slot_iota = iota((LANES, q_rows), 0)
    owner_all = jnp.concatenate([one_hot(owner_iota == place[r : r + 1]) for r in range(COLD)], axis=1)
    slot_all = jnp.concatenate(
        [
            jnp.where(slot_iota == place[COLD + r : COLD + r + 1], weight[r : r + 1], 0.0).astype(BF16)
            for r in range(COLD)
        ],
        axis=1,
    )
    slot_scr[...] = lax.dot_general(owner_all, slot_all, ROWS_DOT, preferred_element_type=F32)
    for g in range(groups):
        part = slice(g * hot_each, (g + 1) * hot_each)
        coef = count_ref[part, :] * jnp.exp(hot_scr[part, :] - log_total) - target_ref[part, :]
        slot_row = jnp.broadcast_to(slot_scr[g : g + 1, :], (8, q_rows))
        pay_ref[g] = jnp.concatenate([coef, slot_row], axis=0).astype(BF16)
    for j in range(slots // chunk):
        ids = iota((chunk, q_rows), 0) + j * chunk
        made = jnp.zeros((chunk, q_rows), F32)
        for r in range(COLD):
            made = jnp.where(ids == dests[r], weight[r : r + 1], made)
        weight_ref[j * chunk : (j + 1) * chunk, :] = made.astype(BF16)


def query_kernel(scale, spot_ref, *refs):
    hot_refs = refs[: X_SIZE * CORES]
    pay_ref, found_ref, weight_ref, out_ref = refs[X_SIZE * CORES :]
    hot_each = hot_refs[0].shape[0] // Z_SIZE
    acc = jnp.zeros(out_ref.shape, F32)
    first = (((0,), (0,)), ((), ()))
    for piece, hot_ref in enumerate(hot_refs):
        owners = [owner_of(spot_ref, piece, z) for z in range(Z_SIZE)]
        coef = jnp.concatenate([pay_ref[o, 0:hot_each, :] for o in owners], axis=0)
        acc = acc + lax.dot_general(coef, hot_ref[...], first, preferred_element_type=F32)
    chunk = 256
    for j in range(found_ref.shape[0] // chunk):
        part = slice(j * chunk, (j + 1) * chunk)
        acc = acc + lax.dot_general(weight_ref[part, :], found_ref[part, :], first, preferred_element_type=F32)
    out_ref[...] = scale * acc


def slab_kernel(scale, pay_ref, query_ref, row_ref, loc_ref, out_ref, terms, hot_acc):
    step = pl.program_id(0)
    groups = pay_ref.shape[0]
    hot_each = hot_acc.shape[0]
    feat = out_ref.shape[1]

    @pl.when(step == 0)
    def _():
        hot_acc[...] = jnp.zeros_like(hot_acc)

    acc = hot_acc[...]
    for n in range(0, groups, 2):
        left = jnp.concatenate([pay_ref[n, 0:hot_each, :], pay_ref[n + 1, 0:hot_each, :]], axis=1)
        right = jnp.concatenate([query_ref[n], query_ref[n + 1]], axis=0)
        acc = acc + jnp.dot(left, right, preferred_element_type=F32)
    hot_acc[...] = acc
    sent = jnp.concatenate([pay_ref[n, hot_each : hot_each + 8, :].astype(F32)[0:1] for n in range(groups)], axis=0)
    cols = jnp.transpose(sent)
    made = []
    for n in range(groups):
        col = scale * jnp.broadcast_to(cols[0:PAD_SLOTS, n : n + 1], (PAD_SLOTS, LANES))
        wide = jnp.concatenate([col] * (feat // LANES), axis=1)
        rows = row_ref[n * PAD_SLOTS : (n + 1) * PAD_SLOTS, :].astype(F32)
        made.append((wide * rows).astype(BF16))
    size = groups * PAD_SLOTS
    terms[pl.ds(pl.multiple_of(step * size, size), size), :] = jnp.concatenate(made, axis=0)

    @pl.when(step == pl.num_programs(0) - 1)
    def _():
        full = scale * hot_acc[...]
        high = full.astype(BF16)
        rest = full - high.astype(F32)
        mid = rest.astype(BF16)
        low = (rest - mid.astype(F32)).astype(BF16)
        base = terms.shape[0] - LANES
        terms[base:, :] = jnp.concatenate([high, mid, low, jnp.zeros_like(low)], axis=0)
        loc = loc_ref[...]
        tile = 512

        def land(j, carry):
            start = pl.multiple_of(j * tile, tile)
            at = one_hot(iota((tile, loc.shape[1]), 0) + start == loc)
            got = jnp.dot(at, terms[...], preferred_element_type=F32)
            out_ref[pl.ds(start, tile), :] = got.astype(BF16)
            return carry

        lax.fori_loop(0, out_ref.shape[0] // tile, land, 0)


def gather_hot(rows):
    def member(x, z, core):
        return (x * Z_SIZE + z) * CORES + core

    chips = [(x, z, c) for x in range(X_SIZE) for z in range(Z_SIZE) for c in range(CORES)]
    along_z = [[member(x, z, c) for z in range(Z_SIZE)] for x in range(X_SIZE) for c in range(CORES)]
    rows = lax.all_gather(rows, "corpus", axis=0, tiled=True, axis_index_groups=along_z)
    pieces = [rows]
    for d in range(1, X_SIZE):
        moves = [(member(x, z, c), member((x + d) % X_SIZE, z, c)) for x, z, c in chips]
        pieces.append(lax.ppermute(rows, "corpus", moves))
    swap = [(member(x, z, c), member(x, z, CORES - 1 - c)) for x, z, c in chips]
    return pieces + [lax.ppermute(p, "corpus", swap) for p in pieces]


def shards(queries, teacher, slab, candidates, hot_ids, location):
    groups = lax.axis_size("corpus")
    reps = lax.axis_size("rep")
    corpus_idx = lax.axis_index("corpus")
    q_rows, feat = queries.shape
    per_owner = slab.shape[0]
    hot_total = hot_ids.shape[0]
    hot_each = hot_total // groups
    cand_count = candidates.shape[1]
    capacity = q_rows * COLD * 3 // (2 * groups)
    scale = 2.0 / math.sqrt(feat)
    gathered = lax.all_gather(queries, "corpus", axis=0, tiled=False)
    cand_t = candidates.T
    req, place, sel = pl.pallas_call(
        functools.partial(request_kernel, per_owner, groups),
        out_shape=(
            jax.ShapeDtypeStruct((groups, LANES), jnp.int32),
            jax.ShapeDtypeStruct((2 * COLD, q_rows), jnp.int32),
            jax.ShapeDtypeStruct((cand_count, q_rows), jnp.int32),
        ),
        in_specs=[VMEM_SPEC] * 3,
        out_specs=(VMEM_SPEC,) * 3,
        scratch_shapes=[pltpu.VMEM((cand_count, q_rows), F32)],
        name="request",
    )(cand_t, hot_ids.reshape(1, hot_total), location.reshape(-1, RADIX))
    asked = lax.all_to_all(req.reshape(groups, 1, LANES), "corpus", split_axis=0, concat_axis=0, tiled=True)
    asked = asked.reshape(groups, LANES)
    wanted = pl.pallas_call(
        functools.partial(fetch_kernel, capacity),
        out_shape=jax.ShapeDtypeStruct((groups * capacity, feat), BF16),
        in_specs=[VMEM_SPEC] * 2,
        out_specs=VMEM_SPEC,
        name="fetch",
    )(asked, slab)
    mine = lax.dynamic_slice_in_dim(hot_ids, corpus_idx * hot_each, hot_each)
    own_hot = location[mine] - corpus_idx * per_owner
    own_rows, wanted = lax.optimization_barrier((slab[own_hot], wanted))
    found = lax.all_to_all(wanted.reshape(groups, capacity, feat), "corpus", split_axis=0, concat_axis=0, tiled=True)
    found = found.reshape(groups * capacity, feat)
    hot_rows = gather_hot(own_rows)
    spot = jnp.stack([corpus_idx // (Z_SIZE * CORES), corpus_idx % CORES]).astype(jnp.int32)
    count, target, misc = pl.pallas_call(
        count_kernel,
        out_shape=(
            jax.ShapeDtypeStruct((hot_total, q_rows), F32),
            jax.ShapeDtypeStruct((hot_total, q_rows), F32),
            jax.ShapeDtypeStruct((2 * COLD, q_rows), F32),
        ),
        in_specs=[VMEM_SPEC] * 4,
        out_specs=(VMEM_SPEC,) * 3,
        scratch_shapes=[pltpu.VMEM((cand_count, q_rows), F32)],
        cost_estimate=pl.CostEstimate(flops=80_000_000, bytes_accessed=3_000_000, transcendentals=10_000),
        name="count",
    )(cand_t, teacher.T, hot_ids.reshape(-1, LANES), sel)

    def whole(shape):
        return pl.BlockSpec(shape, lambda i: (0,) * len(shape))

    slots = groups * capacity
    pay_rows = hot_each + 8
    loss, pay, weight = pl.pallas_call(
        functools.partial(score_kernel, scale, capacity),
        grid=(1,),
        out_shape=(
            jax.ShapeDtypeStruct((1, q_rows), F32),
            jax.ShapeDtypeStruct((groups, pay_rows, q_rows), BF16),
            jax.ShapeDtypeStruct((slots, q_rows), BF16),
        ),
        in_specs=[
            SMEM_SPEC,
            whole((q_rows, feat)),
            *[whole(h.shape) for h in hot_rows],
            whole((slots, feat)),
            whole((hot_total, q_rows)),
            whole((hot_total, q_rows)),
            whole((2 * COLD, q_rows)),
            whole((2 * COLD, q_rows)),
        ],
        out_specs=(whole((1, q_rows)), whole((groups, pay_rows, q_rows)), whole((slots, q_rows))),
        scratch_shapes=[pltpu.VMEM((hot_total, q_rows), F32), pltpu.VMEM((groups, q_rows), F32)],
        name="score",
    )(spot, queries, *hot_rows, found, count, target, place, misc)
    got = lax.all_to_all(pay, "corpus", split_axis=0, concat_axis=0, tiled=True)
    query_grad = pl.pallas_call(
        functools.partial(query_kernel, scale),
        grid=(1,),
        out_shape=jax.ShapeDtypeStruct((q_rows, feat), F32),
        in_specs=[SMEM_SPEC, *[whole(h.shape) for h in hot_rows], whole((groups, pay_rows, q_rows)), whole((slots, feat)), whole((slots, q_rows))],
        out_specs=whole((q_rows, feat)),
        cost_estimate=pl.CostEstimate(flops=700_000_000, bytes_accessed=7_000_000, transcendentals=0),
        name="query_grad",
    )(spot, *hot_rows, pay, found, weight)
    padded = asked[:, :PAD_SLOTS]
    valid = padded >= 0
    source = jnp.arange(groups, dtype=jnp.int32)[:, None] * q_rows
    query_rows = gathered.reshape(-1, feat)[(source + jnp.maximum(padded, 0) // per_owner).reshape(-1)]
    local = jnp.where(valid, padded & (per_owner - 1), -1).reshape(1, -1)
    tail = jnp.full((LANES - 3 * hot_each,), -1, jnp.int32)
    local = jnp.concatenate([local, jnp.concatenate([own_hot, own_hot, own_hot, tail])[None, :]], axis=1)
    step = 8
    partial_grad = pl.pallas_call(
        functools.partial(slab_kernel, scale),
        grid=(groups // step,),
        out_shape=jax.ShapeDtypeStruct((per_owner, feat), BF16),
        in_specs=[
            pl.BlockSpec((step, pay_rows, q_rows), lambda i: (i, 0, 0)),
            pl.BlockSpec((step, q_rows, feat), lambda i: (i, 0, 0)),
            pl.BlockSpec((step * PAD_SLOTS, feat), lambda i: (i, 0)),
            whole((1, groups * PAD_SLOTS + LANES)),
        ],
        out_specs=whole((per_owner, feat)),
        scratch_shapes=[
            pltpu.VMEM((groups * PAD_SLOTS + LANES, feat), BF16),
            pltpu.VMEM((hot_each, feat), F32),
        ],
        name="slab_grad",
    )(got, gathered, query_rows, local)
    parts = lax.all_to_all(
        partial_grad.reshape(reps, per_owner // reps, feat), "rep", split_axis=0, concat_axis=0, tiled=True
    )
    slab_grad = jnp.sum(parts.astype(F32), axis=0)
    return (loss.reshape(q_rows), query_grad, slab_grad)


def solution(mesh):
    return jax.shard_map(
        shards,
        mesh=mesh,
        in_specs=(
            P(("corpus", "rep"), None),
            P(("corpus", "rep"), None),
            P("corpus", None),
            P(("corpus", "rep"), None),
            P(),
            P(),
        ),
        out_specs=(P(("corpus", "rep")), P(("corpus", "rep"), None), P(("corpus", "rep"), None)),
        check_vma=False,
    )
```

```python
import functools
import math

import jax
import jax.numpy as jnp
from jax import lax
from jax.experimental import pallas as pl
from jax.experimental.pallas import tpu as pltpu
from jax.sharding import PartitionSpec as P

COLD = 8
LANES = 128
RADIX = 256
F32 = jnp.float32
BF16 = jnp.bfloat16
VMEM_SPEC = pl.BlockSpec(memory_space=pltpu.VMEM)
SMEM_SPEC = pl.BlockSpec(memory_space=pltpu.SMEM)
ROWS_DOT = (((1,), (1,)), ((), ()))


def iota(shape, axis):
    return lax.broadcasted_iota(jnp.int32, shape, axis)


def one_hot(mask, dtype=BF16):
    return jnp.where(mask, 1.0, 0.0).astype(dtype)


def pick_rows(mask, values):
    return jnp.sum(jnp.where(mask, values, jnp.zeros_like(values)), axis=0, keepdims=True)


def request_kernel(per_owner, capacity, groups, cand_t, hot_ref, loc_ref, req_ref, place_ref, sel_ref, hit_t):
    cand_count, q_rows = cand_t.shape
    hot_total = hot_ref.shape[1]
    high_rows = loc_ref.shape[0] // 2
    hot = hot_ref[...]
    low_hot = one_hot(iota((RADIX, hot_total), 0) == (hot & (RADIX - 1)))
    high_hot = one_hot(iota((high_rows, hot_total), 0) == (hot // RADIX))
    marks = lax.dot_general(low_hot, high_hot, ROWS_DOT, preferred_element_type=F32).astype(BF16)
    low_iota = iota((RADIX, q_rows), 0)
    high_iota = iota((high_rows, q_rows), 0)

    def lookup(tables, ids):
        hots = jnp.concatenate([one_hot(high_iota == (i // RADIX)) for i in ids], axis=1)
        found = [jnp.dot(t, hots, preferred_element_type=F32) for t in tables]
        masks = [low_iota == (i & (RADIX - 1)) for i in ids]
        return [
            [pick_rows(m, f[:, n * q_rows : (n + 1) * q_rows]) for n, m in enumerate(masks)]
            for f in found
        ]

    def check(j, carry):
        start = pl.multiple_of(j * 8, 8)
        rows = cand_t[pl.ds(start, 8), :]
        hits = lookup([marks], [rows[n : n + 1, :] for n in range(8)])[0]
        hit_t[pl.ds(start, 8), :] = jnp.concatenate(hits, axis=0)
        return carry

    lax.fori_loop(0, cand_count // 8, check, 0)
    cold = hit_t[...] < 0.5
    earlier = one_hot(iota((cand_count, cand_count), 0) > iota((cand_count, cand_count), 1))
    order = jnp.dot(earlier, one_hot(cold), preferred_element_type=F32).astype(jnp.int32)
    sel = jnp.where(cold, order, -1)
    sel_ref[...] = sel
    cand = cand_t[...]
    ids = [pick_rows(sel == r, cand) for r in range(COLD)]
    loc = jnp.concatenate([loc_ref[pl.ds(0, high_rows, stride=2), :], loc_ref[pl.ds(1, high_rows, stride=2), :]], axis=1)
    high_table = jnp.transpose((loc // RADIX).astype(F32)).astype(BF16)
    low_table = jnp.transpose((loc & (RADIX - 1)).astype(F32)).astype(BF16)
    high_part, low_part = lookup([high_table, low_table], ids)
    before = one_hot(iota((q_rows, q_rows), 0) < iota((q_rows, q_rows), 1))
    owner_iota = iota((groups, q_rows), 0)
    slot_iota = iota((LANES, q_rows), 0)
    query = iota((1, q_rows), 1).astype(F32)
    base = jnp.zeros((groups, 1), F32)
    owners, ranks, owner_hots, low_vals, high_vals, query_vals = [], [], [], [], [], []
    for r in range(COLD):
        row = high_part[r].astype(jnp.int32) * RADIX + low_part[r].astype(jnp.int32)
        owner = row // per_owner
        local = row & (per_owner - 1)
        owner_hot = one_hot(owner_iota == owner, F32)
        count = jnp.dot(owner_hot.astype(BF16), before, preferred_element_type=F32) + base
        rank = jnp.sum(owner_hot * count, axis=0, keepdims=True).astype(jnp.int32)
        base = base + jnp.sum(owner_hot, axis=1, keepdims=True)
        at_slot = slot_iota == rank
        owners.append(owner)
        ranks.append(rank)
        owner_hots.append(owner_hot.astype(BF16))
        low_vals.append(jnp.where(at_slot, (local & (RADIX - 1)).astype(F32), 0.0).astype(BF16))
        high_vals.append(jnp.where(at_slot, (local // RADIX + RADIX // 2).astype(F32), 0.0).astype(BF16))
        query_vals.append(jnp.where(at_slot, query, 0.0).astype(BF16))
    owner_all = jnp.concatenate(owner_hots, axis=1)

    def spread(vals):
        got = lax.dot_general(owner_all, jnp.concatenate(vals, axis=1), ROWS_DOT, preferred_element_type=F32)
        return got.astype(jnp.int32)

    low_got, high_got, query_got = spread(low_vals), spread(high_vals), spread(query_vals)
    packed = low_got + RADIX * (high_got - RADIX // 2) + per_owner * query_got
    req_ref[...] = jnp.where(high_got > 0, packed, -1)
    place_ref[...] = jnp.concatenate(owners + ranks, axis=0)


def prep_kernel(per_owner, spot_ref, q_ref, hot_ref, loc_ref, slab_ref, out_ref, col_scr):
    hot_each = out_ref.shape[0] - q_ref.shape[0]
    high_rows = loc_ref.shape[0]
    ids = hot_ref[pl.ds(spot_ref[0] * hot_each // LANES, 1), :]
    high_hot = one_hot(iota((high_rows, LANES), 0) == (ids // LANES))
    low_mask = iota((LANES, LANES), 0) == (ids & (LANES - 1))
    loc = loc_ref[...]
    first = (((0,), (0,)), ((), ()))
    high = jnp.transpose((loc // RADIX).astype(F32)).astype(BF16)
    low = jnp.transpose((loc & (RADIX - 1)).astype(F32)).astype(BF16)
    high = pick_rows(low_mask, jnp.dot(high, high_hot, preferred_element_type=F32))
    low = pick_rows(low_mask, jnp.dot(low, high_hot, preferred_element_type=F32))
    local = high * RADIX + low - (spot_ref[0] * per_owner).astype(F32)
    col_scr[...] = jnp.transpose(jnp.broadcast_to(local, (LANES, LANES)))
    start = pl.multiple_of(spot_ref[0] * hot_each % LANES, hot_each)
    cols = jnp.concatenate([col_scr[pl.ds(start, hot_each), :]] * (per_owner // LANES), axis=1)
    picks = one_hot(iota((hot_each, per_owner), 1).astype(F32) == cols)
    rows = jnp.dot(picks, slab_ref[...], preferred_element_type=F32).astype(BF16)
    out_ref[0 : q_ref.shape[0], :] = q_ref[...]
    out_ref[q_ref.shape[0] :, :] = rows


def fetch_kernel(capacity, asked_ref, slab_ref, out_ref):
    groups = asked_ref.shape[0]
    per_owner = slab_ref.shape[0]
    asked = jnp.maximum(asked_ref[...], 0)
    cols = jnp.transpose((asked & (per_owner - 1)).astype(F32))
    lane = iota((capacity, per_owner), 1).astype(F32)
    picks = [
        one_hot(lane == jnp.broadcast_to(cols[0:capacity, n : n + 1], (capacity, per_owner)), F32)
        for n in range(groups)
    ]
    got = jnp.dot(jnp.concatenate(picks, axis=0).astype(BF16), slab_ref[...], preferred_element_type=F32)
    out_ref[...] = got.astype(BF16)


def cold_kernel(scale, capacity, q_ref, found_ref, place_ref, cold_ref):
    q_rows = q_ref.shape[0]
    q = q_ref[...]
    place = place_ref[...]
    dests = [place[r : r + 1] * capacity + place[COLD + r : COLD + r + 1] for r in range(COLD)]
    colds = [jnp.zeros((1, q_rows), F32) for _ in range(COLD)]
    chunk = 256
    for j in range(found_ref.shape[0] // chunk):
        rows = found_ref[j * chunk : (j + 1) * chunk, :]
        got = scale * lax.dot_general(rows, q, ROWS_DOT, preferred_element_type=F32)
        ids = iota((chunk, q_rows), 0) + j * chunk
        for r in range(COLD):
            colds[r] = colds[r] + pick_rows(ids == dests[r], got)
    cold_ref[...] = jnp.concatenate(colds, axis=0)


def count_kernel(cand_t, teacher_ref, hot_ref, sel_ref, count_ref, target_ref, misc_ref, soft_t):
    cand_count, q_rows = cand_t.shape
    teacher = teacher_ref[...]
    shifted = teacher - jnp.max(teacher, axis=0, keepdims=True)
    log_target = shifted - jnp.log(jnp.sum(jnp.exp(shifted), axis=0, keepdims=True))
    target = jnp.exp(log_target)
    soft_t[...] = target
    sel = sel_ref[...]
    entropy = jnp.sum(target * log_target, axis=0, keepdims=True)
    rows = [pick_rows(sel == r, target) for r in range(COLD)]
    misc_ref[...] = jnp.concatenate(rows + [jnp.broadcast_to(entropy, (8, q_rows))], axis=0)
    hot_cols = jnp.transpose(hot_ref[...])
    for a in range(hot_ref.shape[0]):
        column = jnp.broadcast_to(hot_cols[:, a : a + 1], (LANES, q_rows))

        def add(k, carry):
            count, total = carry
            match = column == cand_t[pl.ds(k, 1), :]
            count = count + jnp.where(match, 1.0, 0.0)
            total = total + jnp.where(match, soft_t[pl.ds(k, 1), :], 0.0)
            return count, total

        start = (jnp.ones((LANES, q_rows), F32), jnp.zeros((LANES, q_rows), F32))
        count, total = lax.fori_loop(0, cand_count, add, start, unroll=4)
        count_ref[a * LANES : (a + 1) * LANES, :] = count
        target_ref[a * LANES : (a + 1) * LANES, :] = total


def score_kernel(scale, q_ref, hot_ref, cold_ref, count_ref, target_ref, place_ref, misc_ref, loss_ref, pay_ref, weight_ref, hot_scr, top_scr, slot_scr):
    step = pl.program_id(0)
    each, hot_each, feat = hot_ref.shape
    groups = pay_ref.shape[0]
    q_rows = q_ref.shape[0]
    size = each * hot_each

    @pl.when(step == 0)
    def _():
        top_scr[...] = jnp.max(cold_ref[...], axis=0, keepdims=True)

    got = scale * lax.dot_general(hot_ref[...].reshape(size, feat), q_ref[...], ROWS_DOT, preferred_element_type=F32)
    hot_scr[pl.ds(pl.multiple_of(step * size, size), size), :] = got
    top_scr[...] = jnp.maximum(top_scr[...], jnp.max(got, axis=0, keepdims=True))

    @pl.when(step == pl.num_programs(0) - 1)
    def _():
        cold = cold_ref[...]
        top = top_scr[...]
        place = place_ref[...]
        total = jnp.sum(jnp.exp(cold - top), axis=0, keepdims=True)
        hot_dot = jnp.zeros((1, q_rows), F32)
        for j in range(groups // 8):
            part = slice(j * 8 * hot_each, (j + 1) * 8 * hot_each)
            hot = hot_scr[part, :]
            total = total + jnp.sum(count_ref[part, :] * jnp.exp(hot - top), axis=0, keepdims=True)
            hot_dot = hot_dot + jnp.sum(target_ref[part, :] * hot, axis=0, keepdims=True)
        log_total = top + jnp.log(total)
        cold_target = misc_ref[0:COLD, :]
        entropy = misc_ref[COLD : COLD + 1, :]
        loss_ref[...] = entropy - hot_dot - jnp.sum(cold_target * cold, axis=0, keepdims=True) + log_total
        weight = (jnp.exp(cold - log_total) - cold_target).astype(BF16).astype(F32)
        weight_ref[...] = weight
        owner_iota = iota((groups, q_rows), 0)
        slot_iota = iota((LANES, q_rows), 0)
        owner_all = jnp.concatenate([one_hot(owner_iota == place[r : r + 1]) for r in range(COLD)], axis=1)
        slot_all = jnp.concatenate(
            [
                jnp.where(slot_iota == place[COLD + r : COLD + r + 1], weight[r : r + 1], 0.0).astype(BF16)
                for r in range(COLD)
            ],
            axis=1,
        )
        slot_scr[...] = lax.dot_general(owner_all, slot_all, ROWS_DOT, preferred_element_type=F32)
        for g in range(groups):
            part = slice(g * hot_each, (g + 1) * hot_each)
            coef = count_ref[part, :] * jnp.exp(hot_scr[part, :] - log_total) - target_ref[part, :]
            slot_row = jnp.broadcast_to(slot_scr[g : g + 1, :], (8, q_rows))
            pay_ref[g] = jnp.concatenate([coef, slot_row], axis=0).astype(BF16)


def query_kernel(scale, capacity, hot_ref, pay_ref, found_ref, weight_ref, place_ref, out_ref):
    groups, hot_each, feat = hot_ref.shape
    q_rows = out_ref.shape[0]
    acc = jnp.zeros(out_ref.shape, F32)
    step = 8
    first = (((0,), (0,)), ((), ()))
    for j in range(groups // step):
        rows = hot_ref[j * step : (j + 1) * step].reshape(step * hot_each, feat)
        coef = jnp.concatenate([pay_ref[j * step + n, 0:hot_each, :] for n in range(step)], axis=0)
        acc = acc + lax.dot_general(coef, rows, first, preferred_element_type=F32)
    chunk = 256
    place = place_ref[...]
    weight = weight_ref[...]
    dests = [place[r : r + 1] * capacity + place[COLD + r : COLD + r + 1] for r in range(COLD)]
    for j in range(found_ref.shape[0] // chunk):
        ids = iota((chunk, q_rows), 0) + j * chunk
        made = jnp.zeros((chunk, q_rows), F32)
        for r in range(COLD):
            made = jnp.where(ids == dests[r], weight[r : r + 1], made)
        rows = found_ref[j * chunk : (j + 1) * chunk, :]
        acc = acc + lax.dot_general(made.astype(BF16), rows, first, preferred_element_type=F32)
    out_ref[...] = scale * acc


def slab_kernel(scale, capacity, spot_ref, pay_ref, query_ref, row_ref, loc_ref, *refs):
    outs, (terms, hot_acc) = refs[:-2], refs[-2:]
    step = pl.program_id(0)
    groups = pay_ref.shape[0]
    hot_each, feat = hot_acc.shape

    @pl.when(step == 0)
    def _():
        hot_acc[...] = jnp.zeros_like(hot_acc)

    acc = hot_acc[...]
    for n in range(0, groups, 2):
        left = jnp.concatenate([pay_ref[n, 0:hot_each, :], pay_ref[n + 1, 0:hot_each, :]], axis=1)
        right = jnp.concatenate([query_ref[n], query_ref[n + 1]], axis=0)
        acc = acc + jnp.dot(left, right, preferred_element_type=F32)
    hot_acc[...] = acc
    sent = jnp.concatenate([pay_ref[n, hot_each : hot_each + 8, :].astype(F32)[0:1] for n in range(groups)], axis=0)
    cols = scale * jnp.transpose(sent)
    col = jnp.concatenate(
        [jnp.broadcast_to(cols[0:capacity, n : n + 1], (capacity, LANES)) for n in range(groups)], axis=0
    )
    size = groups * capacity
    wide = jnp.concatenate([col] * (feat // LANES), axis=1)
    made = (wide * row_ref[...].astype(F32)).astype(BF16)
    terms[pl.ds(pl.multiple_of(step * size, size), size), :] = made

    @pl.when(step == pl.num_programs(0) - 1)
    def _():
        full = scale * hot_acc[...]
        high = full.astype(BF16)
        rest = full - high.astype(F32)
        mid = rest.astype(BF16)
        low = (rest - mid.astype(F32)).astype(BF16)
        base = terms.shape[0] - LANES
        terms[base:, :] = jnp.concatenate([high, mid, low, jnp.zeros_like(low)], axis=0)
        loc = loc_ref[...]
        rows = outs[0].shape[0]
        ids = iota((rows, loc.shape[1]), 0)
        for d in range(0, len(outs), 2):
            starts = [(spot_ref[1] + e) % len(outs) * rows for e in (d, d + 1)]
            at = jnp.concatenate([one_hot(ids + start == loc) for start in starts], axis=0)
            got = jnp.dot(at, terms[...], preferred_element_type=F32)
            outs[d][...] = got[:rows].astype(outs[d].dtype)
            outs[d + 1][...] = got[rows:].astype(outs[d + 1].dtype)


def shards(queries, teacher, slab, candidates, hot_ids, location):
    groups = lax.axis_size("corpus")
    reps = lax.axis_size("rep")
    corpus_idx = lax.axis_index("corpus")
    q_rows, feat = queries.shape
    per_owner = slab.shape[0]
    hot_total = hot_ids.shape[0]
    hot_each = hot_total // groups
    cand_count = candidates.shape[1]
    capacity = q_rows * COLD * 3 // (2 * groups)
    scale = 2.0 / math.sqrt(feat)
    rep_idx = lax.axis_index("rep")
    spot = jnp.stack([corpus_idx, rep_idx]).astype(jnp.int32)
    loc_table = location.reshape(-1, LANES)
    hot_table = hot_ids.reshape(-1, LANES)
    sent_rows = pl.pallas_call(
        functools.partial(prep_kernel, per_owner),
        out_shape=jax.ShapeDtypeStruct((q_rows + hot_each, feat), BF16),
        in_specs=[SMEM_SPEC] + [VMEM_SPEC] * 4,
        out_specs=VMEM_SPEC,
        scratch_shapes=[pltpu.VMEM((LANES, LANES), F32)],
        name="prep",
    )(spot, queries, hot_table, loc_table, slab)
    cand_t, sent_rows = lax.optimization_barrier((candidates.T, sent_rows))
    gathered = lax.all_gather(sent_rows, "corpus", axis=0, tiled=False)
    req, place, sel = pl.pallas_call(
        functools.partial(request_kernel, per_owner, capacity, groups),
        out_shape=(
            jax.ShapeDtypeStruct((groups, LANES), jnp.int32),
            jax.ShapeDtypeStruct((2 * COLD, q_rows), jnp.int32),
            jax.ShapeDtypeStruct((cand_count, q_rows), jnp.int32),
        ),
        in_specs=[VMEM_SPEC] * 3,
        out_specs=(VMEM_SPEC,) * 3,
        scratch_shapes=[pltpu.VMEM((cand_count, q_rows), F32)],
        name="request",
    )(cand_t, hot_ids.reshape(1, hot_total), loc_table)
    asked = lax.all_to_all(req.reshape(groups, 1, LANES), "corpus", split_axis=0, concat_axis=0, tiled=True)
    asked = asked.reshape(groups, LANES)
    slots = groups * capacity
    parts = 4
    wanted = pl.pallas_call(
        functools.partial(fetch_kernel, capacity),
        grid=(parts,),
        out_shape=jax.ShapeDtypeStruct((slots, feat), BF16),
        in_specs=[pl.BlockSpec((groups // parts, LANES), lambda i: (i, 0)), pl.BlockSpec((per_owner, feat), lambda i: (0, 0))],
        out_specs=pl.BlockSpec((slots // parts, feat), lambda i: (i, 0)),
        name="fetch",
    )(asked, slab)
    found = lax.all_to_all(wanted.reshape(groups, capacity, feat), "corpus", split_axis=0, concat_axis=0, tiled=True)
    found = found.reshape(groups * capacity, feat)
    count, target, misc = pl.pallas_call(
        count_kernel,
        out_shape=(
            jax.ShapeDtypeStruct((hot_total, q_rows), F32),
            jax.ShapeDtypeStruct((hot_total, q_rows), F32),
            jax.ShapeDtypeStruct((2 * COLD, q_rows), F32),
        ),
        in_specs=[VMEM_SPEC] * 4,
        out_specs=(VMEM_SPEC,) * 3,
        scratch_shapes=[pltpu.VMEM((cand_count, q_rows), F32)],
        cost_estimate=pl.CostEstimate(flops=80_000_000, bytes_accessed=3_000_000, transcendentals=10_000),
        name="count",
    )(cand_t, teacher.T, hot_table, sel)
    hot_block = pl.BlockSpec((groups, hot_each, feat), lambda i: (0, q_rows // hot_each, 0))

    def whole(shape):
        return pl.BlockSpec(shape, lambda i: (0,) * len(shape))

    pay_rows = hot_each + 8
    cold = pl.pallas_call(
        functools.partial(cold_kernel, scale, capacity),
        out_shape=jax.ShapeDtypeStruct((COLD, q_rows), F32),
        in_specs=[VMEM_SPEC] * 3,
        out_specs=VMEM_SPEC,
        name="cold",
    )(queries, found, place)
    each = 8
    loss, pay, weight = pl.pallas_call(
        functools.partial(score_kernel, scale),
        grid=(groups // each,),
        out_shape=(
            jax.ShapeDtypeStruct((1, q_rows), F32),
            jax.ShapeDtypeStruct((groups, pay_rows, q_rows), BF16),
            jax.ShapeDtypeStruct((COLD, q_rows), F32),
        ),
        in_specs=[
            whole((q_rows, feat)),
            pl.BlockSpec((each, hot_each, feat), lambda i: (i, q_rows // hot_each, 0)),
            whole((COLD, q_rows)),
            whole((hot_total, q_rows)),
            whole((hot_total, q_rows)),
            whole((2 * COLD, q_rows)),
            whole((2 * COLD, q_rows)),
        ],
        out_specs=(whole((1, q_rows)), whole((groups, pay_rows, q_rows)), whole((COLD, q_rows))),
        scratch_shapes=[
            pltpu.VMEM((hot_total, q_rows), F32),
            pltpu.VMEM((1, q_rows), F32),
            pltpu.VMEM((groups, q_rows), F32),
        ],
        name="score",
    )(queries, gathered, cold, count, target, place, misc)
    got = lax.all_to_all(pay, "corpus", split_axis=0, concat_axis=0, tiled=True)
    query_grad = pl.pallas_call(
        functools.partial(query_kernel, scale, capacity),
        grid=(1,),
        out_shape=jax.ShapeDtypeStruct((q_rows, feat), F32),
        in_specs=[hot_block, whole((groups, pay_rows, q_rows)), whole((slots, feat)), whole((COLD, q_rows)), whole((2 * COLD, q_rows))],
        out_specs=whole((q_rows, feat)),
        cost_estimate=pl.CostEstimate(flops=700_000_000, bytes_accessed=7_000_000, transcendentals=0),
        name="query_grad",
    )(gathered, pay, found, weight, place)
    padded = asked[:, :capacity]
    source = jnp.arange(groups, dtype=jnp.int32)[:, None] * (q_rows + hot_each)
    query_rows = gathered.reshape(-1, feat)[(source + jnp.maximum(padded, 0) // per_owner).reshape(-1)]
    local = jnp.where(padded >= 0, padded & (per_owner - 1), -1).reshape(1, -1)
    mine = lax.dynamic_slice_in_dim(hot_ids, corpus_idx * hot_each, hot_each)
    own_hot = location[mine] - corpus_idx * per_owner
    tail = jnp.full((LANES - 3 * hot_each,), -1, jnp.int32)
    local = jnp.concatenate([local, jnp.concatenate([own_hot, own_hot, own_hot, tail])[None, :]], axis=1)
    step = 8
    quarter = (per_owner // reps, feat)
    quarters = pl.pallas_call(
        functools.partial(slab_kernel, scale, capacity),
        grid=(groups // step,),
        out_shape=tuple(jax.ShapeDtypeStruct(quarter, F32 if d == 0 else BF16) for d in range(reps)),
        in_specs=[
            SMEM_SPEC,
            pl.BlockSpec((step, pay_rows, q_rows), lambda i: (i, 0, 0)),
            pl.BlockSpec((step, q_rows, feat), lambda i: (i, 0, 0)),
            pl.BlockSpec((step * capacity, feat), lambda i: (i, 0)),
            whole((1, slots + LANES)),
        ],
        out_specs=tuple(whole(quarter) for _ in range(reps)),
        scratch_shapes=[pltpu.VMEM((slots + LANES, feat), BF16), pltpu.VMEM((hot_each, feat), F32)],
        name="slab_grad",
    )(spot, got, gathered, query_rows, local)
    slab_grad = quarters[0]
    received = [
        lax.ppermute(quarters[d], "rep", [(r, (r + d) % reps) for r in range(reps)]) for d in range(1, reps)
    ]
    slab_grad = slab_grad + sum(r.astype(F32) for r in received)
    return (loss.reshape(q_rows), query_grad, slab_grad)


def solution(mesh):
    return jax.shard_map(
        shards,
        mesh=mesh,
        in_specs=(
            P(("corpus", "rep"), None),
            P(("corpus", "rep"), None),
            P("corpus", None),
            P(("corpus", "rep"), None),
            P(),
            P(),
        ),
        out_specs=(P(("corpus", "rep")), P(("corpus", "rep"), None), P(("corpus", "rep"), None)),
        check_vma=False,
    )
```

```python
import functools
import math

import jax
import jax.numpy as jnp
from jax import lax
from jax.experimental import pallas as pl
from jax.experimental.pallas import tpu as pltpu
from jax.sharding import PartitionSpec as P


COLD = 8
LANES = 128
RADIX = 256
F32 = jnp.float32
BF16 = jnp.bfloat16
VMEM_SPEC = pl.BlockSpec(memory_space=pltpu.VMEM)
SMEM_SPEC = pl.BlockSpec(memory_space=pltpu.SMEM)
ROWS_DOT = (((1,), (1,)), ((), ()))


def iota(shape, axis):
    return lax.broadcasted_iota(jnp.int32, shape, axis)


def one_hot(mask, dtype=BF16):
    return jnp.where(mask, 1.0, 0.0).astype(dtype)


def pick_rows(mask, values):
    return jnp.sum(jnp.where(mask, values, jnp.zeros_like(values)), axis=0, keepdims=True)


def request_kernel(per_owner, groups, cand_t, hot_ref, loc_ref, req_ref, place_ref, sel_ref, hit_t):
    cand_count, q_rows = cand_t.shape
    hot_total = hot_ref.shape[1]
    high_rows = loc_ref.shape[0] // 2
    hot = hot_ref[...]
    low_hot = one_hot(iota((RADIX, hot_total), 0) == (hot & (RADIX - 1)))
    high_hot = one_hot(iota((high_rows, hot_total), 0) == (hot // RADIX))
    marks = lax.dot_general(low_hot, high_hot, ROWS_DOT, preferred_element_type=F32).astype(BF16)
    low_iota = iota((RADIX, q_rows), 0)
    high_iota = iota((high_rows, q_rows), 0)

    def lookup(tables, ids):
        hots = jnp.concatenate([one_hot(high_iota == (i // RADIX)) for i in ids], axis=1)
        found = [jnp.dot(t, hots, preferred_element_type=F32) for t in tables]
        masks = [low_iota == (i & (RADIX - 1)) for i in ids]
        return [
            [pick_rows(m, f[:, n * q_rows : (n + 1) * q_rows]) for n, m in enumerate(masks)]
            for f in found
        ]

    def check(j, carry):
        start = pl.multiple_of(j * 8, 8)
        rows = cand_t[pl.ds(start, 8), :]
        hits = lookup([marks], [rows[n : n + 1, :] for n in range(8)])[0]
        hit_t[pl.ds(start, 8), :] = jnp.concatenate(hits, axis=0)
        return carry

    lax.fori_loop(0, cand_count // 8, check, 0)
    cold = hit_t[...] < 0.5
    earlier = one_hot(iota((cand_count, cand_count), 0) > iota((cand_count, cand_count), 1))
    order = jnp.dot(earlier, one_hot(cold), preferred_element_type=F32).astype(jnp.int32)
    sel = jnp.where(cold, order, -1)
    sel_ref[...] = sel
    cand = cand_t[...]
    ids = [pick_rows(sel == r, cand) for r in range(COLD)]
    loc = jnp.concatenate([loc_ref[pl.ds(0, high_rows, stride=2), :], loc_ref[pl.ds(1, high_rows, stride=2), :]], axis=1)
    high_table = jnp.transpose((loc // RADIX).astype(F32)).astype(BF16)
    low_table = jnp.transpose((loc & (RADIX - 1)).astype(F32)).astype(BF16)
    high_part, low_part = lookup([high_table, low_table], ids)
    before = one_hot(iota((q_rows, q_rows), 0) < iota((q_rows, q_rows), 1))
    owner_iota = iota((groups, q_rows), 0)
    slot_iota = iota((LANES, q_rows), 0)
    query = iota((1, q_rows), 1).astype(F32)
    base = jnp.zeros((groups, 1), F32)
    owners, ranks, owner_hots, low_vals, high_vals, query_vals = [], [], [], [], [], []
    for r in range(COLD):
        row = high_part[r].astype(jnp.int32) * RADIX + low_part[r].astype(jnp.int32)
        owner = row // per_owner
        local = row & (per_owner - 1)
        owner_hot = one_hot(owner_iota == owner, F32)
        count = jnp.dot(owner_hot.astype(BF16), before, preferred_element_type=F32) + base
        rank = jnp.sum(owner_hot * count, axis=0, keepdims=True).astype(jnp.int32)
        base = base + jnp.sum(owner_hot, axis=1, keepdims=True)
        at_slot = slot_iota == rank
        owners.append(owner)
        ranks.append(rank)
        owner_hots.append(owner_hot.astype(BF16))
        low_vals.append(jnp.where(at_slot, (local & (RADIX - 1)).astype(F32), 0.0).astype(BF16))
        high_vals.append(jnp.where(at_slot, (local // RADIX + RADIX // 2).astype(F32), 0.0).astype(BF16))
        query_vals.append(jnp.where(at_slot, query, 0.0).astype(BF16))
    owner_all = jnp.concatenate(owner_hots, axis=1)

    def spread(vals):
        got = lax.dot_general(owner_all, jnp.concatenate(vals, axis=1), ROWS_DOT, preferred_element_type=F32)
        return got.astype(jnp.int32)

    low_got, high_got, query_got = spread(low_vals), spread(high_vals), spread(query_vals)
    packed = low_got + RADIX * (high_got - RADIX // 2) + per_owner * query_got
    req_ref[...] = jnp.where(high_got > 0, packed, -1)
    place_ref[...] = jnp.concatenate(owners + ranks, axis=0)


def prep_kernel(per_owner, spot_ref, q_ref, hot_ref, loc_ref, slab_ref, out_ref, col_scr):
    hot_each = out_ref.shape[0] - q_ref.shape[0]
    high_rows = loc_ref.shape[0]
    ids = hot_ref[pl.ds(spot_ref[0] * hot_each // LANES, 1), :]
    high_hot = one_hot(iota((high_rows, LANES), 0) == (ids // LANES))
    low_mask = iota((LANES, LANES), 0) == (ids & (LANES - 1))
    loc = loc_ref[...]
    high = jnp.transpose((loc // RADIX).astype(F32)).astype(BF16)
    low = jnp.transpose((loc & (RADIX - 1)).astype(F32)).astype(BF16)
    high = pick_rows(low_mask, jnp.dot(high, high_hot, preferred_element_type=F32))
    low = pick_rows(low_mask, jnp.dot(low, high_hot, preferred_element_type=F32))
    local = high * RADIX + low - (spot_ref[0] * per_owner).astype(F32)
    col_scr[...] = jnp.transpose(jnp.broadcast_to(local, (LANES, LANES)))
    start = pl.multiple_of(spot_ref[0] * hot_each % LANES, hot_each)
    cols = jnp.concatenate([col_scr[pl.ds(start, hot_each), :]] * (per_owner // LANES), axis=1)
    picks = one_hot(iota((hot_each, per_owner), 1).astype(F32) == cols)
    rows = jnp.dot(picks, slab_ref[...], preferred_element_type=F32).astype(BF16)
    out_ref[0 : q_ref.shape[0], :] = q_ref[...]
    out_ref[q_ref.shape[0] :, :] = rows


def fetch_kernel(capacity, asked_ref, slab_ref, out_ref, picks):
    groups = asked_ref.shape[0]
    per_owner = slab_ref.shape[0]

    @pl.when(pl.program_id(0) == 0)
    def _():
        asked = jnp.maximum(asked_ref[...], 0)
        cols = jnp.transpose((asked & (per_owner - 1)).astype(F32))
        lane = iota((capacity, per_owner), 1).astype(F32)
        for n in range(0, groups, 2):
            pair = [
                one_hot(lane == jnp.broadcast_to(cols[0:capacity, m : m + 1], (capacity, per_owner)), F32)
                for m in (n, n + 1)
            ]
            picks[n * capacity : (n + 2) * capacity, :] = jnp.concatenate(pair, axis=0).astype(BF16)

    out_ref[...] = jnp.dot(picks[...], slab_ref[...], preferred_element_type=F32).astype(BF16)


def cold_kernel(scale, capacity, q_ref, found_ref, place_ref, cold_ref):
    q_rows = q_ref.shape[0]
    q = q_ref[...]
    place = place_ref[...]
    dests = [place[r : r + 1] * capacity + place[COLD + r : COLD + r + 1] for r in range(COLD)]
    colds = [jnp.zeros((1, q_rows), F32) for _ in range(COLD)]
    chunk = 256
    for j in range(found_ref.shape[0] // chunk):
        rows = found_ref[j * chunk : (j + 1) * chunk, :]
        got = scale * lax.dot_general(rows, q, ROWS_DOT, preferred_element_type=F32)
        ids = iota((chunk, q_rows), 0) + j * chunk
        for r in range(COLD):
            colds[r] = colds[r] + pick_rows(ids == dests[r], got)
    cold_ref[...] = jnp.concatenate(colds, axis=0)


def count_kernel(cand_t, teacher_ref, hot_ref, sel_ref, count_ref, target_ref, misc_ref, soft_t):
    cand_count, q_rows = cand_t.shape
    teacher = teacher_ref[...]
    shifted = teacher - jnp.max(teacher, axis=0, keepdims=True)
    log_target = shifted - jnp.log(jnp.sum(jnp.exp(shifted), axis=0, keepdims=True))
    target = jnp.exp(log_target)
    soft_t[...] = target
    sel = sel_ref[...]
    entropy = jnp.sum(target * log_target, axis=0, keepdims=True)
    rows = [pick_rows(sel == r, target) for r in range(COLD)]
    misc_ref[...] = jnp.concatenate(rows + [jnp.broadcast_to(entropy, (8, q_rows))], axis=0)
    hot_cols = jnp.transpose(hot_ref[...])
    for a in range(hot_ref.shape[0]):
        column = jnp.broadcast_to(hot_cols[:, a : a + 1], (LANES, q_rows))

        def add(k, carry):
            count, total = carry
            match = column == cand_t[pl.ds(k, 1), :]
            count = count + jnp.where(match, 1.0, 0.0)
            total = total + jnp.where(match, soft_t[pl.ds(k, 1), :], 0.0)
            return count, total

        start = (jnp.ones((LANES, q_rows), F32), jnp.zeros((LANES, q_rows), F32))
        count, total = lax.fori_loop(0, cand_count, add, start, unroll=4)
        count_ref[a * LANES : (a + 1) * LANES, :] = count
        target_ref[a * LANES : (a + 1) * LANES, :] = total


def score_kernel(scale, q_ref, hot_ref, cold_ref, count_ref, target_ref, place_ref, misc_ref, loss_ref, pay_ref, weight_ref, hot_scr, top_scr, slot_scr):
    step = pl.program_id(0)
    each, hot_each, feat = hot_ref.shape
    groups = pay_ref.shape[0]
    q_rows = q_ref.shape[0]
    size = each * hot_each

    @pl.when(step == 0)
    def _():
        top_scr[...] = jnp.max(cold_ref[...], axis=0, keepdims=True)

    got = scale * lax.dot_general(hot_ref[...].reshape(size, feat), q_ref[...], ROWS_DOT, preferred_element_type=F32)
    hot_scr[pl.ds(pl.multiple_of(step * size, size), size), :] = got
    top_scr[...] = jnp.maximum(top_scr[...], jnp.max(got, axis=0, keepdims=True))

    @pl.when(step == pl.num_programs(0) - 1)
    def _():
        cold = cold_ref[...]
        top = top_scr[...]
        place = place_ref[...]
        total = jnp.sum(jnp.exp(cold - top), axis=0, keepdims=True)
        hot_dot = jnp.zeros((1, q_rows), F32)
        for j in range(groups // 8):
            part = slice(j * 8 * hot_each, (j + 1) * 8 * hot_each)
            hot = hot_scr[part, :]
            total = total + jnp.sum(count_ref[part, :] * jnp.exp(hot - top), axis=0, keepdims=True)
            hot_dot = hot_dot + jnp.sum(target_ref[part, :] * hot, axis=0, keepdims=True)
        log_total = top + jnp.log(total)
        cold_target = misc_ref[0:COLD, :]
        entropy = misc_ref[COLD : COLD + 1, :]
        loss_ref[...] = entropy - hot_dot - jnp.sum(cold_target * cold, axis=0, keepdims=True) + log_total
        weight = (jnp.exp(cold - log_total) - cold_target).astype(BF16).astype(F32)
        weight_ref[...] = weight
        owner_iota = iota((groups, q_rows), 0)
        slot_iota = iota((LANES, q_rows), 0)
        owner_all = jnp.concatenate([one_hot(owner_iota == place[r : r + 1]) for r in range(COLD)], axis=1)
        slot_all = jnp.concatenate(
            [
                jnp.where(slot_iota == place[COLD + r : COLD + r + 1], weight[r : r + 1], 0.0).astype(BF16)
                for r in range(COLD)
            ],
            axis=1,
        )
        slot_scr[...] = lax.dot_general(owner_all, slot_all, ROWS_DOT, preferred_element_type=F32)
        for g in range(groups):
            part = slice(g * hot_each, (g + 1) * hot_each)
            coef = count_ref[part, :] * jnp.exp(hot_scr[part, :] - log_total) - target_ref[part, :]
            slot_row = jnp.broadcast_to(slot_scr[g : g + 1, :], (8, q_rows))
            pay_ref[g] = jnp.concatenate([coef, slot_row], axis=0).astype(BF16)


def query_kernel(scale, capacity, hot_ref, pay_ref, found_ref, weight_ref, place_ref, out_ref):
    groups, hot_each, feat = hot_ref.shape
    q_rows = out_ref.shape[0]
    acc = jnp.zeros(out_ref.shape, F32)
    step = 8
    first = (((0,), (0,)), ((), ()))
    for j in range(groups // step):
        rows = hot_ref[j * step : (j + 1) * step].reshape(step * hot_each, feat)
        coef = jnp.concatenate([pay_ref[j * step + n, 0:hot_each, :] for n in range(step)], axis=0)
        acc = acc + lax.dot_general(coef, rows, first, preferred_element_type=F32)
    chunk = 256
    place = place_ref[...]
    weight = weight_ref[...]
    dests = [place[r : r + 1] * capacity + place[COLD + r : COLD + r + 1] for r in range(COLD)]
    for j in range(found_ref.shape[0] // chunk):
        ids = iota((chunk, q_rows), 0) + j * chunk
        made = jnp.zeros((chunk, q_rows), F32)
        for r in range(COLD):
            made = jnp.where(ids == dests[r], weight[r : r + 1], made)
        rows = found_ref[j * chunk : (j + 1) * chunk, :]
        acc = acc + lax.dot_general(made.astype(BF16), rows, first, preferred_element_type=F32)
    out_ref[...] = scale * acc


def slab_kernel(scale, capacity, reps, spot_ref, pay_ref, query_ref, row_ref, loc_ref, first_ref, second_ref, terms, hot_acc):
    step = pl.program_id(0)
    groups = pay_ref.shape[0]
    hot_each, feat = hot_acc.shape

    @pl.when(step == 0)
    def _():
        hot_acc[...] = jnp.zeros_like(hot_acc)

    acc = hot_acc[...]
    for n in range(0, groups, 2):
        left = jnp.concatenate([pay_ref[n, 0:hot_each, :], pay_ref[n + 1, 0:hot_each, :]], axis=1)
        right = jnp.concatenate([query_ref[n], query_ref[n + 1]], axis=0)
        acc = acc + jnp.dot(left, right, preferred_element_type=F32)
    hot_acc[...] = acc
    sent = jnp.concatenate([pay_ref[n, hot_each : hot_each + 8, :].astype(F32)[0:1] for n in range(groups)], axis=0)
    cols = scale * jnp.transpose(sent)
    col = jnp.concatenate(
        [jnp.broadcast_to(cols[0:capacity, n : n + 1], (capacity, LANES)) for n in range(groups)], axis=0
    )
    size = groups * capacity
    wide = jnp.concatenate([col] * (feat // LANES), axis=1)
    made = (wide * row_ref[...].astype(F32)).astype(BF16)
    terms[pl.ds(pl.multiple_of(step * size, size), size), :] = made

    @pl.when(step == pl.num_programs(0) - 1)
    def _():
        full = scale * hot_acc[...]
        high = full.astype(BF16)
        rest = full - high.astype(F32)
        mid = rest.astype(BF16)
        low = (rest - mid.astype(F32)).astype(BF16)
        base = terms.shape[0] - LANES
        terms[base:, :] = jnp.concatenate([high, mid, low, jnp.zeros_like(low)], axis=0)
        loc = loc_ref[...]
        rows = first_ref.shape[0]
        start = (spot_ref[1] + reps // 2) % reps * (2 * rows)
        at = one_hot(iota((2 * rows, loc.shape[1]), 0) + start == loc)
        got = jnp.dot(at, terms[...], preferred_element_type=F32).astype(BF16)
        first_ref[...] = got[:rows]
        second_ref[...] = got[rows:]


def near_kernel(reps, spot_ref, terms_ref, loc_ref, *outs):
    rows = outs[0].shape[0]
    loc = loc_ref[...]
    ids = iota((rows, loc.shape[1]), 0)
    starts = [(spot_ref[1] + d) % reps * rows for d in (0, 1, reps - 1)]
    at = jnp.concatenate([one_hot(ids + start == loc) for start in starts], axis=0)
    got = jnp.dot(at, terms_ref[...], preferred_element_type=F32)
    for n, out in enumerate(outs):
        out[...] = got[n * rows : (n + 1) * rows]


def shards(queries, teacher, slab, candidates, hot_ids, location):
    groups = lax.axis_size("corpus")
    reps = lax.axis_size("rep")
    corpus_idx = lax.axis_index("corpus")
    q_rows, feat = queries.shape
    per_owner = slab.shape[0]
    hot_total = hot_ids.shape[0]
    hot_each = hot_total // groups
    cand_count = candidates.shape[1]
    capacity = q_rows * COLD * 3 // (2 * groups)
    scale = 2.0 / math.sqrt(feat)
    rep_idx = lax.axis_index("rep")
    spot = jnp.stack([corpus_idx, rep_idx]).astype(jnp.int32)
    loc_table = location.reshape(-1, LANES)
    hot_table = hot_ids.reshape(-1, LANES)
    cand_t = candidates.T
    req, place, sel = pl.pallas_call(
        functools.partial(request_kernel, per_owner, groups),
        out_shape=(
            jax.ShapeDtypeStruct((groups, LANES), jnp.int32),
            jax.ShapeDtypeStruct((2 * COLD, q_rows), jnp.int32),
            jax.ShapeDtypeStruct((cand_count, q_rows), jnp.int32),
        ),
        in_specs=[VMEM_SPEC] * 3,
        out_specs=(VMEM_SPEC,) * 3,
        scratch_shapes=[pltpu.VMEM((cand_count, q_rows), F32)],
        name="request",
    )(cand_t, hot_ids.reshape(1, hot_total), loc_table)
    sent_rows = pl.pallas_call(
        functools.partial(prep_kernel, per_owner),
        out_shape=jax.ShapeDtypeStruct((q_rows + hot_each, feat), BF16),
        in_specs=[SMEM_SPEC] + [VMEM_SPEC] * 4,
        out_specs=VMEM_SPEC,
        scratch_shapes=[pltpu.VMEM((LANES, LANES), F32)],
        name="prep",
    )(spot, queries, hot_table, loc_table, slab)
    gathered = lax.all_gather(sent_rows, "corpus", axis=0, tiled=False)
    asked = lax.all_to_all(req.reshape(groups, 1, LANES), "corpus", split_axis=0, concat_axis=0, tiled=True)
    asked = asked.reshape(groups, LANES)
    slots = groups * capacity
    block = 256
    wanted = pl.pallas_call(
        functools.partial(fetch_kernel, capacity),
        grid=(feat // block,),
        out_shape=jax.ShapeDtypeStruct((slots, feat), BF16),
        in_specs=[pl.BlockSpec((groups, LANES), lambda i: (0, 0)), pl.BlockSpec((per_owner, block), lambda i: (0, i))],
        out_specs=pl.BlockSpec((slots, block), lambda i: (0, i)),
        scratch_shapes=[pltpu.VMEM((slots, per_owner), BF16)],
        name="fetch",
    )(asked, slab)
    found = lax.all_to_all(wanted.reshape(groups, capacity, feat), "corpus", split_axis=0, concat_axis=0, tiled=True)
    found = found.reshape(groups * capacity, feat)
    count, target, misc = pl.pallas_call(
        count_kernel,
        out_shape=(
            jax.ShapeDtypeStruct((hot_total, q_rows), F32),
            jax.ShapeDtypeStruct((hot_total, q_rows), F32),
            jax.ShapeDtypeStruct((2 * COLD, q_rows), F32),
        ),
        in_specs=[VMEM_SPEC] * 4,
        out_specs=(VMEM_SPEC,) * 3,
        scratch_shapes=[pltpu.VMEM((cand_count, q_rows), F32)],
        cost_estimate=pl.CostEstimate(flops=80_000_000, bytes_accessed=3_000_000, transcendentals=10_000),
        name="count",
    )(cand_t, teacher.T, hot_table, sel)
    hot_block = pl.BlockSpec((groups, hot_each, feat), lambda i: (0, q_rows // hot_each, 0))

    def whole(shape):
        return pl.BlockSpec(shape, lambda i: (0,) * len(shape))

    pay_rows = hot_each + 8
    cold = pl.pallas_call(
        functools.partial(cold_kernel, scale, capacity),
        out_shape=jax.ShapeDtypeStruct((COLD, q_rows), F32),
        in_specs=[VMEM_SPEC] * 3,
        out_specs=VMEM_SPEC,
        name="cold",
    )(queries, found, place)
    each = 8
    loss, pay, weight = pl.pallas_call(
        functools.partial(score_kernel, scale),
        grid=(groups // each,),
        out_shape=(
            jax.ShapeDtypeStruct((1, q_rows), F32),
            jax.ShapeDtypeStruct((groups, pay_rows, q_rows), BF16),
            jax.ShapeDtypeStruct((COLD, q_rows), F32),
        ),
        in_specs=[
            whole((q_rows, feat)),
            pl.BlockSpec((each, hot_each, feat), lambda i: (i, q_rows // hot_each, 0)),
            whole((COLD, q_rows)),
            whole((hot_total, q_rows)),
            whole((hot_total, q_rows)),
            whole((2 * COLD, q_rows)),
            whole((2 * COLD, q_rows)),
        ],
        out_specs=(whole((1, q_rows)), whole((groups, pay_rows, q_rows)), whole((COLD, q_rows))),
        scratch_shapes=[
            pltpu.VMEM((hot_total, q_rows), F32),
            pltpu.VMEM((1, q_rows), F32),
            pltpu.VMEM((groups, q_rows), F32),
        ],
        name="score",
    )(queries, gathered, cold, count, target, place, misc)
    got = lax.all_to_all(pay, "corpus", split_axis=0, concat_axis=0, tiled=True)
    query_grad = pl.pallas_call(
        functools.partial(query_kernel, scale, capacity),
        grid=(1,),
        out_shape=jax.ShapeDtypeStruct((q_rows, feat), F32),
        in_specs=[hot_block, whole((groups, pay_rows, q_rows)), whole((slots, feat)), whole((COLD, q_rows)), whole((2 * COLD, q_rows))],
        out_specs=whole((q_rows, feat)),
        cost_estimate=pl.CostEstimate(flops=700_000_000, bytes_accessed=7_000_000, transcendentals=0),
        name="query_grad",
    )(gathered, pay, found, weight, place)
    padded = asked[:, :capacity]
    source = jnp.arange(groups, dtype=jnp.int32)[:, None] * (q_rows + hot_each)
    query_rows = gathered.reshape(-1, feat)[(source + jnp.maximum(padded, 0) // per_owner).reshape(-1)]
    local = jnp.where(padded >= 0, padded & (per_owner - 1), -1).reshape(1, -1)
    mine = lax.dynamic_slice_in_dim(hot_ids, corpus_idx * hot_each, hot_each)
    own_hot = location[mine] - corpus_idx * per_owner
    tail = jnp.full((LANES - 3 * hot_each,), -1, jnp.int32)
    local = jnp.concatenate([local, jnp.concatenate([own_hot, own_hot, own_hot, tail])[None, :]], axis=1)
    step = 8
    rows = per_owner // reps
    half = jax.ShapeDtypeStruct((rows // 2, feat), BF16)
    depth = slots + LANES
    first, second, terms = pl.pallas_call(
        functools.partial(slab_kernel, scale, capacity, reps),
        grid=(groups // step,),
        out_shape=(half, half, jax.ShapeDtypeStruct((depth, feat), BF16)),
        in_specs=[
            SMEM_SPEC,
            pl.BlockSpec((step, pay_rows, q_rows), lambda i: (i, 0, 0)),
            pl.BlockSpec((step, q_rows, feat), lambda i: (i, 0, 0)),
            pl.BlockSpec((step * capacity, feat), lambda i: (i, 0)),
            whole((1, depth)),
        ],
        out_specs=(whole(half.shape), whole(half.shape), whole((depth, feat))),
        scratch_shapes=[pltpu.VMEM((hot_each, feat), F32)],
        name="slab_grad",
    )(spot, got, gathered, query_rows, local)
    ahead = [(r, (r + 1) % reps) for r in range(reps)]
    behind = [(r, (r - 1) % reps) for r in range(reps)]
    first = lax.ppermute(first, "rep", ahead)
    second = lax.ppermute(second, "rep", behind)
    own, after, before = pl.pallas_call(
        functools.partial(near_kernel, reps),
        out_shape=(jax.ShapeDtypeStruct((rows, feat), F32),) * 3,
        in_specs=[SMEM_SPEC, VMEM_SPEC, VMEM_SPEC],
        out_specs=(VMEM_SPEC,) * 3,
        cost_estimate=pl.CostEstimate(flops=2_000_000_000, bytes_accessed=6_000_000, transcendentals=0),
        name="near",
    )(spot, terms, local)
    after = (after + jnp.pad(first.astype(F32), ((0, rows // 2), (0, 0)))).astype(BF16)
    before = (before + jnp.pad(second.astype(F32), ((rows // 2, 0), (0, 0)))).astype(BF16)
    after = lax.ppermute(after, "rep", ahead)
    before = lax.ppermute(before, "rep", behind)
    slab_grad = own + after.astype(F32) + before.astype(F32)
    return (loss.reshape(q_rows), query_grad, slab_grad)


def solution(mesh):
    return jax.shard_map(
        shards,
        mesh=mesh,
        in_specs=(
            P(("corpus", "rep"), None),
            P(("corpus", "rep"), None),
            P("corpus", None),
            P(("corpus", "rep"), None),
            P(),
            P(),
        ),
        out_specs=(P(("corpus", "rep")), P(("corpus", "rep"), None), P(("corpus", "rep"), None)),
        check_vma=False,
    )
```

```python
import functools
import math

import jax
import jax.numpy as jnp
from jax import lax
from jax.experimental import pallas as pl
from jax.experimental.pallas import tpu as pltpu
from jax.sharding import PartitionSpec as P


COLD = 8
LANES = 128
X_SIZE, Z_SIZE, CORES = 4, 8, 2
PIECES = X_SIZE * CORES
RADIX = 256
F32 = jnp.float32
BF16 = jnp.bfloat16
VMEM_SPEC = pl.BlockSpec(memory_space=pltpu.VMEM)
SMEM_SPEC = pl.BlockSpec(memory_space=pltpu.SMEM)
ROWS_DOT = (((1,), (1,)), ((), ()))


def iota(shape, axis):
    return lax.broadcasted_iota(jnp.int32, shape, axis)


def one_hot(mask, dtype=BF16):
    return jnp.where(mask, 1.0, 0.0).astype(dtype)


def pick_rows(mask, values):
    return jnp.sum(jnp.where(mask, values, jnp.zeros_like(values)), axis=0, keepdims=True)


def request_kernel(per_owner, groups, cand_t, hot_ref, loc_ref, req_ref, place_ref, sel_ref, hit_t):
    cand_count, q_rows = cand_t.shape
    hot_total = hot_ref.shape[1]
    high_rows = loc_ref.shape[0] // 2
    hot = hot_ref[...]
    low_hot = one_hot(iota((RADIX, hot_total), 0) == (hot & (RADIX - 1)))
    high_hot = one_hot(iota((high_rows, hot_total), 0) == (hot // RADIX))
    marks = lax.dot_general(low_hot, high_hot, ROWS_DOT, preferred_element_type=F32).astype(BF16)
    low_iota = iota((RADIX, q_rows), 0)
    high_iota = iota((high_rows, q_rows), 0)

    def lookup(tables, ids):
        hots = jnp.concatenate([one_hot(high_iota == (i // RADIX)) for i in ids], axis=1)
        found = [jnp.dot(t, hots, preferred_element_type=F32) for t in tables]
        masks = [low_iota == (i & (RADIX - 1)) for i in ids]
        return [
            [pick_rows(m, f[:, n * q_rows : (n + 1) * q_rows]) for n, m in enumerate(masks)]
            for f in found
        ]

    def check(j, carry):
        start = pl.multiple_of(j * 8, 8)
        rows = cand_t[pl.ds(start, 8), :]
        hits = lookup([marks], [rows[n : n + 1, :] for n in range(8)])[0]
        hit_t[pl.ds(start, 8), :] = jnp.concatenate(hits, axis=0)
        return carry

    lax.fori_loop(0, cand_count // 8, check, 0)
    cold = hit_t[...] < 0.5
    earlier = one_hot(iota((cand_count, cand_count), 0) > iota((cand_count, cand_count), 1))
    order = jnp.dot(earlier, one_hot(cold), preferred_element_type=F32).astype(jnp.int32)
    sel = jnp.where(cold, order, -1)
    sel_ref[...] = sel
    cand = cand_t[...]
    ids = [pick_rows(sel == r, cand) for r in range(COLD)]
    loc = jnp.concatenate([loc_ref[pl.ds(0, high_rows, stride=2), :], loc_ref[pl.ds(1, high_rows, stride=2), :]], axis=1)
    high_table = jnp.transpose((loc // RADIX).astype(F32)).astype(BF16)
    low_table = jnp.transpose((loc & (RADIX - 1)).astype(F32)).astype(BF16)
    high_part, low_part = lookup([high_table, low_table], ids)
    before = one_hot(iota((q_rows, q_rows), 0) < iota((q_rows, q_rows), 1))
    owner_iota = iota((groups, q_rows), 0)
    slot_iota = iota((LANES, q_rows), 0)
    query = iota((1, q_rows), 1).astype(F32)
    base = jnp.zeros((groups, 1), F32)
    owners, ranks, owner_hots, low_vals, high_vals, query_vals = [], [], [], [], [], []
    for r in range(COLD):
        row = high_part[r].astype(jnp.int32) * RADIX + low_part[r].astype(jnp.int32)
        owner = row // per_owner
        local = row & (per_owner - 1)
        owner_hot = one_hot(owner_iota == owner, F32)
        count = jnp.dot(owner_hot.astype(BF16), before, preferred_element_type=F32) + base
        rank = jnp.sum(owner_hot * count, axis=0, keepdims=True).astype(jnp.int32)
        base = base + jnp.sum(owner_hot, axis=1, keepdims=True)
        at_slot = slot_iota == rank
        owners.append(owner)
        ranks.append(rank)
        owner_hots.append(owner_hot.astype(BF16))
        low_vals.append(jnp.where(at_slot, (local & (RADIX - 1)).astype(F32), 0.0).astype(BF16))
        high_vals.append(jnp.where(at_slot, (local // RADIX + RADIX // 2).astype(F32), 0.0).astype(BF16))
        query_vals.append(jnp.where(at_slot, query, 0.0).astype(BF16))
    owner_all = jnp.concatenate(owner_hots, axis=1)

    def spread(vals):
        got = lax.dot_general(owner_all, jnp.concatenate(vals, axis=1), ROWS_DOT, preferred_element_type=F32)
        return got.astype(jnp.int32)

    low_got, high_got, query_got = spread(low_vals), spread(high_vals), spread(query_vals)
    packed = low_got + RADIX * (high_got - RADIX // 2) + per_owner * query_got
    req_ref[...] = jnp.where(high_got > 0, packed, -1)
    place_ref[...] = jnp.concatenate(owners + ranks, axis=0)


def prep_kernel(per_owner, spot_ref, hot_ref, loc_ref, slab_ref, out_ref, col_scr):
    hot_each = out_ref.shape[0]
    high_rows = loc_ref.shape[0]
    ids = hot_ref[pl.ds(spot_ref[0] * hot_each // LANES, 1), :]
    high_hot = one_hot(iota((high_rows, LANES), 0) == (ids // LANES))
    low_mask = iota((LANES, LANES), 0) == (ids & (LANES - 1))
    loc = loc_ref[...]
    high = jnp.transpose((loc // RADIX).astype(F32)).astype(BF16)
    low = jnp.transpose((loc & (RADIX - 1)).astype(F32)).astype(BF16)
    high = pick_rows(low_mask, jnp.dot(high, high_hot, preferred_element_type=F32))
    low = pick_rows(low_mask, jnp.dot(low, high_hot, preferred_element_type=F32))
    local = high * RADIX + low - (spot_ref[0] * per_owner).astype(F32)
    col_scr[...] = jnp.transpose(jnp.broadcast_to(local, (LANES, LANES)))
    start = pl.multiple_of(spot_ref[0] * hot_each % LANES, hot_each)
    cols = jnp.concatenate([col_scr[pl.ds(start, hot_each), :]] * (per_owner // LANES), axis=1)
    picks = one_hot(iota((hot_each, per_owner), 1).astype(F32) == cols)
    out_ref[...] = jnp.dot(picks, slab_ref[...], preferred_element_type=F32).astype(BF16)


def owner_of(spot_ref, piece, d):
    x = (spot_ref[0] // (Z_SIZE * CORES) - piece % X_SIZE) & (X_SIZE - 1)
    z = (spot_ref[0] // CORES - d) & (Z_SIZE - 1)
    core = (spot_ref[0] + piece // X_SIZE) & (CORES - 1)
    return (x * Z_SIZE + z) * CORES + core


def fetch_kernel(capacity, asked_ref, slab_ref, out_ref, picks):
    groups = asked_ref.shape[0]
    per_owner = slab_ref.shape[0]

    @pl.when(pl.program_id(0) == 0)
    def _():
        asked = jnp.maximum(asked_ref[...], 0)
        cols = jnp.transpose((asked & (per_owner - 1)).astype(F32))
        lane = iota((capacity, per_owner), 1).astype(F32)
        for n in range(0, groups, 2):
            pair = [
                one_hot(lane == jnp.broadcast_to(cols[0:capacity, m : m + 1], (capacity, per_owner)), F32)
                for m in (n, n + 1)
            ]
            picks[n * capacity : (n + 2) * capacity, :] = jnp.concatenate(pair, axis=0).astype(BF16)

    out_ref[...] = jnp.dot(picks[...], slab_ref[...], preferred_element_type=F32).astype(BF16)


def cold_kernel(scale, capacity, q_ref, found_ref, place_ref, cold_ref):
    q_rows = q_ref.shape[0]
    q = q_ref[...]
    place = place_ref[...]
    dests = [place[r : r + 1] * capacity + place[COLD + r : COLD + r + 1] for r in range(COLD)]
    chunk = 256

    def score(j, sums):
        start = pl.multiple_of(j * chunk, chunk)
        got = scale * lax.dot_general(found_ref[pl.ds(start, chunk), :], q, ROWS_DOT, preferred_element_type=F32)
        ids = iota((chunk, q_rows), 0) + start
        return [
            total + jnp.sum(jnp.where(ids == dest, got, 0.0).reshape(-1, 8, q_rows), axis=0)
            for total, dest in zip(sums, dests)
        ]

    sums = [jnp.zeros((8, q_rows), F32) for _ in range(COLD)]
    sums = lax.fori_loop(0, found_ref.shape[0] // chunk, score, sums)
    cold_ref[...] = jnp.concatenate([jnp.sum(total, axis=0, keepdims=True) for total in sums], axis=0)


def count_kernel(cand_t, teacher_ref, hot_ref, sel_ref, count_ref, target_ref, misc_ref, soft_t):
    cand_count, q_rows = cand_t.shape
    teacher = teacher_ref[...]
    shifted = teacher - jnp.max(teacher, axis=0, keepdims=True)
    log_target = shifted - jnp.log(jnp.sum(jnp.exp(shifted), axis=0, keepdims=True))
    target = jnp.exp(log_target)
    soft_t[...] = target
    sel = sel_ref[...]
    entropy = jnp.sum(target * log_target, axis=0, keepdims=True)
    rows = [pick_rows(sel == r, target) for r in range(COLD)]
    misc_ref[...] = jnp.concatenate(rows + [jnp.broadcast_to(entropy, (8, q_rows))], axis=0)
    hot_cols = jnp.transpose(hot_ref[...])
    for a in range(hot_ref.shape[0]):
        column = jnp.broadcast_to(hot_cols[:, a : a + 1], (LANES, q_rows))

        def add(k, carry):
            count, total = carry
            match = column == cand_t[pl.ds(k, 1), :]
            count = count + jnp.where(match, 1.0, 0.0)
            total = total + jnp.where(match, soft_t[pl.ds(k, 1), :], 0.0)
            return count, total

        start = (jnp.ones((LANES, q_rows), F32), jnp.zeros((LANES, q_rows), F32))
        count, total = lax.fori_loop(0, cand_count, add, start, unroll=4)
        count_ref[a * LANES : (a + 1) * LANES, :] = count
        target_ref[a * LANES : (a + 1) * LANES, :] = total


def score_kernel(scale, spot_ref, q_ref, *refs):
    score_body(scale, spot_ref, q_ref, refs[:PIECES], *refs[PIECES:])


def score_body(scale, spot_ref, q_ref, hot_refs, cold_ref, count_ref, target_ref, place_ref, misc_ref, loss_ref, pay_ref, weight_ref, hot_scr, slot_scr):
    groups = pay_ref.shape[0]
    q_rows = q_ref.shape[0]
    hot_each = hot_scr.shape[0] // groups
    q = q_ref[...]
    top = jnp.max(cold_ref[...], axis=0, keepdims=True)
    for piece, hot_ref in enumerate(hot_refs):
        got = scale * lax.dot_general(hot_ref[...], q, ROWS_DOT, preferred_element_type=F32)
        for d in range(Z_SIZE):
            start = pl.multiple_of(owner_of(spot_ref, piece, d) * hot_each, hot_each)
            hot_scr[pl.ds(start, hot_each), :] = got[d * hot_each : (d + 1) * hot_each]
        top = jnp.maximum(top, jnp.max(got, axis=0, keepdims=True))
    cold = cold_ref[...]
    place = place_ref[...]
    total = jnp.sum(jnp.exp(cold - top), axis=0, keepdims=True)
    hot_dot = jnp.zeros((1, q_rows), F32)
    for j in range(groups // 8):
        part = slice(j * 8 * hot_each, (j + 1) * 8 * hot_each)
        hot = hot_scr[part, :]
        total = total + jnp.sum(count_ref[part, :] * jnp.exp(hot - top), axis=0, keepdims=True)
        hot_dot = hot_dot + jnp.sum(target_ref[part, :] * hot, axis=0, keepdims=True)
    log_total = top + jnp.log(total)
    cold_target = misc_ref[0:COLD, :]
    entropy = misc_ref[COLD : COLD + 1, :]
    loss_ref[...] = entropy - hot_dot - jnp.sum(cold_target * cold, axis=0, keepdims=True) + log_total
    weight = (jnp.exp(cold - log_total) - cold_target).astype(BF16).astype(F32)
    weight_ref[...] = weight
    owner_iota = iota((groups, q_rows), 0)
    slot_iota = iota((LANES, q_rows), 0)
    owner_all = jnp.concatenate([one_hot(owner_iota == place[r : r + 1]) for r in range(COLD)], axis=1)
    slot_all = jnp.concatenate(
        [
            jnp.where(slot_iota == place[COLD + r : COLD + r + 1], weight[r : r + 1], 0.0).astype(BF16)
            for r in range(COLD)
        ],
        axis=1,
    )
    slot_scr[...] = lax.dot_general(owner_all, slot_all, ROWS_DOT, preferred_element_type=F32)
    for g in range(groups):
        part = slice(g * hot_each, (g + 1) * hot_each)
        coef = count_ref[part, :] * jnp.exp(hot_scr[part, :] - log_total) - target_ref[part, :]
        slot_row = jnp.broadcast_to(slot_scr[g : g + 1, :], (8, q_rows))
        pay_ref[g] = jnp.concatenate([coef, slot_row], axis=0).astype(BF16)


def query_kernel(scale, capacity, spot_ref, *refs):
    hot_refs = refs[:PIECES]
    pay_ref, found_ref, weight_ref, place_ref, out_ref = refs[PIECES:]
    q_rows = out_ref.shape[0]
    hot_each = hot_refs[0].shape[0] // Z_SIZE
    acc = jnp.zeros(out_ref.shape, F32)
    first = (((0,), (0,)), ((), ()))
    for piece, hot_ref in enumerate(hot_refs):
        owners = [owner_of(spot_ref, piece, d) for d in range(Z_SIZE)]
        coef = jnp.concatenate([pay_ref[o, 0:hot_each, :] for o in owners], axis=0)
        acc = acc + lax.dot_general(coef, hot_ref[...], first, preferred_element_type=F32)
    chunk = 256
    place = place_ref[...]
    weight = weight_ref[...]
    dests = [place[r : r + 1] * capacity + place[COLD + r : COLD + r + 1] for r in range(COLD)]
    for j in range(found_ref.shape[0] // chunk):
        ids = iota((chunk, q_rows), 0) + j * chunk
        made = jnp.zeros((chunk, q_rows), F32)
        for r in range(COLD):
            made = jnp.where(ids == dests[r], weight[r : r + 1], made)
        rows = found_ref[j * chunk : (j + 1) * chunk, :]
        acc = acc + lax.dot_general(made.astype(BF16), rows, first, preferred_element_type=F32)
    out_ref[...] = scale * acc


def slab_kernel(scale, capacity, reps, spot_ref, pay_ref, query_ref, row_ref, loc_ref, first_ref, second_ref, terms, hot_acc):
    step = pl.program_id(0)
    groups = pay_ref.shape[0]
    hot_each, feat = hot_acc.shape

    @pl.when(step == 0)
    def _():
        hot_acc[...] = jnp.zeros_like(hot_acc)

    acc = hot_acc[...]
    for n in range(0, groups, 2):
        left = jnp.concatenate([pay_ref[n, 0:hot_each, :], pay_ref[n + 1, 0:hot_each, :]], axis=1)
        right = jnp.concatenate([query_ref[n], query_ref[n + 1]], axis=0)
        acc = acc + jnp.dot(left, right, preferred_element_type=F32)
    hot_acc[...] = acc
    sent = jnp.concatenate([pay_ref[n, hot_each : hot_each + 8, :].astype(F32)[0:1] for n in range(groups)], axis=0)
    cols = scale * jnp.transpose(sent)
    col = jnp.concatenate(
        [jnp.broadcast_to(cols[0:capacity, n : n + 1], (capacity, LANES)) for n in range(groups)], axis=0
    )
    size = groups * capacity
    wide = jnp.concatenate([col] * (feat // LANES), axis=1)
    made = (wide * row_ref[...].astype(F32)).astype(BF16)
    terms[pl.ds(pl.multiple_of(step * size, size), size), :] = made

    @pl.when(step == pl.num_programs(0) - 1)
    def _():
        full = scale * hot_acc[...]
        high = full.astype(BF16)
        rest = full - high.astype(F32)
        mid = rest.astype(BF16)
        low = (rest - mid.astype(F32)).astype(BF16)
        base = terms.shape[0] - LANES
        terms[base:, :] = jnp.concatenate([high, mid, low, jnp.zeros_like(low)], axis=0)
        loc = loc_ref[...]
        rows = first_ref.shape[0]
        start = (spot_ref[1] + reps // 2) % reps * (2 * rows)
        at = one_hot(iota((2 * rows, loc.shape[1]), 0) + start == loc)
        got = jnp.dot(at, terms[...], preferred_element_type=F32).astype(BF16)
        first_ref[...] = got[:rows]
        second_ref[...] = got[rows:]


def near_kernel(reps, shifts, spot_ref, terms_ref, loc_ref, out_ref):
    rows = out_ref.shape[0] // len(shifts)
    loc = loc_ref[...]
    ids = iota((rows, loc.shape[1]), 0)
    starts = [(spot_ref[1] + d) % reps * rows for d in shifts]
    at = jnp.concatenate([one_hot(ids + start == loc) for start in starts], axis=0)
    out_ref[...] = jnp.dot(at, terms_ref[...], preferred_element_type=F32)


def stack_kernel(*refs):
    out_ref = refs[-1]
    size = refs[0].shape[0]
    for n, ref in enumerate(refs[:-1]):
        out_ref[n * size : (n + 1) * size, :] = ref[...]


def merge_kernel(near_ref, first_ref, second_ref, after_ref, before_ref):
    half = first_ref.shape[0]
    after_ref[0:half, :] = (near_ref[0:half, :] + first_ref[...].astype(F32)).astype(BF16)
    after_ref[half:, :] = near_ref[half : 2 * half, :].astype(BF16)
    before_ref[0:half, :] = near_ref[2 * half : 3 * half, :].astype(BF16)
    before_ref[half:, :] = (near_ref[3 * half :, :] + second_ref[...].astype(F32)).astype(BF16)


def gather_hot(rows):
    def member(x, z, core):
        return (x % X_SIZE * Z_SIZE + z % Z_SIZE) * CORES + core % CORES

    spots = [(x, z, c) for x in range(X_SIZE) for z in range(Z_SIZE) for c in range(CORES)]

    def shift(array, dx, dz, dc):
        return lax.ppermute(array, "corpus", [(member(x, z, c), member(x + dx, z + dz, c + dc)) for x, z, c in spots])

    pieces = [rows] + [shift(rows, 0, d, 0) for d in range(1, Z_SIZE)]
    rows = pl.pallas_call(
        stack_kernel,
        out_shape=jax.ShapeDtypeStruct((Z_SIZE * rows.shape[0], rows.shape[1]), BF16),
        in_specs=[VMEM_SPEC] * Z_SIZE,
        out_specs=VMEM_SPEC,
        name="stack",
    )(*pieces)
    pieces = [rows] + [shift(rows, d, 0, 0) for d in range(1, X_SIZE)]
    return pieces + [shift(p, 0, 0, 1) for p in pieces]


def shards(queries, teacher, slab, candidates, hot_ids, location):
    groups = lax.axis_size("corpus")
    reps = lax.axis_size("rep")
    corpus_idx = lax.axis_index("corpus")
    q_rows, feat = queries.shape
    per_owner = slab.shape[0]
    hot_total = hot_ids.shape[0]
    hot_each = hot_total // groups
    cand_count = candidates.shape[1]
    capacity = q_rows * COLD * 3 // (2 * groups)
    scale = 2.0 / math.sqrt(feat)
    rep_idx = lax.axis_index("rep")
    spot = jnp.stack([corpus_idx, rep_idx]).astype(jnp.int32)
    loc_table = location.reshape(-1, LANES)
    hot_table = hot_ids.reshape(-1, LANES)
    gathered = lax.all_gather(queries, "corpus", axis=0, tiled=False)
    cand_t = candidates.T
    req, place, sel = pl.pallas_call(
        functools.partial(request_kernel, per_owner, groups),
        out_shape=(
            jax.ShapeDtypeStruct((groups, LANES), jnp.int32),
            jax.ShapeDtypeStruct((2 * COLD, q_rows), jnp.int32),
            jax.ShapeDtypeStruct((cand_count, q_rows), jnp.int32),
        ),
        in_specs=[VMEM_SPEC] * 3,
        out_specs=(VMEM_SPEC,) * 3,
        scratch_shapes=[pltpu.VMEM((cand_count, q_rows), F32)],
        name="request",
    )(cand_t, hot_ids.reshape(1, hot_total), loc_table)
    own_rows = pl.pallas_call(
        functools.partial(prep_kernel, per_owner),
        out_shape=jax.ShapeDtypeStruct((hot_each, feat), BF16),
        in_specs=[SMEM_SPEC] + [VMEM_SPEC] * 3,
        out_specs=VMEM_SPEC,
        scratch_shapes=[pltpu.VMEM((LANES, LANES), F32)],
        name="prep",
    )(spot, hot_table, loc_table, slab)
    hot_rows = gather_hot(own_rows)
    asked = lax.all_to_all(req.reshape(groups, 1, LANES), "corpus", split_axis=0, concat_axis=0, tiled=True)
    asked = asked.reshape(groups, LANES)
    slots = groups * capacity
    block = 256
    wanted = pl.pallas_call(
        functools.partial(fetch_kernel, capacity),
        grid=(feat // block,),
        out_shape=jax.ShapeDtypeStruct((slots, feat), BF16),
        in_specs=[pl.BlockSpec((groups, LANES), lambda i: (0, 0)), pl.BlockSpec((per_owner, block), lambda i: (0, i))],
        out_specs=pl.BlockSpec((slots, block), lambda i: (0, i)),
        scratch_shapes=[pltpu.VMEM((slots, per_owner), BF16)],
        name="fetch",
    )(asked, slab)
    found = lax.all_to_all(wanted.reshape(groups, capacity, feat), "corpus", split_axis=0, concat_axis=0, tiled=True)
    found = found.reshape(groups * capacity, feat)
    count, target, misc = pl.pallas_call(
        count_kernel,
        out_shape=(
            jax.ShapeDtypeStruct((hot_total, q_rows), F32),
            jax.ShapeDtypeStruct((hot_total, q_rows), F32),
            jax.ShapeDtypeStruct((2 * COLD, q_rows), F32),
        ),
        in_specs=[VMEM_SPEC] * 4,
        out_specs=(VMEM_SPEC,) * 3,
        scratch_shapes=[pltpu.VMEM((cand_count, q_rows), F32)],
        cost_estimate=pl.CostEstimate(flops=80_000_000, bytes_accessed=3_000_000, transcendentals=10_000),
        name="count",
    )(cand_t, teacher.T, hot_table, sel)

    def whole(shape):
        return pl.BlockSpec(shape, lambda i: (0,) * len(shape))

    pay_rows = hot_each + 8
    cold = pl.pallas_call(
        functools.partial(cold_kernel, scale, capacity),
        out_shape=jax.ShapeDtypeStruct((COLD, q_rows), F32),
        in_specs=[VMEM_SPEC] * 3,
        out_specs=VMEM_SPEC,
        name="cold",
    )(queries, found, place)
    loss, pay, weight = pl.pallas_call(
        functools.partial(score_kernel, scale),
        out_shape=(
            jax.ShapeDtypeStruct((1, q_rows), F32),
            jax.ShapeDtypeStruct((groups, pay_rows, q_rows), BF16),
            jax.ShapeDtypeStruct((COLD, q_rows), F32),
        ),
        in_specs=[SMEM_SPEC] + [VMEM_SPEC] * (PIECES + 6),
        out_specs=(VMEM_SPEC,) * 3,
        scratch_shapes=[pltpu.VMEM((hot_total, q_rows), F32), pltpu.VMEM((groups, q_rows), F32)],
        name="score",
    )(spot, queries, *hot_rows, cold, count, target, place, misc)
    got = lax.all_to_all(pay, "corpus", split_axis=0, concat_axis=0, tiled=True)
    query_grad = pl.pallas_call(
        functools.partial(query_kernel, scale, capacity),
        out_shape=jax.ShapeDtypeStruct((q_rows, feat), F32),
        in_specs=[SMEM_SPEC] + [VMEM_SPEC] * (PIECES + 4),
        out_specs=VMEM_SPEC,
        cost_estimate=pl.CostEstimate(flops=700_000_000, bytes_accessed=7_000_000, transcendentals=0),
        name="query_grad",
    )(spot, *hot_rows, pay, found, weight, place)
    padded = asked[:, :capacity]
    source = jnp.arange(groups, dtype=jnp.int32)[:, None] * q_rows
    query_rows = gathered.reshape(-1, feat)[(source + jnp.maximum(padded, 0) // per_owner).reshape(-1)]
    local = jnp.where(padded >= 0, padded & (per_owner - 1), -1).reshape(1, -1)
    mine = lax.dynamic_slice_in_dim(hot_ids, corpus_idx * hot_each, hot_each)
    own_hot = location[mine] - corpus_idx * per_owner
    tail = jnp.full((LANES - 3 * hot_each,), -1, jnp.int32)
    local = jnp.concatenate([local, jnp.concatenate([own_hot, own_hot, own_hot, tail])[None, :]], axis=1)
    step = 8
    rows = per_owner // reps
    half = jax.ShapeDtypeStruct((rows // 2, feat), BF16)
    depth = slots + LANES
    first, second, terms = pl.pallas_call(
        functools.partial(slab_kernel, scale, capacity, reps),
        grid=(groups // step,),
        out_shape=(half, half, jax.ShapeDtypeStruct((depth, feat), BF16)),
        in_specs=[
            SMEM_SPEC,
            pl.BlockSpec((step, pay_rows, q_rows), lambda i: (i, 0, 0)),
            pl.BlockSpec((step, q_rows, feat), lambda i: (i, 0, 0)),
            pl.BlockSpec((step * capacity, feat), lambda i: (i, 0)),
            whole((1, depth)),
        ],
        out_specs=(whole(half.shape), whole(half.shape), whole((depth, feat))),
        scratch_shapes=[pltpu.VMEM((hot_each, feat), F32)],
        name="slab_grad",
    )(spot, got, gathered, query_rows, local)
    ahead = [(r, (r + 1) % reps) for r in range(reps)]
    behind = [(r, (r - 1) % reps) for r in range(reps)]
    first = lax.ppermute(first, "rep", ahead)
    second = lax.ppermute(second, "rep", behind)

    def land(shifts):
        return pl.pallas_call(
            functools.partial(near_kernel, reps, shifts),
            out_shape=jax.ShapeDtypeStruct((len(shifts) * rows, feat), F32),
            in_specs=[SMEM_SPEC, VMEM_SPEC, VMEM_SPEC],
            out_specs=VMEM_SPEC,
            cost_estimate=pl.CostEstimate(flops=2_000_000_000, bytes_accessed=6_000_000, transcendentals=0),
        )(spot, terms, local)

    near = land((1, reps - 1))
    after, before = pl.pallas_call(
        merge_kernel,
        out_shape=(jax.ShapeDtypeStruct((rows, feat), BF16),) * 2,
        in_specs=[VMEM_SPEC] * 3,
        out_specs=(VMEM_SPEC,) * 2,
        name="merge",
    )(near, first, second)
    after = lax.ppermute(after, "rep", ahead)
    before = lax.ppermute(before, "rep", behind)
    slab_grad = land((0,)) + after.astype(F32) + before.astype(F32)
    return (loss.reshape(q_rows), query_grad, slab_grad)


def solution(mesh):
    return jax.shard_map(
        shards,
        mesh=mesh,
        in_specs=(
            P(("corpus", "rep"), None),
            P(("corpus", "rep"), None),
            P("corpus", None),
            P(("corpus", "rep"), None),
            P(),
            P(),
        ),
        out_specs=(P(("corpus", "rep")), P(("corpus", "rep"), None), P(("corpus", "rep"), None)),
        check_vma=False,
    )
```

```python
import functools
import math

import jax
import jax.numpy as jnp
from jax import lax
from jax.experimental import pallas as pl
from jax.experimental.pallas import tpu as pltpu
from jax.sharding import PartitionSpec as P


COLD = 8
LANES = 128
X_SIZE, Z_SIZE, CORES = 4, 8, 2
PIECES = 1 + (X_SIZE - 1) * CORES
RADIX = 256
F32 = jnp.float32
BF16 = jnp.bfloat16
VMEM_SPEC = pl.BlockSpec(memory_space=pltpu.VMEM)
SMEM_SPEC = pl.BlockSpec(memory_space=pltpu.SMEM)
ROWS_DOT = (((1,), (1,)), ((), ()))


def iota(shape, axis):
    return lax.broadcasted_iota(jnp.int32, shape, axis)


def one_hot(mask, dtype=BF16):
    return jnp.where(mask, 1.0, 0.0).astype(dtype)


def pick_rows(mask, values):
    return jnp.sum(jnp.where(mask, values, jnp.zeros_like(values)), axis=0, keepdims=True)


def request_kernel(per_owner, groups, cand_t, hot_ref, loc_ref, req_ref, place_ref, sel_ref, hit_t):
    cand_count, q_rows = cand_t.shape
    hot_total = hot_ref.shape[1]
    high_rows = loc_ref.shape[0] // 2
    hot = hot_ref[...]
    low_hot = one_hot(iota((RADIX, hot_total), 0) == (hot & (RADIX - 1)))
    high_hot = one_hot(iota((high_rows, hot_total), 0) == (hot // RADIX))
    marks = lax.dot_general(low_hot, high_hot, ROWS_DOT, preferred_element_type=F32).astype(BF16)
    low_iota = iota((RADIX, q_rows), 0)
    high_iota = iota((high_rows, q_rows), 0)

    def lookup(tables, ids):
        hots = jnp.concatenate([one_hot(high_iota == (i // RADIX)) for i in ids], axis=1)
        found = [jnp.dot(t, hots, preferred_element_type=F32) for t in tables]
        masks = [low_iota == (i & (RADIX - 1)) for i in ids]
        return [
            [pick_rows(m, f[:, n * q_rows : (n + 1) * q_rows]) for n, m in enumerate(masks)]
            for f in found
        ]

    def check(j, carry):
        start = pl.multiple_of(j * 8, 8)
        rows = cand_t[pl.ds(start, 8), :]
        hits = lookup([marks], [rows[n : n + 1, :] for n in range(8)])[0]
        hit_t[pl.ds(start, 8), :] = jnp.concatenate(hits, axis=0)
        return carry

    lax.fori_loop(0, cand_count // 8, check, 0)
    cold = hit_t[...] < 0.5
    earlier = one_hot(iota((cand_count, cand_count), 0) > iota((cand_count, cand_count), 1))
    order = jnp.dot(earlier, one_hot(cold), preferred_element_type=F32).astype(jnp.int32)
    sel = jnp.where(cold, order, -1)
    sel_ref[...] = sel
    cand = cand_t[...]
    ids = [pick_rows(sel == r, cand) for r in range(COLD)]
    loc = jnp.concatenate([loc_ref[pl.ds(0, high_rows, stride=2), :], loc_ref[pl.ds(1, high_rows, stride=2), :]], axis=1)
    high_table = jnp.transpose((loc // RADIX).astype(F32)).astype(BF16)
    low_table = jnp.transpose((loc & (RADIX - 1)).astype(F32)).astype(BF16)
    high_part, low_part = lookup([high_table, low_table], ids)
    before = one_hot(iota((q_rows, q_rows), 0) < iota((q_rows, q_rows), 1))
    owner_iota = iota((groups, q_rows), 0)
    slot_iota = iota((LANES, q_rows), 0)
    query = iota((1, q_rows), 1).astype(F32)
    base = jnp.zeros((groups, 1), F32)
    owners, ranks, owner_hots, low_vals, high_vals, query_vals = [], [], [], [], [], []
    for r in range(COLD):
        row = high_part[r].astype(jnp.int32) * RADIX + low_part[r].astype(jnp.int32)
        owner = row // per_owner
        local = row & (per_owner - 1)
        owner_hot = one_hot(owner_iota == owner, F32)
        count = jnp.dot(owner_hot.astype(BF16), before, preferred_element_type=F32) + base
        rank = jnp.sum(owner_hot * count, axis=0, keepdims=True).astype(jnp.int32)
        base = base + jnp.sum(owner_hot, axis=1, keepdims=True)
        at_slot = slot_iota == rank
        owners.append(owner)
        ranks.append(rank)
        owner_hots.append(owner_hot.astype(BF16))
        low_vals.append(jnp.where(at_slot, (local & (RADIX - 1)).astype(F32), 0.0).astype(BF16))
        high_vals.append(jnp.where(at_slot, (local // RADIX + RADIX // 2).astype(F32), 0.0).astype(BF16))
        query_vals.append(jnp.where(at_slot, query, 0.0).astype(BF16))
    owner_all = jnp.concatenate(owner_hots, axis=1)

    def spread(vals):
        got = lax.dot_general(owner_all, jnp.concatenate(vals, axis=1), ROWS_DOT, preferred_element_type=F32)
        return got.astype(jnp.int32)

    low_got, high_got, query_got = spread(low_vals), spread(high_vals), spread(query_vals)
    packed = low_got + RADIX * (high_got - RADIX // 2) + per_owner * query_got
    req_ref[...] = jnp.where(high_got > 0, packed, -1)
    place_ref[...] = jnp.concatenate(owners + ranks, axis=0)


def prep_kernel(per_owner, spot_ref, hot_ref, loc_ref, slab_ref, out_ref, col_scr):
    hot_each = out_ref.shape[0] * 2 // 3
    high_rows = loc_ref.shape[0]
    ids = hot_ref[pl.ds(spot_ref[0] * hot_each // LANES, 1), :]
    high_hot = one_hot(iota((high_rows, LANES), 0) == (ids // LANES))
    low_mask = iota((LANES, LANES), 0) == (ids & (LANES - 1))
    loc = loc_ref[...]
    high = jnp.transpose((loc // RADIX).astype(F32)).astype(BF16)
    low = jnp.transpose((loc & (RADIX - 1)).astype(F32)).astype(BF16)
    high = pick_rows(low_mask, jnp.dot(high, high_hot, preferred_element_type=F32))
    low = pick_rows(low_mask, jnp.dot(low, high_hot, preferred_element_type=F32))
    local = high * RADIX + low - (spot_ref[0] * per_owner).astype(F32)
    col_scr[...] = jnp.transpose(jnp.broadcast_to(local, (LANES, LANES)))
    start = pl.multiple_of(spot_ref[0] * hot_each % LANES, hot_each)
    cols = jnp.concatenate([col_scr[pl.ds(start, hot_each), :]] * (per_owner // LANES), axis=1)
    picks = one_hot(iota((hot_each, per_owner), 1).astype(F32) == cols)
    out_ref[0:hot_each, :] = jnp.dot(picks, slab_ref[...], preferred_element_type=F32).astype(BF16)
    out_ref[hot_each:, :] = jnp.zeros((hot_each // 2, out_ref.shape[1]), BF16)


def hot_pieces(spot_ref, hot_refs):
    base = hot_refs[0]
    size = base.shape[0] // CORES
    x, core = spot_ref[0] // (Z_SIZE * CORES), spot_ref[0] & (CORES - 1)

    def owners(dx, c):
        return [(((x - dx) & (X_SIZE - 1)) * Z_SIZE + z) * CORES + c for z in range(Z_SIZE)]

    for c in range(CORES):
        yield base[c * size : (c + 1) * size, :], owners(0, c)
    for n, ref in enumerate(hot_refs[1:]):
        yield ref[...], owners(n % (X_SIZE - 1) + 1, core ^ (n // (X_SIZE - 1)))


def fetch_kernel(capacity, asked_ref, slab_ref, out_ref, picks):
    groups = asked_ref.shape[0]
    per_owner = slab_ref.shape[0]

    @pl.when(pl.program_id(0) == 0)
    def _():
        asked = jnp.maximum(asked_ref[...], 0)
        cols = jnp.transpose((asked & (per_owner - 1)).astype(F32))
        lane = iota((capacity, per_owner), 1).astype(F32)
        for n in range(0, groups, 2):
            pair = [
                one_hot(lane == jnp.broadcast_to(cols[0:capacity, m : m + 1], (capacity, per_owner)), F32)
                for m in (n, n + 1)
            ]
            picks[n * capacity : (n + 2) * capacity, :] = jnp.concatenate(pair, axis=0).astype(BF16)

    out_ref[...] = jnp.dot(picks[...], slab_ref[...], preferred_element_type=F32).astype(BF16)


def cold_kernel(scale, capacity, q_ref, found_ref, place_ref, cold_ref):
    q_rows = q_ref.shape[0]
    q = q_ref[...]
    place = place_ref[...]
    dests = [place[r : r + 1] * capacity + place[COLD + r : COLD + r + 1] for r in range(COLD)]
    chunk = 256

    def score(j, sums):
        start = pl.multiple_of(j * chunk, chunk)
        got = scale * lax.dot_general(found_ref[pl.ds(start, chunk), :], q, ROWS_DOT, preferred_element_type=F32)
        ids = iota((chunk, q_rows), 0) + start
        return [
            total + jnp.sum(jnp.where(ids == dest, got, 0.0).reshape(-1, 8, q_rows), axis=0)
            for total, dest in zip(sums, dests)
        ]

    sums = [jnp.zeros((8, q_rows), F32) for _ in range(COLD)]
    sums = lax.fori_loop(0, found_ref.shape[0] // chunk, score, sums)
    cold_ref[...] = jnp.concatenate([jnp.sum(total, axis=0, keepdims=True) for total in sums], axis=0)


def count_kernel(cand_t, teacher_ref, hot_ref, sel_ref, count_ref, target_ref, misc_ref, soft_t):
    cand_count, q_rows = cand_t.shape
    teacher = teacher_ref[...]
    shifted = teacher - jnp.max(teacher, axis=0, keepdims=True)
    log_target = shifted - jnp.log(jnp.sum(jnp.exp(shifted), axis=0, keepdims=True))
    target = jnp.exp(log_target)
    soft_t[...] = target
    sel = sel_ref[...]
    entropy = jnp.sum(target * log_target, axis=0, keepdims=True)
    rows = [pick_rows(sel == r, target) for r in range(COLD)]
    misc_ref[...] = jnp.concatenate(rows + [jnp.broadcast_to(entropy, (8, q_rows))], axis=0)
    hot_cols = jnp.transpose(hot_ref[...])
    for a in range(hot_ref.shape[0]):
        column = jnp.broadcast_to(hot_cols[:, a : a + 1], (LANES, q_rows))

        def add(k, carry):
            count, total = carry
            match = column == cand_t[pl.ds(k, 1), :]
            count = count + jnp.where(match, 1.0, 0.0)
            total = total + jnp.where(match, soft_t[pl.ds(k, 1), :], 0.0)
            return count, total

        start = (jnp.ones((LANES, q_rows), F32), jnp.zeros((LANES, q_rows), F32))
        count, total = lax.fori_loop(0, cand_count, add, start, unroll=4)
        count_ref[a * LANES : (a + 1) * LANES, :] = count
        target_ref[a * LANES : (a + 1) * LANES, :] = total


def score_kernel(scale, spot_ref, q_ref, *refs):
    score_body(scale, spot_ref, q_ref, refs[:PIECES], *refs[PIECES:])


def score_body(scale, spot_ref, q_ref, hot_refs, cold_ref, count_ref, target_ref, place_ref, misc_ref, loss_ref, pay_ref, weight_ref, hot_scr, slot_scr):
    groups = pay_ref.shape[0]
    q_rows = q_ref.shape[0]
    hot_each = hot_scr.shape[0] // groups
    q = q_ref[...]
    top = jnp.max(cold_ref[...], axis=0, keepdims=True)
    for rows, owners in hot_pieces(spot_ref, hot_refs):
        got = scale * lax.dot_general(rows, q, ROWS_DOT, preferred_element_type=F32)
        for d, owner in enumerate(owners):
            start = pl.multiple_of(owner * hot_each, hot_each)
            hot_scr[pl.ds(start, hot_each), :] = got[d * hot_each : (d + 1) * hot_each]
        top = jnp.maximum(top, jnp.max(got, axis=0, keepdims=True))
    cold = cold_ref[...]
    place = place_ref[...]
    total = jnp.sum(jnp.exp(cold - top), axis=0, keepdims=True)
    hot_dot = jnp.zeros((1, q_rows), F32)
    for j in range(groups // 8):
        part = slice(j * 8 * hot_each, (j + 1) * 8 * hot_each)
        hot = hot_scr[part, :]
        total = total + jnp.sum(count_ref[part, :] * jnp.exp(hot - top), axis=0, keepdims=True)
        hot_dot = hot_dot + jnp.sum(target_ref[part, :] * hot, axis=0, keepdims=True)
    log_total = top + jnp.log(total)
    cold_target = misc_ref[0:COLD, :]
    entropy = misc_ref[COLD : COLD + 1, :]
    loss_ref[...] = entropy - hot_dot - jnp.sum(cold_target * cold, axis=0, keepdims=True) + log_total
    weight = (jnp.exp(cold - log_total) - cold_target).astype(BF16).astype(F32)
    weight_ref[...] = weight
    owner_iota = iota((groups, q_rows), 0)
    slot_iota = iota((LANES, q_rows), 0)
    owner_all = jnp.concatenate([one_hot(owner_iota == place[r : r + 1]) for r in range(COLD)], axis=1)
    slot_all = jnp.concatenate(
        [
            jnp.where(slot_iota == place[COLD + r : COLD + r + 1], weight[r : r + 1], 0.0).astype(BF16)
            for r in range(COLD)
        ],
        axis=1,
    )
    slot_scr[...] = lax.dot_general(owner_all, slot_all, ROWS_DOT, preferred_element_type=F32)
    for g in range(groups):
        part = slice(g * hot_each, (g + 1) * hot_each)
        coef = count_ref[part, :] * jnp.exp(hot_scr[part, :] - log_total) - target_ref[part, :]
        slot_row = jnp.broadcast_to(slot_scr[g : g + 1, :], (8, q_rows))
        pay_ref[g] = jnp.concatenate([coef, slot_row], axis=0).astype(BF16)


def query_kernel(scale, capacity, spot_ref, *refs):
    hot_refs = refs[:PIECES]
    pay_ref, found_ref, weight_ref, place_ref, out_ref = refs[PIECES:]
    q_rows = out_ref.shape[0]
    hot_each = hot_refs[0].shape[0] // (Z_SIZE * CORES)
    acc = jnp.zeros(out_ref.shape, F32)
    first = (((0,), (0,)), ((), ()))
    for rows, owners in hot_pieces(spot_ref, hot_refs):
        coef = jnp.concatenate([pay_ref[o, 0:hot_each, :] for o in owners], axis=0)
        acc = acc + lax.dot_general(coef, rows, first, preferred_element_type=F32)
    chunk = 256
    place = place_ref[...]
    weight = weight_ref[...]
    dests = [place[r : r + 1] * capacity + place[COLD + r : COLD + r + 1] for r in range(COLD)]
    for j in range(found_ref.shape[0] // chunk):
        ids = iota((chunk, q_rows), 0) + j * chunk
        made = jnp.zeros((chunk, q_rows), F32)
        for r in range(COLD):
            made = jnp.where(ids == dests[r], weight[r : r + 1], made)
        rows = found_ref[j * chunk : (j + 1) * chunk, :]
        acc = acc + lax.dot_general(made.astype(BF16), rows, first, preferred_element_type=F32)
    out_ref[...] = scale * acc


def slab_kernel(scale, capacity, reps, spot_ref, pay_ref, query_ref, row_ref, loc_ref, first_ref, second_ref, terms, hot_acc):
    step = pl.program_id(0)
    groups = pay_ref.shape[0]
    hot_each, feat = hot_acc.shape

    @pl.when(step == 0)
    def _():
        hot_acc[...] = jnp.zeros_like(hot_acc)

    acc = hot_acc[...]
    for n in range(0, groups, 2):
        left = jnp.concatenate([pay_ref[n, 0:hot_each, :], pay_ref[n + 1, 0:hot_each, :]], axis=1)
        right = jnp.concatenate([query_ref[n], query_ref[n + 1]], axis=0)
        acc = acc + jnp.dot(left, right, preferred_element_type=F32)
    hot_acc[...] = acc
    sent = jnp.concatenate([pay_ref[n, hot_each : hot_each + 8, :].astype(F32)[0:1] for n in range(groups)], axis=0)
    cols = scale * jnp.transpose(sent)
    col = jnp.concatenate(
        [jnp.broadcast_to(cols[0:capacity, n : n + 1], (capacity, LANES)) for n in range(groups)], axis=0
    )
    size = groups * capacity
    wide = jnp.concatenate([col] * (feat // LANES), axis=1)
    made = (wide * row_ref[...].astype(F32)).astype(BF16)
    terms[pl.ds(pl.multiple_of(step * size, size), size), :] = made

    @pl.when(step == pl.num_programs(0) - 1)
    def _():
        full = scale * hot_acc[...]
        high = full.astype(BF16)
        rest = full - high.astype(F32)
        mid = rest.astype(BF16)
        low = (rest - mid.astype(F32)).astype(BF16)
        base = terms.shape[0] - LANES
        terms[base:, :] = jnp.concatenate([high, mid, low, jnp.zeros_like(low)], axis=0)
        loc = loc_ref[...]
        rows = first_ref.shape[0]
        start = (spot_ref[1] + reps // 2) % reps * (2 * rows)
        at = one_hot(iota((2 * rows, loc.shape[1]), 0) + start == loc)
        got = jnp.dot(at, terms[...], preferred_element_type=F32).astype(BF16)
        first_ref[...] = got[:rows]
        second_ref[...] = got[rows:]


def near_kernel(reps, shifts, spot_ref, terms_ref, loc_ref, out_ref):
    rows = out_ref.shape[0] // len(shifts)
    loc = loc_ref[...]
    ids = iota((rows, loc.shape[1]), 0)
    starts = [(spot_ref[1] + d) % reps * rows for d in shifts]
    at = jnp.concatenate([one_hot(ids + start == loc) for start in starts], axis=0)
    out_ref[...] = jnp.dot(at, terms_ref[...], preferred_element_type=F32)


def merge_kernel(near_ref, first_ref, second_ref, after_ref, before_ref):
    half = first_ref.shape[0]
    after_ref[0:half, :] = (near_ref[0:half, :] + first_ref[...].astype(F32)).astype(BF16)
    after_ref[half:, :] = near_ref[half : 2 * half, :].astype(BF16)
    before_ref[0:half, :] = near_ref[2 * half : 3 * half, :].astype(BF16)
    before_ref[half:, :] = (near_ref[3 * half :, :] + second_ref[...].astype(F32)).astype(BF16)


def gather_hot(rows):
    def member(x, z, core):
        return (x % X_SIZE * Z_SIZE + z % Z_SIZE) * CORES + core % CORES

    spots = [(x, z, c) for x in range(X_SIZE) for z in range(Z_SIZE) for c in range(CORES)]

    def shift(array, dx, dz, dc):
        return lax.ppermute(array, "corpus", [(member(x, z, c), member(x + dx, z + dz, c + dc)) for x, z, c in spots])

    groups = [[member(x, z, c) for c in range(CORES) for z in range(Z_SIZE)] for x in range(X_SIZE)]
    base = lax.all_gather(rows, "corpus", axis=0, tiled=False, axis_index_groups=groups)
    hot_each, feat = rows.shape[0] * 2 // 3, rows.shape[1]
    mine = lax.dynamic_slice_in_dim(base, lax.axis_index("corpus") % CORES * Z_SIZE, Z_SIZE)
    mine = mine[:, :hot_each].reshape(-1, feat)
    base = base[:, :hot_each].reshape(-1, feat)
    moved = [shift(mine, d, 0, 0) for d in range(1, X_SIZE)]
    return [base] + moved + [shift(m, 0, 0, 1) for m in moved]


def shards(queries, teacher, slab, candidates, hot_ids, location):
    groups = lax.axis_size("corpus")
    reps = lax.axis_size("rep")
    corpus_idx = lax.axis_index("corpus")
    q_rows, feat = queries.shape
    per_owner = slab.shape[0]
    hot_total = hot_ids.shape[0]
    hot_each = hot_total // groups
    cand_count = candidates.shape[1]
    capacity = q_rows * COLD * 3 // (2 * groups)
    scale = 2.0 / math.sqrt(feat)
    rep_idx = lax.axis_index("rep")
    spot = jnp.stack([corpus_idx, rep_idx]).astype(jnp.int32)
    loc_table = location.reshape(-1, LANES)
    hot_table = hot_ids.reshape(-1, LANES)
    own_rows = pl.pallas_call(
        functools.partial(prep_kernel, per_owner),
        out_shape=jax.ShapeDtypeStruct((hot_each * 3 // 2, feat), BF16),
        in_specs=[SMEM_SPEC] + [VMEM_SPEC] * 3,
        out_specs=VMEM_SPEC,
        scratch_shapes=[pltpu.VMEM((LANES, LANES), F32)],
        name="prep",
    )(spot, hot_table, loc_table, slab)
    cand_t, own_rows = lax.optimization_barrier((candidates.T, own_rows))
    hot_rows = gather_hot(own_rows)
    gathered = lax.all_gather(queries, "corpus", axis=0, tiled=False)
    req, place, sel = pl.pallas_call(
        functools.partial(request_kernel, per_owner, groups),
        out_shape=(
            jax.ShapeDtypeStruct((groups, LANES), jnp.int32),
            jax.ShapeDtypeStruct((2 * COLD, q_rows), jnp.int32),
            jax.ShapeDtypeStruct((cand_count, q_rows), jnp.int32),
        ),
        in_specs=[VMEM_SPEC] * 3,
        out_specs=(VMEM_SPEC,) * 3,
        scratch_shapes=[pltpu.VMEM((cand_count, q_rows), F32)],
        name="request",
    )(cand_t, hot_ids.reshape(1, hot_total), loc_table)
    asked = lax.all_to_all(req.reshape(groups, 1, LANES), "corpus", split_axis=0, concat_axis=0, tiled=True)
    asked = asked.reshape(groups, LANES)
    slots = groups * capacity
    block = 256
    wanted = pl.pallas_call(
        functools.partial(fetch_kernel, capacity),
        grid=(feat // block,),
        out_shape=jax.ShapeDtypeStruct((slots, feat), BF16),
        in_specs=[pl.BlockSpec((groups, LANES), lambda i: (0, 0)), pl.BlockSpec((per_owner, block), lambda i: (0, i))],
        out_specs=pl.BlockSpec((slots, block), lambda i: (0, i)),
        scratch_shapes=[pltpu.VMEM((slots, per_owner), BF16)],
        name="fetch",
    )(asked, slab)
    found = lax.all_to_all(wanted.reshape(groups, capacity, feat), "corpus", split_axis=0, concat_axis=0, tiled=True)
    found = found.reshape(groups * capacity, feat)
    count, target, misc = pl.pallas_call(
        count_kernel,
        out_shape=(
            jax.ShapeDtypeStruct((hot_total, q_rows), F32),
            jax.ShapeDtypeStruct((hot_total, q_rows), F32),
            jax.ShapeDtypeStruct((2 * COLD, q_rows), F32),
        ),
        in_specs=[VMEM_SPEC] * 4,
        out_specs=(VMEM_SPEC,) * 3,
        scratch_shapes=[pltpu.VMEM((cand_count, q_rows), F32)],
        cost_estimate=pl.CostEstimate(flops=80_000_000, bytes_accessed=3_000_000, transcendentals=10_000),
        name="count",
    )(cand_t, teacher.T, hot_table, sel)

    def whole(shape):
        return pl.BlockSpec(shape, lambda i: (0,) * len(shape))

    pay_rows = hot_each + 8
    cold = pl.pallas_call(
        functools.partial(cold_kernel, scale, capacity),
        out_shape=jax.ShapeDtypeStruct((COLD, q_rows), F32),
        in_specs=[VMEM_SPEC] * 3,
        out_specs=VMEM_SPEC,
        name="cold",
    )(queries, found, place)
    loss, pay, weight = pl.pallas_call(
        functools.partial(score_kernel, scale),
        out_shape=(
            jax.ShapeDtypeStruct((1, q_rows), F32),
            jax.ShapeDtypeStruct((groups, pay_rows, q_rows), BF16),
            jax.ShapeDtypeStruct((COLD, q_rows), F32),
        ),
        in_specs=[SMEM_SPEC] + [VMEM_SPEC] * (PIECES + 6),
        out_specs=(VMEM_SPEC,) * 3,
        scratch_shapes=[pltpu.VMEM((hot_total, q_rows), F32), pltpu.VMEM((groups, q_rows), F32)],
        name="score",
    )(spot, queries, *hot_rows, cold, count, target, place, misc)
    got = lax.all_to_all(pay, "corpus", split_axis=0, concat_axis=0, tiled=True)
    query_grad = pl.pallas_call(
        functools.partial(query_kernel, scale, capacity),
        out_shape=jax.ShapeDtypeStruct((q_rows, feat), F32),
        in_specs=[SMEM_SPEC] + [VMEM_SPEC] * (PIECES + 4),
        out_specs=VMEM_SPEC,
        cost_estimate=pl.CostEstimate(flops=700_000_000, bytes_accessed=7_000_000, transcendentals=0),
        name="query_grad",
    )(spot, *hot_rows, pay, found, weight, place)
    padded = asked[:, :capacity]
    source = jnp.arange(groups, dtype=jnp.int32)[:, None] * q_rows
    query_rows = gathered.reshape(-1, feat)[(source + jnp.maximum(padded, 0) // per_owner).reshape(-1)]
    local = jnp.where(padded >= 0, padded & (per_owner - 1), -1).reshape(1, -1)
    mine = lax.dynamic_slice_in_dim(hot_ids, corpus_idx * hot_each, hot_each)
    own_hot = location[mine] - corpus_idx * per_owner
    tail = jnp.full((LANES - 3 * hot_each,), -1, jnp.int32)
    local = jnp.concatenate([local, jnp.concatenate([own_hot, own_hot, own_hot, tail])[None, :]], axis=1)
    step = 8
    rows = per_owner // reps
    half = jax.ShapeDtypeStruct((rows // 2, feat), BF16)
    depth = slots + LANES
    first, second, terms = pl.pallas_call(
        functools.partial(slab_kernel, scale, capacity, reps),
        grid=(groups // step,),
        out_shape=(half, half, jax.ShapeDtypeStruct((depth, feat), BF16)),
        in_specs=[
            SMEM_SPEC,
            pl.BlockSpec((step, pay_rows, q_rows), lambda i: (i, 0, 0)),
            pl.BlockSpec((step, q_rows, feat), lambda i: (i, 0, 0)),
            pl.BlockSpec((step * capacity, feat), lambda i: (i, 0)),
            whole((1, depth)),
        ],
        out_specs=(whole(half.shape), whole(half.shape), whole((depth, feat))),
        scratch_shapes=[pltpu.VMEM((hot_each, feat), F32)],
        name="slab_grad",
    )(spot, got, gathered, query_rows, local)
    ahead = [(r, (r + 1) % reps) for r in range(reps)]
    behind = [(r, (r - 1) % reps) for r in range(reps)]
    first = lax.ppermute(first, "rep", ahead)
    second = lax.ppermute(second, "rep", behind)

    def land(shifts):
        return pl.pallas_call(
            functools.partial(near_kernel, reps, shifts),
            out_shape=jax.ShapeDtypeStruct((len(shifts) * rows, feat), F32),
            in_specs=[SMEM_SPEC, VMEM_SPEC, VMEM_SPEC],
            out_specs=VMEM_SPEC,
            cost_estimate=pl.CostEstimate(flops=2_000_000_000, bytes_accessed=6_000_000, transcendentals=0),
        )(spot, terms, local)

    near = land((1, reps - 1))
    after, before = pl.pallas_call(
        merge_kernel,
        out_shape=(jax.ShapeDtypeStruct((rows, feat), BF16),) * 2,
        in_specs=[VMEM_SPEC] * 3,
        out_specs=(VMEM_SPEC,) * 2,
        name="merge",
    )(near, first, second)
    after = lax.ppermute(after, "rep", ahead)
    before = lax.ppermute(before, "rep", behind)
    slab_grad = land((0,)) + after.astype(F32) + before.astype(F32)
    return (loss.reshape(q_rows), query_grad, slab_grad)


def solution(mesh):
    return jax.shard_map(
        shards,
        mesh=mesh,
        in_specs=(
            P(("corpus", "rep"), None),
            P(("corpus", "rep"), None),
            P("corpus", None),
            P(("corpus", "rep"), None),
            P(),
            P(),
        ),
        out_specs=(P(("corpus", "rep")), P(("corpus", "rep"), None), P(("corpus", "rep"), None)),
        check_vma=False,
    )
```

```python
import functools
import math

import jax
import jax.numpy as jnp
from jax import lax
from jax.experimental import pallas as pl
from jax.experimental.pallas import tpu as pltpu
from jax.sharding import PartitionSpec as P


COLD = 8
LANES = 128
RADIX = 256
F32 = jnp.float32
BF16 = jnp.bfloat16
VMEM_SPEC = pl.BlockSpec(memory_space=pltpu.VMEM)
SMEM_SPEC = pl.BlockSpec(memory_space=pltpu.SMEM)
ROWS_DOT = (((1,), (1,)), ((), ()))


def iota(shape, axis):
    return lax.broadcasted_iota(jnp.int32, shape, axis)


def one_hot(mask, dtype=BF16):
    return jnp.where(mask, 1.0, 0.0).astype(dtype)


def pick_rows(mask, values):
    return jnp.sum(jnp.where(mask, values, jnp.zeros_like(values)), axis=0, keepdims=True)


def request_kernel(per_owner, groups, cand_t, hot_ref, loc_ref, req_ref, place_ref, sel_ref, hit_t):
    cand_count, q_rows = cand_t.shape
    hot_total = hot_ref.shape[1]
    high_rows = loc_ref.shape[0] // 2
    hot = hot_ref[...]
    low_hot = one_hot(iota((RADIX, hot_total), 0) == (hot & (RADIX - 1)))
    high_hot = one_hot(iota((high_rows, hot_total), 0) == (hot // RADIX))
    marks = lax.dot_general(low_hot, high_hot, ROWS_DOT, preferred_element_type=F32).astype(BF16)
    low_iota = iota((RADIX, q_rows), 0)
    high_iota = iota((high_rows, q_rows), 0)

    def lookup(tables, ids):
        hots = jnp.concatenate([one_hot(high_iota == (i // RADIX)) for i in ids], axis=1)
        found = [jnp.dot(t, hots, preferred_element_type=F32) for t in tables]
        masks = [low_iota == (i & (RADIX - 1)) for i in ids]
        return [
            [pick_rows(m, f[:, n * q_rows : (n + 1) * q_rows]) for n, m in enumerate(masks)]
            for f in found
        ]

    def check(j, carry):
        start = pl.multiple_of(j * 8, 8)
        rows = cand_t[pl.ds(start, 8), :]
        hits = lookup([marks], [rows[n : n + 1, :] for n in range(8)])[0]
        hit_t[pl.ds(start, 8), :] = jnp.concatenate(hits, axis=0)
        return carry

    lax.fori_loop(0, cand_count // 8, check, 0)
    cold = hit_t[...] < 0.5
    earlier = one_hot(iota((cand_count, cand_count), 0) > iota((cand_count, cand_count), 1))
    order = jnp.dot(earlier, one_hot(cold), preferred_element_type=F32).astype(jnp.int32)
    sel = jnp.where(cold, order, -1)
    sel_ref[...] = sel
    cand = cand_t[...]
    ids = [pick_rows(sel == r, cand) for r in range(COLD)]
    loc = jnp.concatenate([loc_ref[pl.ds(0, high_rows, stride=2), :], loc_ref[pl.ds(1, high_rows, stride=2), :]], axis=1)
    high_table = jnp.transpose((loc // RADIX).astype(F32)).astype(BF16)
    low_table = jnp.transpose((loc & (RADIX - 1)).astype(F32)).astype(BF16)
    high_part, low_part = lookup([high_table, low_table], ids)
    before = one_hot(iota((q_rows, q_rows), 0) < iota((q_rows, q_rows), 1))
    owner_iota = iota((groups, q_rows), 0)
    slot_iota = iota((LANES, q_rows), 0)
    query = iota((1, q_rows), 1).astype(F32)
    base = jnp.zeros((groups, 1), F32)
    owners, ranks, owner_hots, low_vals, high_vals, query_vals = [], [], [], [], [], []
    for r in range(COLD):
        row = high_part[r].astype(jnp.int32) * RADIX + low_part[r].astype(jnp.int32)
        owner = row // per_owner
        local = row & (per_owner - 1)
        owner_hot = one_hot(owner_iota == owner, F32)
        count = jnp.dot(owner_hot.astype(BF16), before, preferred_element_type=F32) + base
        rank = jnp.sum(owner_hot * count, axis=0, keepdims=True).astype(jnp.int32)
        base = base + jnp.sum(owner_hot, axis=1, keepdims=True)
        at_slot = slot_iota == rank
        owners.append(owner)
        ranks.append(rank)
        owner_hots.append(owner_hot.astype(BF16))
        low_vals.append(jnp.where(at_slot, (local & (RADIX - 1)).astype(F32), 0.0).astype(BF16))
        high_vals.append(jnp.where(at_slot, (local // RADIX + RADIX // 2).astype(F32), 0.0).astype(BF16))
        query_vals.append(jnp.where(at_slot, query, 0.0).astype(BF16))
    owner_all = jnp.concatenate(owner_hots, axis=1)

    def spread(vals):
        got = lax.dot_general(owner_all, jnp.concatenate(vals, axis=1), ROWS_DOT, preferred_element_type=F32)
        return got.astype(jnp.int32)

    low_got, high_got, query_got = spread(low_vals), spread(high_vals), spread(query_vals)
    packed = low_got + RADIX * (high_got - RADIX // 2) + per_owner * query_got
    req_ref[...] = jnp.where(high_got > 0, packed, -1)
    place_ref[...] = jnp.concatenate(owners + ranks, axis=0)


def prep_kernel(per_owner, spot_ref, q_ref, hot_ref, loc_ref, slab_ref, out_ref, col_scr):
    hot_each = out_ref.shape[0] - q_ref.shape[0]
    high_rows = loc_ref.shape[0]
    ids = hot_ref[pl.ds(spot_ref[0] * hot_each // LANES, 1), :]
    high_hot = one_hot(iota((high_rows, LANES), 0) == (ids // LANES))
    low_mask = iota((LANES, LANES), 0) == (ids & (LANES - 1))
    loc = loc_ref[...]
    high = jnp.transpose((loc // RADIX).astype(F32)).astype(BF16)
    low = jnp.transpose((loc & (RADIX - 1)).astype(F32)).astype(BF16)
    high = pick_rows(low_mask, jnp.dot(high, high_hot, preferred_element_type=F32))
    low = pick_rows(low_mask, jnp.dot(low, high_hot, preferred_element_type=F32))
    local = high * RADIX + low - (spot_ref[0] * per_owner).astype(F32)
    col_scr[...] = jnp.transpose(jnp.broadcast_to(local, (LANES, LANES)))
    start = pl.multiple_of(spot_ref[0] * hot_each % LANES, hot_each)
    cols = jnp.concatenate([col_scr[pl.ds(start, hot_each), :]] * (per_owner // LANES), axis=1)
    picks = one_hot(iota((hot_each, per_owner), 1).astype(F32) == cols)
    rows = jnp.dot(picks, slab_ref[...], preferred_element_type=F32).astype(BF16)
    out_ref[0 : q_ref.shape[0], :] = q_ref[...]
    out_ref[q_ref.shape[0] :, :] = rows


def fetch_kernel(capacity, asked_ref, slab_ref, out_ref):
    groups = asked_ref.shape[0]
    per_owner = slab_ref.shape[0]
    asked = jnp.maximum(asked_ref[...], 0)
    cols = jnp.transpose((asked & (per_owner - 1)).astype(F32))
    lane = iota((capacity, per_owner), 1).astype(F32)
    picks = [
        one_hot(lane == jnp.broadcast_to(cols[0:capacity, n : n + 1], (capacity, per_owner)), F32)
        for n in range(groups)
    ]
    got = jnp.dot(jnp.concatenate(picks, axis=0).astype(BF16), slab_ref[...], preferred_element_type=F32)
    out_ref[...] = got.astype(BF16)


def cold_kernel(scale, capacity, q_ref, found_ref, place_ref, cold_ref):
    q_rows = q_ref.shape[0]
    q = q_ref[...]
    place = place_ref[...]
    dests = [place[r : r + 1] * capacity + place[COLD + r : COLD + r + 1] for r in range(COLD)]
    colds = [jnp.zeros((1, q_rows), F32) for _ in range(COLD)]
    chunk = 256
    for j in range(found_ref.shape[0] // chunk):
        rows = found_ref[j * chunk : (j + 1) * chunk, :]
        got = scale * lax.dot_general(rows, q, ROWS_DOT, preferred_element_type=F32)
        ids = iota((chunk, q_rows), 0) + j * chunk
        for r in range(COLD):
            colds[r] = colds[r] + pick_rows(ids == dests[r], got)
    cold_ref[...] = jnp.concatenate(colds, axis=0)


def count_kernel(cand_t, teacher_ref, hot_ref, sel_ref, count_ref, target_ref, misc_ref, soft_t):
    cand_count, q_rows = cand_t.shape
    teacher = teacher_ref[...]
    shifted = teacher - jnp.max(teacher, axis=0, keepdims=True)
    log_target = shifted - jnp.log(jnp.sum(jnp.exp(shifted), axis=0, keepdims=True))
    target = jnp.exp(log_target)
    soft_t[...] = target
    sel = sel_ref[...]
    entropy = jnp.sum(target * log_target, axis=0, keepdims=True)
    rows = [pick_rows(sel == r, target) for r in range(COLD)]
    misc_ref[...] = jnp.concatenate(rows + [jnp.broadcast_to(entropy, (8, q_rows))], axis=0)
    hot_cols = jnp.transpose(hot_ref[...])
    for a in range(hot_ref.shape[0]):
        column = jnp.broadcast_to(hot_cols[:, a : a + 1], (LANES, q_rows))

        def add(k, carry):
            count, total = carry
            match = column == cand_t[pl.ds(k, 1), :]
            count = count + jnp.where(match, 1.0, 0.0)
            total = total + jnp.where(match, soft_t[pl.ds(k, 1), :], 0.0)
            return count, total

        start = (jnp.ones((LANES, q_rows), F32), jnp.zeros((LANES, q_rows), F32))
        count, total = lax.fori_loop(0, cand_count, add, start, unroll=4)
        count_ref[a * LANES : (a + 1) * LANES, :] = count
        target_ref[a * LANES : (a + 1) * LANES, :] = total


def score_kernel(scale, q_ref, hot_ref, cold_ref, count_ref, target_ref, place_ref, misc_ref, loss_ref, pay_ref, weight_ref, hot_scr, slot_scr):
    groups, hot_each, feat = hot_ref.shape
    q_rows = q_ref.shape[0]
    q = q_ref[...]
    top = jnp.max(cold_ref[...], axis=0, keepdims=True)
    step = 8
    for j in range(groups // step):
        size = step * hot_each
        rows = hot_ref[j * step : (j + 1) * step].reshape(size, feat)
        got = scale * lax.dot_general(rows, q, ROWS_DOT, preferred_element_type=F32)
        hot_scr[j * size : (j + 1) * size, :] = got
        top = jnp.maximum(top, jnp.max(got, axis=0, keepdims=True))
    cold = cold_ref[...]
    place = place_ref[...]
    total = jnp.sum(jnp.exp(cold - top), axis=0, keepdims=True)
    hot_dot = jnp.zeros((1, q_rows), F32)
    for j in range(groups // 8):
        part = slice(j * 8 * hot_each, (j + 1) * 8 * hot_each)
        hot = hot_scr[part, :]
        total = total + jnp.sum(count_ref[part, :] * jnp.exp(hot - top), axis=0, keepdims=True)
        hot_dot = hot_dot + jnp.sum(target_ref[part, :] * hot, axis=0, keepdims=True)
    log_total = top + jnp.log(total)
    cold_target = misc_ref[0:COLD, :]
    entropy = misc_ref[COLD : COLD + 1, :]
    loss_ref[...] = entropy - hot_dot - jnp.sum(cold_target * cold, axis=0, keepdims=True) + log_total
    weight = (jnp.exp(cold - log_total) - cold_target).astype(BF16).astype(F32)
    weight_ref[...] = weight
    owner_iota = iota((groups, q_rows), 0)
    slot_iota = iota((LANES, q_rows), 0)
    owner_all = jnp.concatenate([one_hot(owner_iota == place[r : r + 1]) for r in range(COLD)], axis=1)
    slot_all = jnp.concatenate(
        [
            jnp.where(slot_iota == place[COLD + r : COLD + r + 1], weight[r : r + 1], 0.0).astype(BF16)
            for r in range(COLD)
        ],
        axis=1,
    )
    slot_scr[...] = lax.dot_general(owner_all, slot_all, ROWS_DOT, preferred_element_type=F32)
    for g in range(groups):
        part = slice(g * hot_each, (g + 1) * hot_each)
        coef = count_ref[part, :] * jnp.exp(hot_scr[part, :] - log_total) - target_ref[part, :]
        slot_row = jnp.broadcast_to(slot_scr[g : g + 1, :], (8, q_rows))
        pay_ref[g] = jnp.concatenate([coef, slot_row], axis=0).astype(BF16)


def query_kernel(scale, capacity, hot_ref, pay_ref, found_ref, weight_ref, place_ref, out_ref):
    groups, hot_each, feat = hot_ref.shape
    q_rows = out_ref.shape[0]
    acc = jnp.zeros(out_ref.shape, F32)
    step = 8
    first = (((0,), (0,)), ((), ()))
    for j in range(groups // step):
        rows = hot_ref[j * step : (j + 1) * step].reshape(step * hot_each, feat)
        coef = jnp.concatenate([pay_ref[j * step + n, 0:hot_each, :] for n in range(step)], axis=0)
        acc = acc + lax.dot_general(coef, rows, first, preferred_element_type=F32)
    chunk = 256
    place = place_ref[...]
    weight = weight_ref[...]
    dests = [place[r : r + 1] * capacity + place[COLD + r : COLD + r + 1] for r in range(COLD)]
    for j in range(found_ref.shape[0] // chunk):
        ids = iota((chunk, q_rows), 0) + j * chunk
        made = jnp.zeros((chunk, q_rows), F32)
        for r in range(COLD):
            made = jnp.where(ids == dests[r], weight[r : r + 1], made)
        rows = found_ref[j * chunk : (j + 1) * chunk, :]
        acc = acc + lax.dot_general(made.astype(BF16), rows, first, preferred_element_type=F32)
    out_ref[...] = scale * acc


def slab_kernel(scale, capacity, hot_each, spot_ref, pay_ref, row_ref, loc_ref, *refs):
    outs, terms = refs[:-1], refs[-1]
    step = pl.program_id(0)
    groups = pay_ref.shape[0]
    feat = terms.shape[1]
    sent = jnp.concatenate([pay_ref[n, hot_each : hot_each + 8, :].astype(F32)[0:1] for n in range(groups)], axis=0)
    cols = scale * jnp.transpose(sent)
    col = jnp.concatenate(
        [jnp.broadcast_to(cols[0:capacity, n : n + 1], (capacity, LANES)) for n in range(groups)], axis=0
    )
    size = groups * capacity
    wide = jnp.concatenate([col] * (feat // LANES), axis=1)
    made = (wide * row_ref[...].astype(F32)).astype(BF16)
    terms[pl.ds(pl.multiple_of(step * size, size), size), :] = made

    @pl.when(step == pl.num_programs(0) - 1)
    def _():
        loc = loc_ref[...]
        rows = outs[0].shape[0]
        ids = iota((rows, loc.shape[1]), 0)
        for d in range(0, len(outs), 2):
            starts = [(spot_ref[1] + e) % len(outs) * rows for e in (d, d + 1)]
            at = jnp.concatenate([one_hot(ids + start == loc) for start in starts], axis=0)
            got = jnp.dot(at, terms[...], preferred_element_type=F32)
            outs[d][...] = got[:rows].astype(outs[d].dtype)
            outs[d + 1][...] = got[rows:].astype(outs[d + 1].dtype)


def hot_sum_kernel(scale, pay_ref, query_ref, out_ref):
    step = pl.program_id(0)
    groups = pay_ref.shape[0]
    hot_each = out_ref.shape[0]

    @pl.when(step == 0)
    def _():
        out_ref[...] = jnp.zeros_like(out_ref)

    acc = out_ref[...]
    for n in range(0, groups, 2):
        left = jnp.concatenate([pay_ref[n, 0:hot_each, :], pay_ref[n + 1, 0:hot_each, :]], axis=1)
        right = jnp.concatenate([query_ref[n], query_ref[n + 1]], axis=0)
        acc = acc + scale * jnp.dot(left, right, preferred_element_type=F32)
    out_ref[...] = acc


def finish_kernel(reps, spot_ref, hot_loc_ref, *refs):
    hots, parts, out_ref = refs[:reps], refs[reps:-1], refs[-1]
    rows = out_ref.shape[0]
    full = hots[0][...]
    for hot in hots[1:]:
        full = full + hot[...]
    high = full.astype(BF16)
    rest = full - high.astype(F32)
    mid = rest.astype(BF16)
    low = (rest - mid.astype(F32)).astype(BF16)
    pieces = jnp.concatenate([high, mid, low, jnp.zeros_like(low)], axis=0)
    loc = hot_loc_ref[...]
    at = one_hot(iota((rows, loc.shape[1]), 0) + spot_ref[1] * rows == loc)
    total = jnp.dot(at, pieces, preferred_element_type=F32)
    for part in parts:
        total = total + part[...].astype(F32)
    out_ref[...] = total


def shards(queries, teacher, slab, candidates, hot_ids, location):
    groups = lax.axis_size("corpus")
    reps = lax.axis_size("rep")
    corpus_idx = lax.axis_index("corpus")
    q_rows, feat = queries.shape
    per_owner = slab.shape[0]
    hot_total = hot_ids.shape[0]
    hot_each = hot_total // groups
    cand_count = candidates.shape[1]
    capacity = q_rows * COLD * 3 // (2 * groups)
    scale = 2.0 / math.sqrt(feat)
    rep_idx = lax.axis_index("rep")
    spot = jnp.stack([corpus_idx, rep_idx]).astype(jnp.int32)
    loc_table = location.reshape(-1, LANES)
    hot_table = hot_ids.reshape(-1, LANES)
    sent_rows = pl.pallas_call(
        functools.partial(prep_kernel, per_owner),
        out_shape=jax.ShapeDtypeStruct((q_rows + hot_each, feat), BF16),
        in_specs=[SMEM_SPEC] + [VMEM_SPEC] * 4,
        out_specs=VMEM_SPEC,
        scratch_shapes=[pltpu.VMEM((LANES, LANES), F32)],
        name="prep",
    )(spot, queries, hot_table, loc_table, slab)
    cand_t, sent_rows = lax.optimization_barrier((candidates.T, sent_rows))
    gathered = lax.all_gather(sent_rows, "corpus", axis=0, tiled=False)
    req, place, sel = pl.pallas_call(
        functools.partial(request_kernel, per_owner, groups),
        out_shape=(
            jax.ShapeDtypeStruct((groups, LANES), jnp.int32),
            jax.ShapeDtypeStruct((2 * COLD, q_rows), jnp.int32),
            jax.ShapeDtypeStruct((cand_count, q_rows), jnp.int32),
        ),
        in_specs=[VMEM_SPEC] * 3,
        out_specs=(VMEM_SPEC,) * 3,
        scratch_shapes=[pltpu.VMEM((cand_count, q_rows), F32)],
        name="request",
    )(cand_t, hot_ids.reshape(1, hot_total), loc_table)
    asked = lax.all_to_all(req.reshape(groups, 1, LANES), "corpus", split_axis=0, concat_axis=0, tiled=True)
    asked = asked.reshape(groups, LANES)
    slots = groups * capacity
    parts = 4
    wanted = pl.pallas_call(
        functools.partial(fetch_kernel, capacity),
        grid=(parts,),
        out_shape=jax.ShapeDtypeStruct((slots, feat), BF16),
        in_specs=[pl.BlockSpec((groups // parts, LANES), lambda i: (i, 0)), pl.BlockSpec((per_owner, feat), lambda i: (0, 0))],
        out_specs=pl.BlockSpec((slots // parts, feat), lambda i: (i, 0)),
        name="fetch",
    )(asked, slab)
    found = lax.all_to_all(wanted.reshape(groups, capacity, feat), "corpus", split_axis=0, concat_axis=0, tiled=True)
    found = found.reshape(groups * capacity, feat)
    count, target, misc = pl.pallas_call(
        count_kernel,
        out_shape=(
            jax.ShapeDtypeStruct((hot_total, q_rows), F32),
            jax.ShapeDtypeStruct((hot_total, q_rows), F32),
            jax.ShapeDtypeStruct((2 * COLD, q_rows), F32),
        ),
        in_specs=[VMEM_SPEC] * 4,
        out_specs=(VMEM_SPEC,) * 3,
        scratch_shapes=[pltpu.VMEM((cand_count, q_rows), F32)],
        cost_estimate=pl.CostEstimate(flops=80_000_000, bytes_accessed=3_000_000, transcendentals=10_000),
        name="count",
    )(cand_t, teacher.T, hot_table, sel)
    hot_block = pl.BlockSpec((groups, hot_each, feat), lambda i: (0, q_rows // hot_each, 0))

    def whole(shape):
        return pl.BlockSpec(shape, lambda i: (0,) * len(shape))

    pay_rows = hot_each + 8
    cold = pl.pallas_call(
        functools.partial(cold_kernel, scale, capacity),
        out_shape=jax.ShapeDtypeStruct((COLD, q_rows), F32),
        in_specs=[VMEM_SPEC] * 3,
        out_specs=VMEM_SPEC,
        name="cold",
    )(queries, found, place)
    loss, pay, weight = pl.pallas_call(
        functools.partial(score_kernel, scale),
        grid=(1,),
        out_shape=(
            jax.ShapeDtypeStruct((1, q_rows), F32),
            jax.ShapeDtypeStruct((groups, pay_rows, q_rows), BF16),
            jax.ShapeDtypeStruct((COLD, q_rows), F32),
        ),
        in_specs=[
            whole((q_rows, feat)),
            hot_block,
            whole((COLD, q_rows)),
            whole((hot_total, q_rows)),
            whole((hot_total, q_rows)),
            whole((2 * COLD, q_rows)),
            whole((2 * COLD, q_rows)),
        ],
        out_specs=(whole((1, q_rows)), whole((groups, pay_rows, q_rows)), whole((COLD, q_rows))),
        scratch_shapes=[
            pltpu.VMEM((hot_total, q_rows), F32),
            pltpu.VMEM((groups, q_rows), F32),
        ],
        name="score",
    )(queries, gathered, cold, count, target, place, misc)
    got = lax.all_to_all(pay, "corpus", split_axis=0, concat_axis=0, tiled=True)
    query_grad = pl.pallas_call(
        functools.partial(query_kernel, scale, capacity),
        grid=(1,),
        out_shape=jax.ShapeDtypeStruct((q_rows, feat), F32),
        in_specs=[hot_block, whole((groups, pay_rows, q_rows)), whole((slots, feat)), whole((COLD, q_rows)), whole((2 * COLD, q_rows))],
        out_specs=whole((q_rows, feat)),
        cost_estimate=pl.CostEstimate(flops=700_000_000, bytes_accessed=7_000_000, transcendentals=0),
        name="query_grad",
    )(gathered, pay, found, weight, place)
    padded = asked[:, :capacity]
    source = jnp.arange(groups, dtype=jnp.int32)[:, None] * (q_rows + hot_each)
    query_rows = gathered.reshape(-1, feat)[(source + jnp.maximum(padded, 0) // per_owner).reshape(-1)]
    local = jnp.where(padded >= 0, padded & (per_owner - 1), -1).reshape(1, -1)
    mine = lax.dynamic_slice_in_dim(hot_ids, corpus_idx * hot_each, hot_each)
    own_hot = location[mine] - corpus_idx * per_owner
    tail = jnp.full((LANES - 3 * hot_each,), -1, jnp.int32)
    hot_loc = jnp.concatenate([own_hot, own_hot, own_hot, tail])[None, :]
    step = 16
    quarter = (per_owner // reps, feat)
    quarters = pl.pallas_call(
        functools.partial(slab_kernel, scale, capacity, hot_each),
        grid=(groups // step,),
        out_shape=tuple(jax.ShapeDtypeStruct(quarter, F32 if d == 0 else BF16) for d in range(reps)),
        in_specs=[
            SMEM_SPEC,
            pl.BlockSpec((step, pay_rows, q_rows), lambda i: (i, 0, 0)),
            pl.BlockSpec((step * capacity, feat), lambda i: (i, 0)),
            whole((1, slots)),
        ],
        out_specs=tuple(whole(quarter) for _ in range(reps)),
        scratch_shapes=[pltpu.VMEM((slots, feat), BF16)],
        name="slab_grad",
    )(spot, got, query_rows, local)

    def turn(array, d):
        return lax.ppermute(array, "rep", [(r, (r + d) % reps) for r in range(reps)])

    received = [turn(quarters[d], d) for d in (2, 1, 3)]
    hot_sum = pl.pallas_call(
        functools.partial(hot_sum_kernel, scale),
        grid=(groups // step,),
        out_shape=jax.ShapeDtypeStruct((hot_each, feat), F32),
        in_specs=[
            pl.BlockSpec((step, pay_rows, q_rows), lambda i: (i, 0, 0)),
            pl.BlockSpec((step, q_rows, feat), lambda i: (i, 0, 0)),
        ],
        out_specs=whole((hot_each, feat)),
        cost_estimate=pl.CostEstimate(flops=3_000_000_000, bytes_accessed=13_000_000, transcendentals=0),
        name="hot_sum",
    )(got, gathered)
    hots = [hot_sum] + [turn(hot_sum, d) for d in range(1, reps)]
    slab_grad = pl.pallas_call(
        functools.partial(finish_kernel, reps),
        out_shape=jax.ShapeDtypeStruct(quarter, F32),
        in_specs=[SMEM_SPEC] + [VMEM_SPEC] * (2 * reps + 1),
        out_specs=VMEM_SPEC,
        name="finish",
    )(spot, hot_loc, *hots, quarters[0], *received)
    return (loss.reshape(q_rows), query_grad, slab_grad)


def solution(mesh):
    return jax.shard_map(
        shards,
        mesh=mesh,
        in_specs=(
            P(("corpus", "rep"), None),
            P(("corpus", "rep"), None),
            P("corpus", None),
            P(("corpus", "rep"), None),
            P(),
            P(),
        ),
        out_specs=(P(("corpus", "rep")), P(("corpus", "rep"), None), P(("corpus", "rep"), None)),
        check_vma=False,
    )
```

```python
import functools
import math

import jax
import jax.numpy as jnp
from jax import lax
from jax.experimental import pallas as pl
from jax.experimental.pallas import tpu as pltpu
from jax.sharding import PartitionSpec as P


COLD = 8
LANES = 128
RADIX = 256
F32 = jnp.float32
BF16 = jnp.bfloat16
VMEM_SPEC = pl.BlockSpec(memory_space=pltpu.VMEM)
SMEM_SPEC = pl.BlockSpec(memory_space=pltpu.SMEM)
ROWS_DOT = (((1,), (1,)), ((), ()))


def iota(shape, axis):
    return lax.broadcasted_iota(jnp.int32, shape, axis)


def one_hot(mask, dtype=BF16):
    return jnp.where(mask, 1.0, 0.0).astype(dtype)


def pick_rows(mask, values):
    return jnp.sum(jnp.where(mask, values, jnp.zeros_like(values)), axis=0, keepdims=True)


def request_kernel(per_owner, groups, cand_t, hot_ref, loc_ref, req_ref, place_ref, sel_ref, hit_t):
    cand_count, q_rows = cand_t.shape
    hot_total = hot_ref.shape[1]
    high_rows = loc_ref.shape[0] // 2
    hot = hot_ref[...]
    low_hot = one_hot(iota((RADIX, hot_total), 0) == (hot & (RADIX - 1)))
    high_hot = one_hot(iota((high_rows, hot_total), 0) == (hot // RADIX))
    marks = lax.dot_general(low_hot, high_hot, ROWS_DOT, preferred_element_type=F32).astype(BF16)
    low_iota = iota((RADIX, q_rows), 0)
    high_iota = iota((high_rows, q_rows), 0)

    def lookup(tables, ids):
        hots = jnp.concatenate([one_hot(high_iota == (i // RADIX)) for i in ids], axis=1)
        found = [jnp.dot(t, hots, preferred_element_type=F32) for t in tables]
        masks = [low_iota == (i & (RADIX - 1)) for i in ids]
        return [
            [pick_rows(m, f[:, n * q_rows : (n + 1) * q_rows]) for n, m in enumerate(masks)]
            for f in found
        ]

    def check(j, carry):
        start = pl.multiple_of(j * 8, 8)
        rows = cand_t[pl.ds(start, 8), :]
        hits = lookup([marks], [rows[n : n + 1, :] for n in range(8)])[0]
        hit_t[pl.ds(start, 8), :] = jnp.concatenate(hits, axis=0)
        return carry

    lax.fori_loop(0, cand_count // 8, check, 0)
    cold = hit_t[...] < 0.5
    earlier = one_hot(iota((cand_count, cand_count), 0) > iota((cand_count, cand_count), 1))
    order = jnp.dot(earlier, one_hot(cold), preferred_element_type=F32).astype(jnp.int32)
    sel = jnp.where(cold, order, -1)
    sel_ref[...] = sel
    cand = cand_t[...]
    ids = [pick_rows(sel == r, cand) for r in range(COLD)]
    loc = jnp.concatenate([loc_ref[pl.ds(0, high_rows, stride=2), :], loc_ref[pl.ds(1, high_rows, stride=2), :]], axis=1)
    high_table = jnp.transpose((loc // RADIX).astype(F32)).astype(BF16)
    low_table = jnp.transpose((loc & (RADIX - 1)).astype(F32)).astype(BF16)
    high_part, low_part = lookup([high_table, low_table], ids)
    before = one_hot(iota((q_rows, q_rows), 0) < iota((q_rows, q_rows), 1))
    owner_iota = iota((groups, q_rows), 0)
    slot_iota = iota((LANES, q_rows), 0)
    query = iota((1, q_rows), 1).astype(F32)
    base = jnp.zeros((groups, 1), F32)
    owners, ranks, owner_hots, low_vals, high_vals, query_vals = [], [], [], [], [], []
    for r in range(COLD):
        row = high_part[r].astype(jnp.int32) * RADIX + low_part[r].astype(jnp.int32)
        owner = row // per_owner
        local = row & (per_owner - 1)
        owner_hot = one_hot(owner_iota == owner, F32)
        count = jnp.dot(owner_hot.astype(BF16), before, preferred_element_type=F32) + base
        rank = jnp.sum(owner_hot * count, axis=0, keepdims=True).astype(jnp.int32)
        base = base + jnp.sum(owner_hot, axis=1, keepdims=True)
        at_slot = slot_iota == rank
        owners.append(owner)
        ranks.append(rank)
        owner_hots.append(owner_hot.astype(BF16))
        low_vals.append(jnp.where(at_slot, (local & (RADIX - 1)).astype(F32), 0.0).astype(BF16))
        high_vals.append(jnp.where(at_slot, (local // RADIX + RADIX // 2).astype(F32), 0.0).astype(BF16))
        query_vals.append(jnp.where(at_slot, query, 0.0).astype(BF16))
    owner_all = jnp.concatenate(owner_hots, axis=1)

    def spread(vals):
        got = lax.dot_general(owner_all, jnp.concatenate(vals, axis=1), ROWS_DOT, preferred_element_type=F32)
        return got.astype(jnp.int32)

    low_got, high_got, query_got = spread(low_vals), spread(high_vals), spread(query_vals)
    packed = low_got + RADIX * (high_got - RADIX // 2) + per_owner * query_got
    req_ref[...] = jnp.where(high_got > 0, packed, -1)
    place_ref[...] = jnp.concatenate(owners + ranks, axis=0)


def prep_kernel(per_owner, spot_ref, q_ref, hot_ref, loc_ref, slab_ref, out_ref, col_scr):
    hot_each = out_ref.shape[0] - q_ref.shape[0]
    high_rows = loc_ref.shape[0]
    ids = hot_ref[pl.ds(spot_ref[0] * hot_each // LANES, 1), :]
    high_hot = one_hot(iota((high_rows, LANES), 0) == (ids // LANES))
    low_mask = iota((LANES, LANES), 0) == (ids & (LANES - 1))
    loc = loc_ref[...]
    high = jnp.transpose((loc // RADIX).astype(F32)).astype(BF16)
    low = jnp.transpose((loc & (RADIX - 1)).astype(F32)).astype(BF16)
    high = pick_rows(low_mask, jnp.dot(high, high_hot, preferred_element_type=F32))
    low = pick_rows(low_mask, jnp.dot(low, high_hot, preferred_element_type=F32))
    local = high * RADIX + low - (spot_ref[0] * per_owner).astype(F32)
    col_scr[...] = jnp.transpose(jnp.broadcast_to(local, (LANES, LANES)))
    start = pl.multiple_of(spot_ref[0] * hot_each % LANES, hot_each)
    cols = jnp.concatenate([col_scr[pl.ds(start, hot_each), :]] * (per_owner // LANES), axis=1)
    picks = one_hot(iota((hot_each, per_owner), 1).astype(F32) == cols)
    rows = jnp.dot(picks, slab_ref[...], preferred_element_type=F32).astype(BF16)
    out_ref[0 : q_ref.shape[0], :] = q_ref[...]
    out_ref[q_ref.shape[0] :, :] = rows


def fetch_kernel(capacity, asked_ref, slab_ref, out_ref):
    groups = asked_ref.shape[0]
    per_owner = slab_ref.shape[0]
    asked = jnp.maximum(asked_ref[...], 0)
    cols = jnp.transpose((asked & (per_owner - 1)).astype(F32))
    lane = iota((capacity, per_owner), 1).astype(F32)
    picks = [
        one_hot(lane == jnp.broadcast_to(cols[0:capacity, n : n + 1], (capacity, per_owner)), F32)
        for n in range(groups)
    ]
    got = jnp.dot(jnp.concatenate(picks, axis=0).astype(BF16), slab_ref[...], preferred_element_type=F32)
    out_ref[...] = got.astype(BF16)


def cold_kernel(scale, capacity, q_ref, found_ref, place_ref, cold_ref):
    q_rows = q_ref.shape[0]
    q = q_ref[...]
    place = place_ref[...]
    dests = [place[r : r + 1] * capacity + place[COLD + r : COLD + r + 1] for r in range(COLD)]
    colds = [jnp.zeros((1, q_rows), F32) for _ in range(COLD)]
    chunk = 256
    for j in range(found_ref.shape[0] // chunk):
        rows = found_ref[j * chunk : (j + 1) * chunk, :]
        got = scale * lax.dot_general(rows, q, ROWS_DOT, preferred_element_type=F32)
        ids = iota((chunk, q_rows), 0) + j * chunk
        for r in range(COLD):
            colds[r] = colds[r] + pick_rows(ids == dests[r], got)
    cold_ref[...] = jnp.concatenate(colds, axis=0)


def count_kernel(cand_t, teacher_ref, hot_ref, sel_ref, count_ref, target_ref, misc_ref, soft_t):
    cand_count, q_rows = cand_t.shape
    teacher = teacher_ref[...]
    shifted = teacher - jnp.max(teacher, axis=0, keepdims=True)
    log_target = shifted - jnp.log(jnp.sum(jnp.exp(shifted), axis=0, keepdims=True))
    target = jnp.exp(log_target)
    soft_t[...] = target
    sel = sel_ref[...]
    entropy = jnp.sum(target * log_target, axis=0, keepdims=True)
    rows = [pick_rows(sel == r, target) for r in range(COLD)]
    misc_ref[...] = jnp.concatenate(rows + [jnp.broadcast_to(entropy, (8, q_rows))], axis=0)
    hot_cols = jnp.transpose(hot_ref[...])
    for a in range(hot_ref.shape[0]):
        column = jnp.broadcast_to(hot_cols[:, a : a + 1], (LANES, q_rows))

        def add(k, carry):
            count, total = carry
            match = column == cand_t[pl.ds(k, 1), :]
            count = count + jnp.where(match, 1.0, 0.0)
            total = total + jnp.where(match, soft_t[pl.ds(k, 1), :], 0.0)
            return count, total

        start = (jnp.ones((LANES, q_rows), F32), jnp.zeros((LANES, q_rows), F32))
        count, total = lax.fori_loop(0, cand_count, add, start, unroll=4)
        count_ref[a * LANES : (a + 1) * LANES, :] = count
        target_ref[a * LANES : (a + 1) * LANES, :] = total


def score_kernel(scale, q_ref, hot_ref, cold_ref, count_ref, target_ref, place_ref, misc_ref, loss_ref, pay_ref, weight_ref, hot_scr, slot_scr):
    groups, hot_each, feat = hot_ref.shape
    q_rows = q_ref.shape[0]
    q = q_ref[...]
    top = jnp.max(cold_ref[...], axis=0, keepdims=True)
    step = 8
    for j in range(groups // step):
        size = step * hot_each
        rows = hot_ref[j * step : (j + 1) * step].reshape(size, feat)
        got = scale * lax.dot_general(rows, q, ROWS_DOT, preferred_element_type=F32)
        hot_scr[j * size : (j + 1) * size, :] = got
        top = jnp.maximum(top, jnp.max(got, axis=0, keepdims=True))
    cold = cold_ref[...]
    place = place_ref[...]
    total = jnp.sum(jnp.exp(cold - top), axis=0, keepdims=True)
    hot_dot = jnp.zeros((1, q_rows), F32)
    for j in range(groups // 8):
        part = slice(j * 8 * hot_each, (j + 1) * 8 * hot_each)
        hot = hot_scr[part, :]
        total = total + jnp.sum(count_ref[part, :] * jnp.exp(hot - top), axis=0, keepdims=True)
        hot_dot = hot_dot + jnp.sum(target_ref[part, :] * hot, axis=0, keepdims=True)
    log_total = top + jnp.log(total)
    cold_target = misc_ref[0:COLD, :]
    entropy = misc_ref[COLD : COLD + 1, :]
    loss_ref[...] = entropy - hot_dot - jnp.sum(cold_target * cold, axis=0, keepdims=True) + log_total
    weight = (jnp.exp(cold - log_total) - cold_target).astype(BF16).astype(F32)
    weight_ref[...] = weight
    owner_iota = iota((groups, q_rows), 0)
    slot_iota = iota((LANES, q_rows), 0)
    owner_all = jnp.concatenate([one_hot(owner_iota == place[r : r + 1]) for r in range(COLD)], axis=1)
    slot_all = jnp.concatenate(
        [
            jnp.where(slot_iota == place[COLD + r : COLD + r + 1], weight[r : r + 1], 0.0).astype(BF16)
            for r in range(COLD)
        ],
        axis=1,
    )
    slot_scr[...] = lax.dot_general(owner_all, slot_all, ROWS_DOT, preferred_element_type=F32)
    for g in range(groups):
        part = slice(g * hot_each, (g + 1) * hot_each)
        coef = count_ref[part, :] * jnp.exp(hot_scr[part, :] - log_total) - target_ref[part, :]
        slot_row = jnp.broadcast_to(slot_scr[g : g + 1, :], (8, q_rows))
        pay_ref[g] = jnp.concatenate([coef, slot_row], axis=0).astype(BF16)


def query_kernel(scale, capacity, hot_ref, pay_ref, found_ref, weight_ref, place_ref, out_ref):
    groups, hot_each, feat = hot_ref.shape
    q_rows = out_ref.shape[0]
    acc = jnp.zeros(out_ref.shape, F32)
    step = 8
    first = (((0,), (0,)), ((), ()))
    for j in range(groups // step):
        rows = hot_ref[j * step : (j + 1) * step].reshape(step * hot_each, feat)
        coef = jnp.concatenate([pay_ref[j * step + n, 0:hot_each, :] for n in range(step)], axis=0)
        acc = acc + lax.dot_general(coef, rows, first, preferred_element_type=F32)
    chunk = 256
    place = place_ref[...]
    weight = weight_ref[...]
    dests = [place[r : r + 1] * capacity + place[COLD + r : COLD + r + 1] for r in range(COLD)]
    for j in range(found_ref.shape[0] // chunk):
        ids = iota((chunk, q_rows), 0) + j * chunk
        made = jnp.zeros((chunk, q_rows), F32)
        for r in range(COLD):
            made = jnp.where(ids == dests[r], weight[r : r + 1], made)
        rows = found_ref[j * chunk : (j + 1) * chunk, :]
        acc = acc + lax.dot_general(made.astype(BF16), rows, first, preferred_element_type=F32)
    out_ref[...] = scale * acc


def slab_kernel(scale, capacity, hot_each, spot_ref, pay_ref, row_ref, loc_ref, *refs):
    outs, terms = refs[:-1], refs[-1]
    step = pl.program_id(0)
    groups = pay_ref.shape[0]
    feat = terms.shape[1]
    sent = jnp.concatenate([pay_ref[n, hot_each : hot_each + 8, :].astype(F32)[0:1] for n in range(groups)], axis=0)
    cols = scale * jnp.transpose(sent)
    col = jnp.concatenate(
        [jnp.broadcast_to(cols[0:capacity, n : n + 1], (capacity, LANES)) for n in range(groups)], axis=0
    )
    size = groups * capacity
    wide = jnp.concatenate([col] * (feat // LANES), axis=1)
    made = (wide * row_ref[...].astype(F32)).astype(BF16)
    terms[pl.ds(pl.multiple_of(step * size, size), size), :] = made

    @pl.when(step == pl.num_programs(0) - 1)
    def _():
        loc = loc_ref[...]
        rows = outs[0].shape[0]
        ids = iota((rows, loc.shape[1]), 0)
        for d in range(0, len(outs), 2):
            starts = [(spot_ref[1] + e) % len(outs) * rows for e in (d, d + 1)]
            at = jnp.concatenate([one_hot(ids + start == loc) for start in starts], axis=0)
            got = jnp.dot(at, terms[...], preferred_element_type=F32)
            outs[d][...] = got[:rows].astype(outs[d].dtype)
            outs[d + 1][...] = got[rows:].astype(outs[d + 1].dtype)


def hot_sum_kernel(scale, pay_ref, query_ref, out_ref):
    step = pl.program_id(0)
    groups = pay_ref.shape[0]
    hot_each = out_ref.shape[0]

    @pl.when(step == 0)
    def _():
        out_ref[...] = jnp.zeros_like(out_ref)

    acc = out_ref[...]
    for n in range(0, groups, 2):
        left = jnp.concatenate([pay_ref[n, 0:hot_each, :], pay_ref[n + 1, 0:hot_each, :]], axis=1)
        right = jnp.concatenate([query_ref[n], query_ref[n + 1]], axis=0)
        acc = acc + scale * jnp.dot(left, right, preferred_element_type=F32)
    out_ref[...] = acc


def finish_kernel(reps, spot_ref, hot_loc_ref, *refs):
    hots, parts, out_ref = refs[:reps], refs[reps:-1], refs[-1]
    rows = out_ref.shape[0]
    full = hots[0][...]
    for hot in hots[1:]:
        full = full + hot[...]
    high = full.astype(BF16)
    rest = full - high.astype(F32)
    mid = rest.astype(BF16)
    low = (rest - mid.astype(F32)).astype(BF16)
    pieces = jnp.concatenate([high, mid, low, jnp.zeros_like(low)], axis=0)
    loc = hot_loc_ref[...]
    at = one_hot(iota((rows, loc.shape[1]), 0) + spot_ref[1] * rows == loc)
    total = jnp.dot(at, pieces, preferred_element_type=F32)
    for part in parts:
        total = total + part[...].astype(F32)
    out_ref[...] = total


def shards(queries, teacher, slab, candidates, hot_ids, location):
    groups = lax.axis_size("corpus")
    reps = lax.axis_size("rep")
    corpus_idx = lax.axis_index("corpus")
    q_rows, feat = queries.shape
    per_owner = slab.shape[0]
    hot_total = hot_ids.shape[0]
    hot_each = hot_total // groups
    cand_count = candidates.shape[1]
    capacity = q_rows * COLD * 3 // (2 * groups)
    scale = 2.0 / math.sqrt(feat)
    rep_idx = lax.axis_index("rep")
    spot = jnp.stack([corpus_idx, rep_idx]).astype(jnp.int32)
    loc_table = location.reshape(-1, LANES)
    hot_table = hot_ids.reshape(-1, LANES)
    sent_rows = pl.pallas_call(
        functools.partial(prep_kernel, per_owner),
        out_shape=jax.ShapeDtypeStruct((q_rows + hot_each, feat), BF16),
        in_specs=[SMEM_SPEC] + [VMEM_SPEC] * 4,
        out_specs=VMEM_SPEC,
        scratch_shapes=[pltpu.VMEM((LANES, LANES), F32)],
        name="prep",
    )(spot, queries, hot_table, loc_table, slab)
    cand_t, sent_rows = lax.optimization_barrier((candidates.T, sent_rows))
    gathered = lax.all_gather(sent_rows, "corpus", axis=0, tiled=False)
    req, place, sel = pl.pallas_call(
        functools.partial(request_kernel, per_owner, groups),
        out_shape=(
            jax.ShapeDtypeStruct((groups, LANES), jnp.int32),
            jax.ShapeDtypeStruct((2 * COLD, q_rows), jnp.int32),
            jax.ShapeDtypeStruct((cand_count, q_rows), jnp.int32),
        ),
        in_specs=[VMEM_SPEC] * 3,
        out_specs=(VMEM_SPEC,) * 3,
        scratch_shapes=[pltpu.VMEM((cand_count, q_rows), F32)],
        name="request",
    )(cand_t, hot_ids.reshape(1, hot_total), loc_table)
    asked = lax.all_to_all(req.reshape(groups, 1, LANES), "corpus", split_axis=0, concat_axis=0, tiled=True)
    asked = asked.reshape(groups, LANES)
    slots = groups * capacity
    parts = 2
    wanted = pl.pallas_call(
        functools.partial(fetch_kernel, capacity),
        grid=(parts,),
        out_shape=jax.ShapeDtypeStruct((slots, feat), BF16),
        in_specs=[pl.BlockSpec((groups // parts, LANES), lambda i: (i, 0)), pl.BlockSpec((per_owner, feat), lambda i: (0, 0))],
        out_specs=pl.BlockSpec((slots // parts, feat), lambda i: (i, 0)),
        name="fetch",
    )(asked, slab)
    found = lax.all_to_all(wanted.reshape(groups, capacity, feat), "corpus", split_axis=0, concat_axis=0, tiled=True)
    found = found.reshape(groups * capacity, feat)
    count, target, misc = pl.pallas_call(
        count_kernel,
        out_shape=(
            jax.ShapeDtypeStruct((hot_total, q_rows), F32),
            jax.ShapeDtypeStruct((hot_total, q_rows), F32),
            jax.ShapeDtypeStruct((2 * COLD, q_rows), F32),
        ),
        in_specs=[VMEM_SPEC] * 4,
        out_specs=(VMEM_SPEC,) * 3,
        scratch_shapes=[pltpu.VMEM((cand_count, q_rows), F32)],
        cost_estimate=pl.CostEstimate(flops=80_000_000, bytes_accessed=3_000_000, transcendentals=10_000),
        name="count",
    )(cand_t, teacher.T, hot_table, sel)
    hot_block = pl.BlockSpec((groups, hot_each, feat), lambda i: (0, q_rows // hot_each, 0))

    def whole(shape):
        return pl.BlockSpec(shape, lambda i: (0,) * len(shape))

    pay_rows = hot_each + 8
    cold = pl.pallas_call(
        functools.partial(cold_kernel, scale, capacity),
        out_shape=jax.ShapeDtypeStruct((COLD, q_rows), F32),
        in_specs=[VMEM_SPEC] * 3,
        out_specs=VMEM_SPEC,
        name="cold",
    )(queries, found, place)
    loss, pay, weight = pl.pallas_call(
        functools.partial(score_kernel, scale),
        grid=(1,),
        out_shape=(
            jax.ShapeDtypeStruct((1, q_rows), F32),
            jax.ShapeDtypeStruct((groups, pay_rows, q_rows), BF16),
            jax.ShapeDtypeStruct((COLD, q_rows), F32),
        ),
        in_specs=[
            whole((q_rows, feat)),
            hot_block,
            whole((COLD, q_rows)),
            whole((hot_total, q_rows)),
            whole((hot_total, q_rows)),
            whole((2 * COLD, q_rows)),
            whole((2 * COLD, q_rows)),
        ],
        out_specs=(whole((1, q_rows)), whole((groups, pay_rows, q_rows)), whole((COLD, q_rows))),
        scratch_shapes=[
            pltpu.VMEM((hot_total, q_rows), F32),
            pltpu.VMEM((groups, q_rows), F32),
        ],
        name="score",
    )(queries, gathered, cold, count, target, place, misc)
    got = lax.all_to_all(pay, "corpus", split_axis=0, concat_axis=0, tiled=True)
    query_grad = pl.pallas_call(
        functools.partial(query_kernel, scale, capacity),
        grid=(1,),
        out_shape=jax.ShapeDtypeStruct((q_rows, feat), F32),
        in_specs=[hot_block, whole((groups, pay_rows, q_rows)), whole((slots, feat)), whole((COLD, q_rows)), whole((2 * COLD, q_rows))],
        out_specs=whole((q_rows, feat)),
        cost_estimate=pl.CostEstimate(flops=700_000_000, bytes_accessed=7_000_000, transcendentals=0),
        name="query_grad",
    )(gathered, pay, found, weight, place)
    padded = asked[:, :capacity]
    source = jnp.arange(groups, dtype=jnp.int32)[:, None] * (q_rows + hot_each)
    query_rows = gathered.reshape(-1, feat)[(source + jnp.maximum(padded, 0) // per_owner).reshape(-1)]
    local = jnp.where(padded >= 0, padded & (per_owner - 1), -1).reshape(1, -1)
    mine = lax.dynamic_slice_in_dim(hot_ids, corpus_idx * hot_each, hot_each)
    own_hot = location[mine] - corpus_idx * per_owner
    tail = jnp.full((LANES - 3 * hot_each,), -1, jnp.int32)
    hot_loc = jnp.concatenate([own_hot, own_hot, own_hot, tail])[None, :]
    step = 32
    quarter = (per_owner // reps, feat)
    quarters = pl.pallas_call(
        functools.partial(slab_kernel, scale, capacity, hot_each),
        grid=(groups // step,),
        out_shape=tuple(jax.ShapeDtypeStruct(quarter, F32 if d == 0 else BF16) for d in range(reps)),
        in_specs=[
            SMEM_SPEC,
            pl.BlockSpec((step, pay_rows, q_rows), lambda i: (i, 0, 0)),
            pl.BlockSpec((step * capacity, feat), lambda i: (i, 0)),
            whole((1, slots)),
        ],
        out_specs=tuple(whole(quarter) for _ in range(reps)),
        scratch_shapes=[pltpu.VMEM((slots, feat), BF16)],
        name="slab_grad",
    )(spot, got, query_rows, local)

    def turn(array, d):
        return lax.ppermute(array, "rep", [(r, (r + d) % reps) for r in range(reps)])

    received = [turn(quarters[d], d) for d in (2, 1, 3)]
    hot_sum = pl.pallas_call(
        functools.partial(hot_sum_kernel, scale),
        grid=(groups // step,),
        out_shape=jax.ShapeDtypeStruct((hot_each, feat), F32),
        in_specs=[
            pl.BlockSpec((step, pay_rows, q_rows), lambda i: (i, 0, 0)),
            pl.BlockSpec((step, q_rows, feat), lambda i: (i, 0, 0)),
        ],
        out_specs=whole((hot_each, feat)),
        cost_estimate=pl.CostEstimate(flops=3_000_000_000, bytes_accessed=13_000_000, transcendentals=0),
        name="hot_sum",
    )(got, gathered)
    after, before = turn(hot_sum, 1), turn(hot_sum, reps - 1)
    hots = [hot_sum, after, before, turn(before, reps - 1)]
    slab_grad = pl.pallas_call(
        functools.partial(finish_kernel, reps),
        out_shape=jax.ShapeDtypeStruct(quarter, F32),
        in_specs=[SMEM_SPEC] + [VMEM_SPEC] * (2 * reps + 1),
        out_specs=VMEM_SPEC,
        name="finish",
    )(spot, hot_loc, *hots, quarters[0], *received)
    return (loss.reshape(q_rows), query_grad, slab_grad)


def solution(mesh):
    return jax.shard_map(
        shards,
        mesh=mesh,
        in_specs=(
            P(("corpus", "rep"), None),
            P(("corpus", "rep"), None),
            P("corpus", None),
            P(("corpus", "rep"), None),
            P(),
            P(),
        ),
        out_specs=(P(("corpus", "rep")), P(("corpus", "rep"), None), P(("corpus", "rep"), None)),
        check_vma=False,
    )
```
